32 devices in a mesh: groups: 2 (over y), ctx: 4 (over z), ch: 4 (over x, core).
Axes of the slice: x: 2, y: 2, z: 4, core: 2. Of those that a mesh axis runs over, the one named last changes fastest.
Arguments:
- projections: bfloat16 [1024, 3, 4096], P(('groups', 'ctx'), None, 'ch'), parts along dimension 0, may hold values from -6 to 6
- short_taps: float32 [3, 3, 4096], P(None, None, 'ch'), may hold values from -3 to 3
- residues: float32 [4096, 16], P(('ch', 'ctx')), may hold values from -2 to 2
- decay_rates: float32 [4096, 16], P(('ch', 'ctx')), may hold values from 0.25 to 16
- skip_gain: float32 [4096], P(('ch', 'ctx')), may hold values from -3 to 3
- grad_mixed: bfloat16 [1024, 2048], P(('groups', 'ctx'), 'ch'), parts along dimension 0, may hold values from -6 to 6
- out_weight: bfloat16 [4096, 2048], P('ch', 'ctx'), may hold values from -0.09375 to 0.09375
Outputs:
- grad_projections: bfloat16 [1024, 3, 4096], P(('groups', 'ctx'), None, 'ch'), parts along dimension 0
- grad_short: float32 [6, 3, 4096], P('groups', None, 'ch'), parts along dimension 0
- grad_skip: float32 [8192], P(('groups', 'ch', 'ctx')), parts along dimension 0
- grad_residues: float32 [8192, 16], P(('groups', 'ch', 'ctx')), parts along dimension 0
- grad_log_rates: float32 [8192, 16], P(('groups', 'ch', 'ctx')), parts along dimension 0
- grad_weight: float32 [8192, 2048], P(('groups', 'ch'), 'ctx'), parts along dimension 0
The draws below stay inside these ranges and needn't reach their ends.
There are 2 independent parts, one for each index of `groups`. The reference program is written for one: setup_inputs(seed, part) draws one part's arguments, and reference() takes and returns one part's arrays. A program takes and returns all parts, laid end to end along the dimension named above; an argument that names none is the same for every part. Nothing has to cross between parts.
All inputs are finite; a program needn't handle non-finite values.
Results may differ from the reference program's by a relative error of at most 0.006.
Values may be sent and summed in bfloat16 or wider, within the bound.
A program may use at most 64 MiB of HBM per device.

```python
import math
from functools import partial
import jax
import jax.numpy as jnp
from jax import lax

CHANNELS = 4096
OUT_WIDTH = 2048
SHORT = 3
ORDER = 16
SEQ = 512


def level_of(own_key, extent, cuts, least, high):
    gain = 1.0
    for dim, shards_of in cuts:
        steps = jax.random.uniform(jax.random.fold_in(jax.random.fold_in(own_key, 6), dim), (shards_of,), jnp.float32, least / len(cuts), high / len(cuts))
        gain = gain * jnp.repeat(jnp.exp(steps), extent[dim] // shards_of).reshape((-1,) + (1,) * (len(extent) - 1 - dim))
    return gain


def normal_values(key, extent, deviation, limit, cuts=(), kind=jnp.bfloat16):
    array = deviation * jax.random.normal(key, extent, jnp.float32)
    if cuts:
        array = array * level_of(key, extent, cuts, -0.22, 0.18)
    return jnp.clip(array, -limit, limit).astype(kind)


def setup_inputs(seed: int = 0, part: int = 0) -> dict:
    streams_of = jax.random.split(jax.random.key(seed), 8)
    own_keys = jax.random.split(jax.random.fold_in(streams_of[7], part), 8)
    projections = normal_values(own_keys[0], (SEQ, 3, CHANNELS), 1.0, 6.0, ((0, 4), (2, 4)))
    short_taps = normal_values(streams_of[1], (SHORT, 3, CHANNELS), 0.5, 3.0, ((2, 4),), jnp.float32)
    residues = normal_values(streams_of[2], (CHANNELS, ORDER), 0.3, 2.0, ((0, 16),), jnp.float32)
    decay_rates = jnp.clip(jnp.exp(math.log(16.0) - 4.158883 * jax.random.uniform(streams_of[3], (CHANNELS, ORDER), jnp.float32) ** level_of(streams_of[3], (CHANNELS, ORDER), ((0, 16),), -0.2, 0.2)), 0.25, 16.0)
    skip_gain = normal_values(streams_of[4], (CHANNELS,), 0.5, 3.0, ((0, 16),), jnp.float32)
    grad_mixed = normal_values(own_keys[5], (SEQ, OUT_WIDTH), 1.0, 6.0, ((0, 4), (1, 4)))
    out_weight = normal_values(streams_of[6], (CHANNELS, OUT_WIDTH), CHANNELS ** -0.5, 0.09375, ((0, 4), (1, 4)))
    return dict(projections=projections, short_taps=short_taps, residues=residues, decay_rates=decay_rates, skip_gain=skip_gain, grad_mixed=grad_mixed, out_weight=out_weight)


def make_filter(residues, decay_rates, seq_len):
    positions = jnp.arange(seq_len, dtype=jnp.float32) / seq_len
    amplitude = residues * jnp.sqrt(2.0 * decay_rates / seq_len)
    basis = jnp.exp(-decay_rates[:, :, None] * positions[None, None, :])
    return jnp.einsum('cn,cnt->ct', amplitude, basis, precision=lax.Precision.HIGHEST)

def reference(projections, short_taps, residues, decay_rates, skip_gain, grad_mixed, out_weight):
    seq_len = projections.shape[0]
    norm_factor = math.sqrt(seq_len)
    padded_in = jnp.pad(projections.astype(jnp.float32), ((SHORT - 1, 0), (0, 0), (0, 0)))
    mixed_in = jnp.zeros(projections.shape, jnp.float32)
    for lag_index in range(SHORT):
        start_row = SHORT - 1 - lag_index
        mixed_in = mixed_in + short_taps[lag_index] * padded_in[start_row:start_row + seq_len]
    query_rows = mixed_in[:, 0]
    key_rows = mixed_in[:, 1]
    value_rows = mixed_in[:, 2]
    gated_rows = (key_rows * value_rows).astype(jnp.bfloat16)
    grad_out = jnp.dot(grad_mixed, out_weight.T, preferred_element_type=jnp.float32)
    grad_y = (grad_out * query_rows).astype(jnp.bfloat16)
    width = 256
    count = CHANNELS // width
    length = 2 * seq_len

    def long_block(inputs):
        res_blk, rate_blk, gain_blk, gate_blk, grad_blk = inputs
        long_filter, filter_vjp = jax.vjp(partial(make_filter, seq_len=seq_len), res_blk, rate_blk)
        gate_f = gate_blk.astype(jnp.float32)
        grad_f = grad_blk.astype(jnp.float32)
        spec_h = jnp.fft.rfft(long_filter, n=length)
        spec_u = jnp.fft.rfft(gate_f, n=length)
        spec_g = jnp.fft.rfft(grad_f, n=length)
        mix_cols = (jnp.fft.irfft(spec_h * spec_u, n=length)[:, :seq_len] + gain_blk[:, None] * gate_f).astype(jnp.bfloat16)
        grad_cols = (jnp.fft.irfft(jnp.conj(spec_h) * spec_g, n=length)[:, :seq_len] + gain_blk[:, None] * grad_f).astype(jnp.bfloat16)
        grad_filter = jnp.fft.irfft(spec_g * jnp.conj(spec_u), n=length)[:, :seq_len].astype(jnp.float32)
        grad_res, grad_rate = filter_vjp(grad_filter)
        skip_sum = lax.optimization_barrier(jnp.sum(grad_f * gate_f, axis=1))
        return (mix_cols, grad_cols, grad_res / norm_factor, grad_rate * rate_blk / norm_factor, skip_sum / norm_factor)
    mix_b, grad_b, res_b, rate_b, skip_b = lax.map(long_block, (residues.reshape(count, width, ORDER), decay_rates.reshape(count, width, ORDER), skip_gain.reshape(count, width), gated_rows.T.reshape(count, width, seq_len), grad_y.T.reshape(count, width, seq_len)))
    mix_rows = mix_b.reshape(CHANNELS, seq_len).T
    grad_gated = grad_b.reshape(CHANNELS, seq_len).T
    grad_residues = res_b.reshape(CHANNELS, ORDER)
    grad_log_rates = rate_b.reshape(CHANNELS, ORDER)
    grad_skip = skip_b.reshape(CHANNELS)
    mixed_out = (query_rows * mix_rows).astype(jnp.bfloat16)
    grad_mix = jnp.stack([grad_out * mix_rows, grad_gated * value_rows, grad_gated * key_rows], axis=1)
    padded_grad = jnp.pad(grad_mix, ((0, SHORT - 1), (0, 0), (0, 0)))
    running = jnp.zeros(grad_mix.shape, jnp.float32)
    short_terms = []
    for lag_index in range(SHORT):
        running = running + short_taps[lag_index] * padded_grad[lag_index:lag_index + seq_len]
        start_row = SHORT - 1 - lag_index
        short_terms.append(lax.optimization_barrier(jnp.sum(grad_mix * padded_in[start_row:start_row + seq_len], axis=0)))
    grad_projections = running.astype(jnp.bfloat16)
    grad_short = jnp.stack(short_terms, axis=0) / norm_factor
    grad_weight = jnp.dot(mixed_out.T, grad_mixed, preferred_element_type=jnp.float32) / norm_factor
    return (grad_projections, grad_short, grad_skip, grad_residues, grad_log_rates, grad_weight)
```

```python
from functools import partial
import math

import jax
import jax.numpy as jnp
import numpy as np
from jax import lax
from jax.experimental import pallas as pl
from jax.experimental.pallas import tpu as pltpu
from jax.sharding import PartitionSpec as P

SHORT = 3


def from_behind(x, axis, by):
    peers = lax.axis_size(axis)
    pairs = [(i, i + by) for i in range(peers) if 0 <= i + by < peers]
    return lax.ppermute(x, axis, pairs)


def make_filter(residues, decay_rates, seq_len):
    positions = jnp.arange(seq_len, dtype=jnp.float32) / seq_len
    amplitude = residues * jnp.sqrt(2.0 * decay_rates / seq_len)
    basis = jnp.exp(-decay_rates[:, :, None] * positions[None, None, :])
    return jnp.einsum("cn,cnt->ct", amplitude, basis, precision=lax.Precision.HIGHEST)


def circle(rows_count, cols_count, period):
    left_idx = jnp.arange(rows_count, dtype=jnp.int32)[:, None]
    right_idx = jnp.arange(cols_count, dtype=jnp.int32)[None, :]
    angle = (left_idx * right_idx % period).astype(jnp.float32) * (2.0 * math.pi / period)
    return (jnp.cos(angle), jnp.sin(angle))


def spectral_tables(length):
    factor_a = 1
    while factor_a * factor_a * 4 <= length and length % (factor_a * 2) == 0:
        factor_a = factor_a * 2
    factor_b = length // factor_a
    a_cos, a_sin = circle(factor_a, factor_a, factor_a)
    b_cos, b_sin = circle(factor_b, factor_b, factor_b)
    t_cos, t_sin = circle(factor_a, factor_b, length)
    return (length, factor_a, factor_b, a_cos, a_sin, b_cos, b_sin, t_cos, t_sin)


def forward_dft(signal, tables):
    length, factor_a, factor_b, a_cos, a_sin, b_cos, b_sin, t_cos, t_sin = tables
    highest = lax.Precision.HIGHEST
    channels, seq_len = signal.shape
    grid = jnp.pad(signal, ((0, 0), (0, length - seq_len))).reshape(channels, factor_a, factor_b)
    part_real = jnp.einsum("ka,cab->ckb", a_cos, grid, precision=highest)
    part_imag = -jnp.einsum("ka,cab->ckb", a_sin, grid, precision=highest)
    turn_real = part_real * t_cos + part_imag * t_sin
    turn_imag = part_imag * t_cos - part_real * t_sin
    out_real = jnp.einsum("ckb,bm->ckm", turn_real, b_cos, precision=highest) + jnp.einsum(
        "ckb,bm->ckm", turn_imag, b_sin, precision=highest
    )
    out_imag = jnp.einsum("ckb,bm->ckm", turn_imag, b_cos, precision=highest) - jnp.einsum(
        "ckb,bm->ckm", turn_real, b_sin, precision=highest
    )
    return (out_real, out_imag)


def inverse_dft(spec_real, spec_imag, seq_len, tables):
    length, factor_a, factor_b, a_cos, a_sin, b_cos, b_sin, t_cos, t_sin = tables
    highest = lax.Precision.HIGHEST
    channels = spec_real.shape[0]
    mid_real = jnp.einsum("ckm,mb->ckb", spec_real, b_cos, precision=highest) - jnp.einsum(
        "ckm,mb->ckb", spec_imag, b_sin, precision=highest
    )
    mid_imag = jnp.einsum("ckm,mb->ckb", spec_imag, b_cos, precision=highest) + jnp.einsum(
        "ckm,mb->ckb", spec_real, b_sin, precision=highest
    )
    turn_real = mid_real * t_cos - mid_imag * t_sin
    turn_imag = mid_imag * t_cos + mid_real * t_sin
    values = jnp.einsum("ak,ckb->cab", a_cos, turn_real, precision=highest) - jnp.einsum(
        "ak,ckb->cab", a_sin, turn_imag, precision=highest
    )
    return values.reshape(channels, length)[:, :seq_len] / length


def short_mix(extended, short_taps, tokens):
    running = jnp.zeros((tokens,) + extended.shape[1:], jnp.float32)
    for lag_index in range(SHORT):
        start_row = SHORT - 1 - lag_index
        running = running + short_taps[lag_index] * extended[start_row : start_row + tokens]
    return running


def mix_long(gate_cols, spec_h, gain, seq_len, tables):
    gate_f = gate_cols.astype(jnp.float32)
    u_real, u_imag = forward_dft(gate_f, tables)
    prod_real = spec_h[0] * u_real - spec_h[1] * u_imag
    prod_imag = spec_h[0] * u_imag + spec_h[1] * u_real
    mix_cols = (inverse_dft(prod_real, prod_imag, seq_len, tables) + gain[:, None] * gate_f).astype(
        jnp.bfloat16
    )
    return (mix_cols, (u_real, u_imag))


def grad_long(grad_cols_in, gate_cols, spec_u, spec_h, gain, seq_len, tables):
    grad_f = grad_cols_in.astype(jnp.float32)
    g_real, g_imag = forward_dft(grad_f, tables)
    back_real = spec_h[0] * g_real + spec_h[1] * g_imag
    back_imag = spec_h[0] * g_imag - spec_h[1] * g_real
    grad_cols = (
        inverse_dft(back_real, back_imag, seq_len, tables) + gain[:, None] * grad_f
    ).astype(jnp.bfloat16)
    corr_real = g_real * spec_u[0] + g_imag * spec_u[1]
    corr_imag = g_imag * spec_u[0] - g_real * spec_u[1]
    grad_filter = inverse_dft(corr_real, corr_imag, seq_len, tables)
    skip_sum = jnp.sum(grad_f * gate_cols.astype(jnp.float32), axis=1)
    return (grad_cols, grad_filter, skip_sum)


def body_factored(projections, short_taps, residues, decay_rates, skip_gain, grad_mixed, out_weight):
    tokens = projections.shape[0]
    seq_len = tokens * lax.axis_size("ctx")
    norm_factor = math.sqrt(seq_len)
    tables = spectral_tables(2 * seq_len)
    earlier = from_behind(projections[tokens - SHORT + 1 :], "ctx", 1)
    ext_proj = jnp.concatenate([earlier, projections], axis=0)
    mixed_in = short_mix(ext_proj, short_taps, tokens)
    query_rows = mixed_in[:, 0]
    key_rows = mixed_in[:, 1]
    value_rows = mixed_in[:, 2]
    gated_rows = (key_rows * value_rows).astype(jnp.bfloat16)
    long_filter, filter_vjp = jax.vjp(partial(make_filter, seq_len=seq_len), residues, decay_rates)
    spec_h = forward_dft(long_filter, tables)
    out_rows = lax.all_gather(grad_mixed, "ch", axis=1, tiled=True)
    grad_out = lax.dot_general(
        out_rows,
        lax.all_gather(out_weight, "ctx", axis=1, tiled=True),
        (((1,), (1,)), ((), ())),
        preferred_element_type=jnp.float32,
    )
    grad_y = (grad_out * query_rows).astype(jnp.bfloat16)
    gate_cols, grad_cols_in = (
        lax.all_to_all(gated_rows.T, "ctx", split_axis=0, concat_axis=1, tiled=True),
        lax.all_to_all(grad_y.T, "ctx", split_axis=0, concat_axis=1, tiled=True),
    )
    mix_cols, spec_u = mix_long(gate_cols, spec_h, skip_gain, seq_len, tables)
    grad_cols, grad_filter, skip_sum = grad_long(
        grad_cols_in, gate_cols, spec_u, spec_h, skip_gain, seq_len, tables
    )
    returned = (
        lax.all_to_all(mix_cols, "ctx", split_axis=1, concat_axis=0, tiled=True),
        lax.all_to_all(grad_cols, "ctx", split_axis=1, concat_axis=0, tiled=True),
    )
    mix_rows = returned[0].T
    grad_gated = returned[1].T
    grad_res, grad_rate = filter_vjp(grad_filter)
    grad_residues = grad_res / norm_factor
    grad_log_rates = grad_rate * decay_rates / norm_factor
    grad_skip = skip_sum / norm_factor
    mixed_out = (query_rows * mix_rows).astype(jnp.bfloat16)
    grad_mix = jnp.stack(
        [grad_out * mix_rows, grad_gated * value_rows, grad_gated * key_rows], axis=1
    )
    later = from_behind(grad_mix[: SHORT - 1], "ctx", -1)
    ext_grad = jnp.concatenate([grad_mix, later], axis=0)
    running = jnp.zeros(grad_mix.shape, jnp.float32)
    short_terms = []
    for lag_index in range(SHORT):
        running = running + short_taps[lag_index] * ext_grad[lag_index : lag_index + tokens]
        start_row = SHORT - 1 - lag_index
        short_terms.append(jnp.sum(grad_mix * ext_proj[start_row : start_row + tokens], axis=0))
    grad_projections = running.astype(jnp.bfloat16)
    grad_short = lax.psum(jnp.stack(short_terms, axis=0), "ctx") / norm_factor
    partial_term = lax.dot_general(
        mixed_out, out_rows, (((0,), (0,)), ((), ())), preferred_element_type=jnp.float32
    )
    weight_sum = lax.psum_scatter(partial_term, "ctx", scatter_dimension=1, tiled=True)
    grad_weight = weight_sum / norm_factor
    return (grad_projections, grad_short, grad_skip, grad_residues, grad_log_rates, grad_weight)


def split(x):
    high = x.astype(jnp.bfloat16)
    return high, (x - high.astype(jnp.float32)).astype(jnp.bfloat16)


LANES = 256


def line_tables(tokens):
    steps = np.arange(tokens, dtype=np.int64)[None, :]
    freqs = 2 * np.arange(tokens, dtype=np.int64)[:, None] + 1
    angle = (freqs * steps % (4 * tokens)) * (2.0 * math.pi / (4 * tokens))
    wave = np.concatenate([np.cos(angle), np.sin(angle)], axis=0).astype(np.float32)
    high = wave.astype(jnp.bfloat16)
    low = (wave - high.astype(np.float32)).astype(jnp.bfloat16)
    ahead = np.concatenate([high, low], axis=1)
    back = np.concatenate([high.T, low.T], axis=0)
    return ahead, back


def fused_kernel(
    peers,
    chans,
    order,
    proj,
    taps,
    params,
    gm,
    weight,
    ahead,
    back,
    gproj,
    gshort,
    gparams,
    gweight,
    par,
    halo,
    ext,
    qkv,
    gated,
    drop,
    states,
    s_in,
    s_out,
    pq,
    ab,
    mix,
    gm_all,
    up_in,
    up_out,
    dn_in,
    dn_out,
    mo_all,
    go,
    gy,
    gg,
    gf,
    r_in,
    r_out,
    mom_out,
    mom_in,
    gx,
    sh_in,
    local_sem,
    halo_sem,
    par_sem,
    gm1_sem,
    gm2_sem,
    s_sem,
    up_sem,
    dn_sem,
    agu_sem,
    agd_sem,
    r_sem,
    mom_sem,
    gx_sem,
    sh_sem,
):
    f32, bf16 = jnp.float32, jnp.bfloat16
    k = lax.axis_index("ctx")
    j = lax.axis_index("ch")
    _, tokens, width = proj.shape
    cols = width // peers
    quarter = tokens // chans
    half = tokens // 2
    seq_len = tokens * peers
    norm = math.sqrt(seq_len)
    last = peers - 1

    def copy(src, dst, send, recv, where):
        return pltpu.make_async_remote_copy(
            src_ref=src,
            dst_ref=dst,
            send_sem=send,
            recv_sem=recv,
            device_id=where,
            device_id_type=pl.DeviceIdType.MESH,
        )

    def tiles(fn, lanes=LANES):
        def step(i, carry):
            fn(pl.ds(pl.multiple_of(i * lanes, lanes), lanes))
            return carry

        lax.fori_loop(0, width // lanes, step, 0)

    def dot(a, b):
        return lax.dot_general(a, b, (((1,), (0,)), ((), ())), preferred_element_type=f32)

    def forward_exact(x):
        return dot(ahead[...], jnp.concatenate([x, x], axis=0))

    def forward(x):
        high, low = split(x)
        return forward_exact(high) + dot(ahead[:, :tokens], low)

    def backward(top, bottom):
        high, low = split(jnp.concatenate([top, bottom], axis=0))
        both = dot(back[...], high)
        return (both[:tokens] + both[tokens:] + dot(back[:tokens], low)) * (1.0 / tokens)

    barrier = pltpu.get_barrier_semaphore()
    for dk in range(peers):
        for dj in range(chans):
            if dk or dj:
                pl.semaphore_signal(
                    barrier,
                    inc=1,
                    device_id={"ctx": lax.rem(k + dk, peers), "ch": lax.rem(j + dj, chans)},
                    device_id_type=pl.DeviceIdType.MESH,
                )
    pl.semaphore_wait(barrier, peers * chans - 1)

    def gm_first(d):
        q = lax.rem(j + d, chans)
        return copy(
            gm.at[pl.ds(pl.multiple_of(q * quarter, quarter), quarter)],
            gm_all.at[k, q],
            gm1_sem.at[0, d],
            gm1_sem.at[1, k],
            {"ctx": j, "ch": q},
        )

    def gm_own():
        return pltpu.make_async_copy(
            gm.at[pl.ds(pl.multiple_of(j * quarter, quarter), quarter)], gm_all.at[k, j], local_sem
        )

    for d in range(1, chans):
        gm_first(d).start()

    @pl.when(j != k)
    def _():
        gm_first(0).start()

    @pl.when(j == k)
    def _():
        gm_own().start()

    halo_copy = copy(
        proj.at[:, tokens - 16 : tokens], halo, halo_sem.at[0], halo_sem.at[1], {"ctx": lax.rem(k + 1, peers)}
    )

    @pl.when(k < last)
    def _():
        halo_copy.start()

    mine = pl.ds(pl.multiple_of(k * cols, cols), cols)

    def par_copy(d):
        return copy(params, par.at[:, mine], par_sem.at[0, d], par_sem.at[1, d], {"ctx": lax.rem(k + d, peers)})

    for d in range(1, peers):
        par_copy(d).start()
    par[:, mine] = params[...]

    def widen(at):
        for g in range(3):
            ext[g, 8 : 8 + tokens, at] = proj[g, :, at].astype(f32)

    tiles(widen)

    @pl.when(k > 0)
    def _():
        halo_copy.wait_recv()
        for g in range(3):
            ext[g, 0:8] = halo[g].astype(f32)[8:]

    @pl.when(k == 0)
    def _():
        for g in range(3):
            ext[g, 0:8] = jnp.zeros((8, width), f32)

    def short(at):
        rows = []
        for g in range(3):
            total = taps[0, g : g + 1, at] * ext[g, 8 : 8 + tokens, at]
            for lag in range(1, SHORT):
                total = total + taps[lag, g : g + 1, at] * ext[g, 8 - lag : 8 - lag + tokens, at]
            qkv[g, :, at] = total
            rows.append(total)
        gated[:, at] = (rows[1] * rows[2]).astype(bf16).astype(f32)

    tiles(short, 128)

    def gm_second(b, d):
        return copy(
            gm_all.at[b, j],
            gm_all.at[b, j],
            gm2_sem.at[0, b, d],
            gm2_sem.at[1, b, d],
            {"ch": lax.rem(j + d, chans)},
        )

    def gm_arrived(b):
        copy(gm_all.at[b, j], gm_all.at[b, j], gm1_sem.at[0, 0], gm1_sem.at[1, b], {"ctx": k, "ch": j}).wait_recv()

    for b in range(peers):

        @pl.when((j != k) | (k != b))
        def _():
            gm_arrived(b)

        @pl.when((j == k) & (k == b))
        def _():
            gm_own().wait()

        for d in range(1, chans):
            gm_second(b, d).start()

    for d in range(1, peers):
        par_copy(d).wait_recv()
    rate = par[0:order]
    drop[0] = jnp.exp(rate * (-1.0 / seq_len))
    drop[1] = jnp.exp(rate * (-8.0 / seq_len))
    drop[2] = jnp.exp(rate * (-16.0 / seq_len))
    drop[3] = jnp.exp(rate * (-32.0 / seq_len))
    drop[4] = jnp.exp(rate * (-float(tokens) / seq_len))
    drop[5] = par[order : 2 * order] * jnp.sqrt(2.0 * rate / seq_len)

    def scan_up(source):
        decay = drop[0]

        def step(i, carry):
            s, s1 = carry
            for r in range(8):
                u = s + source[pl.ds(i * 8 + r, 1)]
                s1 = decay * (s1 + u)
                s = decay * u
            return s, s1

        zero = jnp.zeros((order, width), f32)
        return lax.fori_loop(0, tokens // 8, step, (zero, zero))

    def scan_down(source):
        decay = drop[0]

        def step(i, carry):
            s, s1 = carry
            for r in range(8):
                s1 = decay * (s1 + s)
                s = decay * s + source[pl.ds(tokens - 1 - i * 8 - r, 1)]
            return s, s1

        zero = jnp.zeros((order, width), f32)
        return lax.fori_loop(0, tokens // 8, step, (zero, zero))

    def spread(head, at, start, falling):
        lanes = at.size
        iota = lax.broadcasted_iota(jnp.int32, (8, lanes), 0).astype(f32)
        place = (iota if falling else 7.0 - iota) + start
        count = tokens // 8

        def mode(n, acc):
            row = pl.ds(n, 1)
            v = head(row) * jnp.exp(par[row, at] * (place * (-1.0 / seq_len)))
            d8, d16, d32 = drop[1, row, at], drop[2, row, at], drop[3, row, at]
            first = [v, v * d8]
            first = first + [x * d16 for x in first]
            out = []
            for i in range(0, count, 4):
                out += [acc[i + m] + first[m] for m in range(4)]
                first = [x * d32 for x in first]
            return tuple(out)

        zero = jnp.zeros((8, lanes), f32)
        acc = lax.fori_loop(0, order, mode, (zero,) * count)
        return jnp.concatenate(acc if falling else acc[::-1], axis=0)

    s0, s1 = scan_up(gated)
    states[0] = s0
    states[1] = s1

    def s_copy(i):
        return copy(s_out.at[i], s_in.at[i], s_sem.at[0, i], s_sem.at[1, i], {"ctx": lax.rem(k + 1, peers)})

    @pl.when(k == 0)
    def _():
        s_in[...] = jnp.zeros(s_in.shape, f32)
        s_out[...] = states[...]
        s_copy(0).start()
        s_copy(1).start()

    def conv(at):
        filt = spread(lambda row: drop[5, row, at], at, 0.0, True)
        f = forward(filt)
        x = gated[:, at]
        u = forward_exact(x.astype(bf16))
        pq[:, at] = f
        ab[:, at] = u
        p, q, a, b = f[:tokens], f[tokens:], u[:tokens], u[tokens:]
        mix[:, at] = backward(p * a - q * b, p * b + q * a) + par[2 * order : 2 * order + 1, at] * x

    tiles(conv)

    @pl.when(k > 0)
    def _():
        s_copy(0).wait_recv()

        @pl.when(k < last)
        def _():
            s_out[0] = states[0] + drop[4] * s_in[0]
            s_copy(0).start()

    for b in range(peers):
        for d in range(1, chans):
            gm_second(b, d).wait_recv()

    def part(b, c, at):
        rows = gm_all[b, c * (chans // 2) : (c + 1) * (chans // 2)].reshape(half, gm_all.shape[-1])
        return lax.dot_general(
            rows, weight[at, :], (((1,), (1,)), ((), ())), preferred_element_type=f32
        )

    def up_copy(b, c):
        rows = pl.ds(c * half, half)
        return copy(
            up_out.at[b, rows], up_in.at[b, rows], up_sem.at[0, b, c], up_sem.at[1, b, c],
            {"ctx": lax.rem(k + 1, peers)},
        )

    def dn_copy(b, c):
        rows = pl.ds(c * half, half)
        return copy(
            dn_out.at[b, rows], dn_in.at[b, rows], dn_sem.at[0, b, c], dn_sem.at[1, b, c],
            {"ctx": lax.rem(k + peers - 1, peers)},
        )

    def hop(make, source, sink, first, middle, b, c):
        rows = slice(c * half, (c + 1) * half)

        @pl.when(first)
        def _():
            def fill(at):
                sink[b, rows, at] = part(b, c, at).astype(bf16)

            tiles(fill)
            make(b, c).start()

        @pl.when(middle)
        def _():
            make(b, c).wait_recv()

            def fill(at):
                sink[b, rows, at] = (part(b, c, at) + source[b, rows, at].astype(f32)).astype(bf16)

            tiles(fill)
            make(b, c).start()

    for i in range(peers - 1):
        for c in range(2):
            b = last - i
            hop(up_copy, up_in, up_out, k == 0, (k > 0) & (k < b), b, c)
            hop(dn_copy, dn_in, dn_out, k == last, (k < last) & (k > i), i, c)

    def finish_mix(at):
        total = mix[:, at] + spread(lambda row: drop[5, row, at] * s_in[0, row, at], at, 0.0, True)
        total = total.astype(bf16).astype(f32)
        mix[:, at] = total
        mo_all[k, at] = (qkv[0, :, at] * total).T.astype(bf16)

    tiles(finish_mix)

    def agu_copy(d):
        s = lax.rem(k + peers - d, peers)
        return copy(
            mo_all.at[s], mo_all.at[s], agu_sem.at[0, d], agu_sem.at[1, d + 1], {"ctx": lax.rem(k + 1, peers)}
        )

    def agu_wait(d):
        s = lax.rem(k + peers - d, peers)
        copy(mo_all.at[s], mo_all.at[s], agu_sem.at[0, d], agu_sem.at[1, d], {"ctx": k}).wait_recv()

    def agd_copy(d):
        s = lax.rem(k + d, peers)
        return copy(
            mo_all.at[s], mo_all.at[s], agd_sem.at[0, d], agd_sem.at[1, d + 1],
            {"ctx": lax.rem(k + peers - 1, peers)},
        )

    def agd_wait(d):
        s = lax.rem(k + d, peers)
        copy(mo_all.at[s], mo_all.at[s], agd_sem.at[0, d], agd_sem.at[1, d], {"ctx": k}).wait_recv()

    @pl.when(k < last)
    def _():
        agu_copy(0).start()

    @pl.when(k > 0)
    def _():
        agd_copy(0).start()

    @pl.when(k > 0)
    def _():
        s_copy(1).wait_recv()

        @pl.when(k < last)
        def _():
            s_out[1] = states[1] + drop[4] * (s_in[1] + float(tokens) * s_in[0])
            s_copy(1).start()

    @pl.when(k > 0)
    def _():
        for c in range(2):
            copy(
                up_out.at[k, pl.ds(c * half, half)], up_in.at[k, pl.ds(c * half, half)],
                up_sem.at[0, k, c], up_sem.at[1, k, c], {"ctx": k},
            ).wait_recv()

    @pl.when(k < last)
    def _():
        for c in range(2):
            copy(
                dn_out.at[k, pl.ds(c * half, half)], dn_in.at[k, pl.ds(c * half, half)],
                dn_sem.at[0, k, c], dn_sem.at[1, k, c], {"ctx": k},
            ).wait_recv()

    @pl.when(k == 0)
    def _():
        up_in[0] = jnp.zeros(up_in.shape[1:], bf16)

    @pl.when(k == last)
    def _():
        dn_in[last] = jnp.zeros(dn_in.shape[1:], bf16)

    def own(at):
        rows = gm_all[k].reshape(tokens, gm_all.shape[-1])
        total = lax.dot_general(
            rows, weight[at, :], (((1,), (1,)), ((), ())), preferred_element_type=f32
        )
        total = total + up_in[k, :, at].astype(f32) + dn_in[k, :, at].astype(f32)
        go[:, at] = total
        gy[:, at] = (total * qkv[0, :, at]).astype(bf16).astype(f32)

    tiles(own)

    g0, g1 = scan_down(gy)
    states[0] = g0
    states[1] = g1

    r_copy = copy(r_out, r_in, r_sem.at[0], r_sem.at[1], {"ctx": lax.rem(k + peers - 1, peers)})

    @pl.when(k == last)
    def _():
        r_in[...] = jnp.zeros(r_in.shape, f32)
        r_out[...] = states[0]
        r_copy.start()

    def conv_back(at):
        x = gy[:, at]
        w = forward_exact(x.astype(bf16))
        f, u = pq[:, at], ab[:, at]
        p, q, a, b = f[:tokens], f[tokens:], u[:tokens], u[tokens:]
        d, e = w[:tokens], w[tokens:]
        gg[:, at] = backward(p * d + q * e, p * e - q * d) + par[2 * order : 2 * order + 1, at] * x
        gf[:, at] = backward(d * a + e * b, e * a - d * b)
        mom_out[2 * order : 2 * order + 8, at] = jnp.broadcast_to(
            jnp.sum(x * gated[:, at], axis=0, keepdims=True) / norm, (8, x.shape[1])
        )

    tiles(conv_back)

    @pl.when(k < last)
    def _():
        r_copy.wait_recv()

        @pl.when(k > 0)
        def _():
            r_out[...] = states[0] + drop[4] * r_in[...]
            r_copy.start()

    m0, m1 = scan_down(gf)
    m0 = m0 + states[0] * s_in[0]
    m1 = m1 + states[1] * s_in[0] + states[0] * s_in[1]
    mom_out[0:order] = jnp.sqrt(2.0 * par[0:order] / seq_len) * m0 * (1.0 / norm)
    mom_out[order : 2 * order] = drop[5] * (0.5 * m0 - par[0:order] * m1 * (1.0 / seq_len)) * (1.0 / norm)

    def mom_copy(d):
        to = lax.rem(k + d, peers)
        return copy(
            mom_out.at[:, pl.ds(pl.multiple_of(to * cols, cols), cols)],
            mom_in.at[d],
            mom_sem.at[0, d],
            mom_sem.at[1, d],
            {"ctx": to},
        )

    for d in range(1, peers):
        mom_copy(d).start()

    def grads(at):
        total = gg[:, at] + spread(lambda row: drop[5, row, at] * r_in[row, at], at, 1.0, False)
        total = total.astype(bf16).astype(f32)
        gx[0, 0:tokens, at] = go[:, at] * mix[:, at]
        gx[1, 0:tokens, at] = total * qkv[2, :, at]
        gx[2, 0:tokens, at] = total * qkv[1, :, at]

    tiles(grads)

    gx_copy = copy(
        gx.at[:, 0:8], gx.at[:, tokens : tokens + 8], gx_sem.at[0], gx_sem.at[1],
        {"ctx": lax.rem(k + peers - 1, peers)},
    )

    @pl.when(k > 0)
    def _():
        gx_copy.start()

    def shorts(at):
        rows = []
        for lag in range(SHORT):
            for g in range(3):
                rows.append(
                    jnp.sum(gx[g, 0:tokens, at] * ext[g, 8 - lag : 8 - lag + tokens, at], axis=0, keepdims=True)
                )
        rows.append(jnp.zeros((16 - len(rows), rows[0].shape[1]), f32))
        sh_in[0, :, at] = jnp.concatenate(rows, axis=0) * (1.0 / norm)

    tiles(shorts, 128)

    def sh_copy(d):
        return copy(sh_in.at[0], sh_in.at[d], sh_sem.at[0, d], sh_sem.at[1, d], {"ctx": lax.rem(k + d, peers)})

    for d in range(1, peers):
        sh_copy(d).start()

    @pl.when(k < last)
    def _():
        gx_copy.wait_recv()

    @pl.when(k == last)
    def _():
        gx[:, tokens : tokens + 8] = jnp.zeros((3, 8, width), f32)

    def out_rows(at):
        for g in range(3):
            total = taps[0, g : g + 1, at] * gx[g, 0:tokens, at]
            for lag in range(1, SHORT):
                total = total + taps[lag, g : g + 1, at] * gx[g, lag : lag + tokens, at]
            gproj[g, :, at] = total.astype(bf16)

    tiles(out_rows, 128)

    for d in range(1, peers):

        @pl.when(k >= d)
        def _():
            agu_wait(d)

            @pl.when(k < last)
            def _():
                agu_copy(d).start()

        @pl.when(k + d < peers)
        def _():
            agd_wait(d)

            @pl.when(k > 0)
            def _():
                agd_copy(d).start()

    def weight_rows(at):
        left = jnp.concatenate([mo_all[b, at] for b in range(peers)], axis=1)
        right = gm_all[...].reshape(seq_len, gm_all.shape[-1])
        gweight[at, :] = dot(left, right) * (1.0 / norm)

    tiles(weight_rows)

    for d in range(1, peers):
        mom_copy(d).wait_recv()
    gparams[...] = sum((mom_in[d] for d in range(1, peers)), mom_out[:, mine])
    for d in range(1, peers):
        sh_copy(d).wait_recv()
    gshort[...] = sum((sh_in[d] for d in range(1, peers)), sh_in[0])

    for d in range(1, chans):
        gm_first(d).wait_send()

    @pl.when(j != k)
    def _():
        gm_first(0).wait_send()

    for b in range(peers):
        for d in range(1, chans):
            gm_second(b, d).wait_send()
    for d in range(1, peers):
        par_copy(d).wait_send()
        mom_copy(d).wait_send()
        sh_copy(d).wait_send()

    @pl.when(k < last)
    def _():
        halo_copy.wait_send()
        s_copy(0).wait_send()
        s_copy(1).wait_send()

    @pl.when(k > 0)
    def _():
        r_copy.wait_send()
        gx_copy.wait_send()

    for i in range(peers - 1):
        for c in range(2):

            @pl.when(k < last - i)
            def _():
                up_copy(last - i, c).wait_send()

            @pl.when(k > i)
            def _():
                dn_copy(i, c).wait_send()

    for d in range(peers - 1):

        @pl.when((k >= d) & (k < last))
        def _():
            agu_copy(d).wait_send()

        @pl.when((k + d < peers) & (k > 0))
        def _():
            agd_copy(d).wait_send()


def body_fused(projections, short_taps, residues, decay_rates, skip_gain, grad_mixed, out_weight):
    tokens, _, width = projections.shape
    peers, chans = lax.axis_size("ctx"), lax.axis_size("ch")
    order = residues.shape[1]
    cols = width // peers
    wide = out_weight.shape[1]
    f32, bf16 = jnp.float32, jnp.bfloat16
    params = jnp.concatenate(
        [decay_rates.T, residues.T, jnp.broadcast_to(skip_gain[None], (8, cols))], axis=0
    )
    ahead, back = line_tables(tokens)
    rows = 2 * order + 8
    vmem = pl.BlockSpec(memory_space=pltpu.VMEM)
    dma = pltpu.SemaphoreType.DMA
    gproj, gshort, gparams, gweight = pl.pallas_call(
        partial(fused_kernel, peers, chans, order),
        out_shape=(
            jax.ShapeDtypeStruct((3, tokens, width), bf16),
            jax.ShapeDtypeStruct((16, width), f32),
            jax.ShapeDtypeStruct((rows, cols), f32),
            jax.ShapeDtypeStruct((width, wide), f32),
        ),
        in_specs=[vmem] * 7,
        out_specs=(vmem,) * 4,
        scratch_shapes=[
            pltpu.VMEM((rows, width), f32),
            pltpu.VMEM((3, 16, width), bf16),
            pltpu.VMEM((3, tokens + 8, width), f32),
            pltpu.VMEM((3, tokens, width), f32),
            pltpu.VMEM((tokens, width), f32),
            pltpu.VMEM((6, order, width), f32),
            pltpu.VMEM((2, order, width), f32),
            pltpu.VMEM((2, order, width), f32),
            pltpu.VMEM((2, order, width), f32),
            pltpu.VMEM((2 * tokens, width), f32),
            pltpu.VMEM((2 * tokens, width), f32),
            pltpu.VMEM((tokens, width), f32),
            pltpu.VMEM((peers, chans, tokens // chans, wide), bf16),
            pltpu.VMEM((peers, tokens, width), bf16),
            pltpu.VMEM((peers, tokens, width), bf16),
            pltpu.VMEM((peers, tokens, width), bf16),
            pltpu.VMEM((peers, tokens, width), bf16),
            pltpu.VMEM((peers, width, tokens), bf16),
            pltpu.VMEM((tokens, width), f32),
            pltpu.VMEM((tokens, width), f32),
            pltpu.VMEM((tokens, width), f32),
            pltpu.VMEM((tokens, width), f32),
            pltpu.VMEM((order, width), f32),
            pltpu.VMEM((order, width), f32),
            pltpu.VMEM((rows, width), f32),
            pltpu.VMEM((peers, rows, cols), f32),
            pltpu.VMEM((3, tokens + 8, width), f32),
            pltpu.VMEM((peers, 16, width), f32),
            dma,
            dma((2,)),
            dma((2, peers)),
            dma((2, max(peers, chans))),
            dma((2, peers, chans)),
            dma((2, 2)),
            dma((2, peers, 2)),
            dma((2, peers, 2)),
            dma((2, peers)),
            dma((2, peers)),
            dma((2,)),
            dma((2, peers)),
            dma((2,)),
            dma((2, peers)),
        ],
        compiler_params=pltpu.CompilerParams(
            collective_id=0, has_side_effects=True, vmem_limit_bytes=56 * 1024 * 1024
        ),
    )(
        projections.transpose(1, 0, 2),
        short_taps,
        params,
        grad_mixed,
        out_weight,
        jnp.asarray(ahead),
        jnp.asarray(back),
    )
    return (
        gproj.transpose(1, 0, 2),
        gshort[: SHORT * 3].reshape(SHORT, 3, width),
        gparams[2 * order],
        gparams[:order].T,
        gparams[order : 2 * order].T,
        gweight,
    )


def body(*args):
    peers, chans = lax.axis_size("ctx"), lax.axis_size("ch")
    if peers * args[0].shape[0] > 1024 or peers != chans:
        return body_factored(*args)
    return body_fused(*args)


def solution(mesh):
    return jax.shard_map(
        body,
        mesh=mesh,
        in_specs=(
            P(("groups", "ctx"), None, "ch"),
            P(None, None, "ch"),
            P(("ch", "ctx"), None),
            P(("ch", "ctx"), None),
            P(("ch", "ctx")),
            P(("groups", "ctx"), "ch"),
            P("ch", "ctx"),
        ),
        out_specs=(
            P(("groups", "ctx"), None, "ch"),
            P("groups", None, "ch"),
            P(("groups", "ch", "ctx")),
            P(("groups", "ch", "ctx"), None),
            P(("groups", "ch", "ctx"), None),
            P(("groups", "ch"), "ctx"),
        ),
        check_vma=False,
    )
```

```python
from functools import partial
import math

import jax
import jax.numpy as jnp
import numpy as np
from jax import lax
from jax.experimental import pallas as pl
from jax.experimental.pallas import tpu as pltpu
from jax.sharding import PartitionSpec as P

SHORT = 3


def from_behind(x, axis, by):
    peers = lax.axis_size(axis)
    pairs = [(i, i + by) for i in range(peers) if 0 <= i + by < peers]
    return lax.ppermute(x, axis, pairs)


def make_filter(residues, decay_rates, seq_len):
    positions = jnp.arange(seq_len, dtype=jnp.float32) / seq_len
    amplitude = residues * jnp.sqrt(2.0 * decay_rates / seq_len)
    basis = jnp.exp(-decay_rates[:, :, None] * positions[None, None, :])
    return jnp.einsum("cn,cnt->ct", amplitude, basis, precision=lax.Precision.HIGHEST)


def circle(rows_count, cols_count, period):
    left_idx = jnp.arange(rows_count, dtype=jnp.int32)[:, None]
    right_idx = jnp.arange(cols_count, dtype=jnp.int32)[None, :]
    angle = (left_idx * right_idx % period).astype(jnp.float32) * (2.0 * math.pi / period)
    return (jnp.cos(angle), jnp.sin(angle))


def spectral_tables(length):
    factor_a = 1
    while factor_a * factor_a * 4 <= length and length % (factor_a * 2) == 0:
        factor_a = factor_a * 2
    factor_b = length // factor_a
    a_cos, a_sin = circle(factor_a, factor_a, factor_a)
    b_cos, b_sin = circle(factor_b, factor_b, factor_b)
    t_cos, t_sin = circle(factor_a, factor_b, length)
    return (length, factor_a, factor_b, a_cos, a_sin, b_cos, b_sin, t_cos, t_sin)


def forward_dft(signal, tables):
    length, factor_a, factor_b, a_cos, a_sin, b_cos, b_sin, t_cos, t_sin = tables
    highest = lax.Precision.HIGHEST
    channels, seq_len = signal.shape
    grid = jnp.pad(signal, ((0, 0), (0, length - seq_len))).reshape(channels, factor_a, factor_b)
    part_real = jnp.einsum("ka,cab->ckb", a_cos, grid, precision=highest)
    part_imag = -jnp.einsum("ka,cab->ckb", a_sin, grid, precision=highest)
    turn_real = part_real * t_cos + part_imag * t_sin
    turn_imag = part_imag * t_cos - part_real * t_sin
    out_real = jnp.einsum("ckb,bm->ckm", turn_real, b_cos, precision=highest) + jnp.einsum(
        "ckb,bm->ckm", turn_imag, b_sin, precision=highest
    )
    out_imag = jnp.einsum("ckb,bm->ckm", turn_imag, b_cos, precision=highest) - jnp.einsum(
        "ckb,bm->ckm", turn_real, b_sin, precision=highest
    )
    return (out_real, out_imag)


def inverse_dft(spec_real, spec_imag, seq_len, tables):
    length, factor_a, factor_b, a_cos, a_sin, b_cos, b_sin, t_cos, t_sin = tables
    highest = lax.Precision.HIGHEST
    channels = spec_real.shape[0]
    mid_real = jnp.einsum("ckm,mb->ckb", spec_real, b_cos, precision=highest) - jnp.einsum(
        "ckm,mb->ckb", spec_imag, b_sin, precision=highest
    )
    mid_imag = jnp.einsum("ckm,mb->ckb", spec_imag, b_cos, precision=highest) + jnp.einsum(
        "ckm,mb->ckb", spec_real, b_sin, precision=highest
    )
    turn_real = mid_real * t_cos - mid_imag * t_sin
    turn_imag = mid_imag * t_cos + mid_real * t_sin
    values = jnp.einsum("ak,ckb->cab", a_cos, turn_real, precision=highest) - jnp.einsum(
        "ak,ckb->cab", a_sin, turn_imag, precision=highest
    )
    return values.reshape(channels, length)[:, :seq_len] / length


def short_mix(extended, short_taps, tokens):
    running = jnp.zeros((tokens,) + extended.shape[1:], jnp.float32)
    for lag_index in range(SHORT):
        start_row = SHORT - 1 - lag_index
        running = running + short_taps[lag_index] * extended[start_row : start_row + tokens]
    return running


def mix_long(gate_cols, spec_h, gain, seq_len, tables):
    gate_f = gate_cols.astype(jnp.float32)
    u_real, u_imag = forward_dft(gate_f, tables)
    prod_real = spec_h[0] * u_real - spec_h[1] * u_imag
    prod_imag = spec_h[0] * u_imag + spec_h[1] * u_real
    mix_cols = (inverse_dft(prod_real, prod_imag, seq_len, tables) + gain[:, None] * gate_f).astype(
        jnp.bfloat16
    )
    return (mix_cols, (u_real, u_imag))


def grad_long(grad_cols_in, gate_cols, spec_u, spec_h, gain, seq_len, tables):
    grad_f = grad_cols_in.astype(jnp.float32)
    g_real, g_imag = forward_dft(grad_f, tables)
    back_real = spec_h[0] * g_real + spec_h[1] * g_imag
    back_imag = spec_h[0] * g_imag - spec_h[1] * g_real
    grad_cols = (
        inverse_dft(back_real, back_imag, seq_len, tables) + gain[:, None] * grad_f
    ).astype(jnp.bfloat16)
    corr_real = g_real * spec_u[0] + g_imag * spec_u[1]
    corr_imag = g_imag * spec_u[0] - g_real * spec_u[1]
    grad_filter = inverse_dft(corr_real, corr_imag, seq_len, tables)
    skip_sum = jnp.sum(grad_f * gate_cols.astype(jnp.float32), axis=1)
    return (grad_cols, grad_filter, skip_sum)


def body_factored(projections, short_taps, residues, decay_rates, skip_gain, grad_mixed, out_weight):
    tokens = projections.shape[0]
    seq_len = tokens * lax.axis_size("ctx")
    norm_factor = math.sqrt(seq_len)
    tables = spectral_tables(2 * seq_len)
    earlier = from_behind(projections[tokens - SHORT + 1 :], "ctx", 1)
    ext_proj = jnp.concatenate([earlier, projections], axis=0)
    mixed_in = short_mix(ext_proj, short_taps, tokens)
    query_rows = mixed_in[:, 0]
    key_rows = mixed_in[:, 1]
    value_rows = mixed_in[:, 2]
    gated_rows = (key_rows * value_rows).astype(jnp.bfloat16)
    long_filter, filter_vjp = jax.vjp(partial(make_filter, seq_len=seq_len), residues, decay_rates)
    spec_h = forward_dft(long_filter, tables)
    out_rows = lax.all_gather(grad_mixed, "ch", axis=1, tiled=True)
    grad_out = lax.dot_general(
        out_rows,
        lax.all_gather(out_weight, "ctx", axis=1, tiled=True),
        (((1,), (1,)), ((), ())),
        preferred_element_type=jnp.float32,
    )
    grad_y = (grad_out * query_rows).astype(jnp.bfloat16)
    gate_cols, grad_cols_in = (
        lax.all_to_all(gated_rows.T, "ctx", split_axis=0, concat_axis=1, tiled=True),
        lax.all_to_all(grad_y.T, "ctx", split_axis=0, concat_axis=1, tiled=True),
    )
    mix_cols, spec_u = mix_long(gate_cols, spec_h, skip_gain, seq_len, tables)
    grad_cols, grad_filter, skip_sum = grad_long(
        grad_cols_in, gate_cols, spec_u, spec_h, skip_gain, seq_len, tables
    )
    returned = (
        lax.all_to_all(mix_cols, "ctx", split_axis=1, concat_axis=0, tiled=True),
        lax.all_to_all(grad_cols, "ctx", split_axis=1, concat_axis=0, tiled=True),
    )
    mix_rows = returned[0].T
    grad_gated = returned[1].T
    grad_res, grad_rate = filter_vjp(grad_filter)
    grad_residues = grad_res / norm_factor
    grad_log_rates = grad_rate * decay_rates / norm_factor
    grad_skip = skip_sum / norm_factor
    mixed_out = (query_rows * mix_rows).astype(jnp.bfloat16)
    grad_mix = jnp.stack(
        [grad_out * mix_rows, grad_gated * value_rows, grad_gated * key_rows], axis=1
    )
    later = from_behind(grad_mix[: SHORT - 1], "ctx", -1)
    ext_grad = jnp.concatenate([grad_mix, later], axis=0)
    running = jnp.zeros(grad_mix.shape, jnp.float32)
    short_terms = []
    for lag_index in range(SHORT):
        running = running + short_taps[lag_index] * ext_grad[lag_index : lag_index + tokens]
        start_row = SHORT - 1 - lag_index
        short_terms.append(jnp.sum(grad_mix * ext_proj[start_row : start_row + tokens], axis=0))
    grad_projections = running.astype(jnp.bfloat16)
    grad_short = lax.psum(jnp.stack(short_terms, axis=0), "ctx") / norm_factor
    partial_term = lax.dot_general(
        mixed_out, out_rows, (((0,), (0,)), ((), ())), preferred_element_type=jnp.float32
    )
    weight_sum = lax.psum_scatter(partial_term, "ctx", scatter_dimension=1, tiled=True)
    grad_weight = weight_sum / norm_factor
    return (grad_projections, grad_short, grad_skip, grad_residues, grad_log_rates, grad_weight)


def split(x):
    high = x.astype(jnp.bfloat16)
    return high, (x - high.astype(jnp.float32)).astype(jnp.bfloat16)


LANES = 256


def line_tables(tokens):
    steps = np.arange(tokens, dtype=np.int64)[None, :]
    freqs = 2 * np.arange(tokens, dtype=np.int64)[:, None] + 1
    angle = (freqs * steps % (4 * tokens)) * (2.0 * math.pi / (4 * tokens))
    wave = np.concatenate([np.cos(angle), np.sin(angle)], axis=0).astype(np.float32)
    high = wave.astype(jnp.bfloat16)
    low = (wave - high.astype(np.float32)).astype(jnp.bfloat16)
    ahead = np.concatenate([high, low], axis=1)
    back = np.concatenate([high.T, low.T], axis=0)
    return ahead, back


def fused_kernel(
    peers, chans, order,
    proj, taps, rates, amps, gain, gm, weight, ahead, back,
    gproj_out, sh_out, par_out, mo_out, gm_out,
    par, hal_out, hal_in, ext, qkv, gated, drop, states, x_out, x_in, s_in, pq, ab, mix, gm_all, parts, line_in, line_out,
    mo_all, go, gy, gg, gf, g_out, g_in, r_in, mom_out, mom_in, gx, gx_out, gx_in, skip, sh_q, sh_v, shq, shv, gproj,
    local_sem, halo_sem, par_sem, gm1_sem, gm2_sem, x_sem, line_sem, agu_sem, agd_sem, r_sem, mom_sem, gx_sem,
    shq_sem, shv_sem, out_sem,
):
    f32, bf16 = jnp.float32, jnp.bfloat16
    k = lax.axis_index("ctx")
    j = lax.axis_index("ch")
    _, tokens, width = proj.shape
    cols = width // peers
    quarter = tokens // chans
    half = tokens // 2
    seq_len = tokens * peers
    norm = math.sqrt(seq_len)
    last = peers - 1

    def copy(src, dst, send, recv, where):
        return pltpu.make_async_remote_copy(
            src_ref=src,
            dst_ref=dst,
            send_sem=send,
            recv_sem=recv,
            device_id=where,
            device_id_type=pl.DeviceIdType.MESH,
        )

    def tiles(fn, lanes=LANES):
        def step(i, carry):
            fn(pl.ds(pl.multiple_of(i * lanes, lanes), lanes))
            return carry

        lax.fori_loop(0, width // lanes, step, 0)

    def dot(a, b):
        return lax.dot_general(a, b, (((1,), (0,)), ((), ())), preferred_element_type=f32)

    def forward_exact(x):
        return dot(ahead[...], jnp.concatenate([x, x], axis=0))

    def forward(x):
        high, low = split(x)
        return forward_exact(high) + dot(ahead[:, :tokens], low)

    def backward(top, bottom):
        high, low = split(jnp.concatenate([top, bottom], axis=0))
        both = dot(back[...], high)
        return (both[:tokens] + both[tokens:] + dot(back[:tokens], low)) * (1.0 / tokens)

    barrier = pltpu.get_barrier_semaphore()
    for dk in range(peers):
        for dj in range(chans):
            if dk or dj:
                pl.semaphore_signal(
                    barrier,
                    inc=1,
                    device_id={"ctx": lax.rem(k + dk, peers), "ch": lax.rem(j + dj, chans)},
                    device_id_type=pl.DeviceIdType.MESH,
                )

    def widen(at):
        for g in range(3):
            ext[g, 0:8, at] = jnp.zeros((8, at.size), f32)
            ext[g, 8 : 8 + tokens, at] = proj[g, :, at].astype(f32)

    tiles(widen)

    def short_rows(at, count):
        rows = []
        for g in range(3):
            total = taps[0, g : g + 1, at] * ext[g, 8 : 8 + count, at]
            for lag in range(1, SHORT):
                total = total + taps[lag, g : g + 1, at] * ext[g, 8 - lag : 8 - lag + count, at]
            qkv[g, 0:count, at] = total
            rows.append(total)
        gated[0:count, at] = (rows[1] * rows[2]).astype(bf16).astype(f32)

    def short(at):
        short_rows(at, tokens)

    tiles(short, 128)
    mine = pl.ds(pl.multiple_of(k * cols, cols), cols)
    par[0:order, mine] = rates[...]
    par[order : 2 * order, mine] = amps[...]
    edge = [ext[g, 8 + tokens - (SHORT - 1) : 8 + tokens] for g in range(3)]
    edge = jnp.concatenate(edge + [jnp.zeros((2, width), f32)], axis=0)
    hal_out[...] = jnp.concatenate([edge[:, : width // 2], edge[:, width // 2 :]], axis=0).astype(bf16)
    par[2 * order : 2 * order + 8, mine] = jnp.broadcast_to(gain[...], (8, cols))
    pl.semaphore_wait(barrier, peers * chans - 1)

    def gm_first(d):
        q = lax.rem(j + d, chans)
        return copy(
            gm.at[pl.ds(pl.multiple_of(q * quarter, quarter), quarter)],
            gm_all.at[k, q],
            gm1_sem.at[0, d],
            gm1_sem.at[1, k],
            {"ctx": j, "ch": q},
        )

    def gm_own():
        return pltpu.make_async_copy(
            gm.at[pl.ds(pl.multiple_of(j * quarter, quarter), quarter)], gm_all.at[k, j], local_sem
        )

    for d in range(1, chans):
        gm_first(d).start()

    @pl.when(j != k)
    def _():
        gm_first(0).start()

    @pl.when(j == k)
    def _():
        gm_own().start()

    halo_copy = copy(hal_out, hal_in, halo_sem.at[0], halo_sem.at[1], {"ctx": lax.rem(k + 1, peers)})

    @pl.when(k < last)
    def _():
        halo_copy.start()


    def par_copy(d):
        return copy(par.at[:, mine], par.at[:, mine], par_sem.at[0, d], par_sem.at[1, d], {"ctx": lax.rem(k + d, peers)})

    for d in range(1, peers):
        par_copy(d).start()

    @pl.when(k > 0)
    def _():
        halo_copy.wait_recv()
        edge = hal_in[...].astype(f32)
        for g in range(3):
            ext[g, 6:8, : width // 2] = edge[2 * g : 2 * g + 2]
            ext[g, 6:8, width // 2 :] = edge[8 + 2 * g : 10 + 2 * g]

        def short_head(at):
            short_rows(at, 8)

        tiles(short_head)

    def gm_second(b, d):
        return copy(
            gm_all.at[b, j],
            gm_all.at[b, j],
            gm2_sem.at[0, b, d],
            gm2_sem.at[1, b, d],
            {"ch": lax.rem(j + d, chans)},
        )

    def gm_arrived(b):
        copy(gm_all.at[b, j], gm_all.at[b, j], gm1_sem.at[0, 0], gm1_sem.at[1, b], {"ctx": k, "ch": j}).wait_recv()

    for d in range(1, peers):
        par_copy(d).wait_recv()
    rate = par[0:order]
    drop[0] = jnp.exp(rate * (-1.0 / seq_len))
    drop[1] = jnp.exp(rate * (-8.0 / seq_len))
    drop[2] = jnp.exp(rate * (-16.0 / seq_len))
    drop[3] = jnp.exp(rate * (-32.0 / seq_len))
    drop[4] = jnp.exp(rate * (-float(tokens) / seq_len))
    drop[5] = par[order : 2 * order] * jnp.sqrt(2.0 * rate / seq_len)

    def scan_up(source):
        decay = drop[0]

        def step(i, carry):
            s, s1 = carry
            for r in range(8):
                u = s + source[pl.ds(i * 8 + r, 1)]
                s1 = decay * (s1 + u)
                s = decay * u
            return s, s1

        zero = jnp.zeros((order, width), f32)
        return lax.fori_loop(0, tokens // 8, step, (zero, zero))

    def scan_down(source):
        decay = drop[0]

        def step(i, carry):
            s, s1 = carry
            for r in range(8):
                s1 = decay * (s1 + s)
                s = decay * s + source[pl.ds(tokens - 1 - i * 8 - r, 1)]
            return s, s1

        zero = jnp.zeros((order, width), f32)
        return lax.fori_loop(0, tokens // 8, step, (zero, zero))

    def spread(head, at, start, falling):
        lanes = at.size
        iota = lax.broadcasted_iota(jnp.int32, (8, lanes), 0).astype(f32)
        place = (iota if falling else 7.0 - iota) + start
        count = tokens // 8

        def mode(n, acc):
            row = pl.ds(n, 1)
            v = head(row) * jnp.exp(par[row, at] * (place * (-1.0 / seq_len)))
            d8, d16, d32 = drop[1, row, at], drop[2, row, at], drop[3, row, at]
            first = [v, v * d8]
            first = first + [x * d16 for x in first]
            out = []
            for i in range(0, count, 4):
                out += [acc[i + m] + first[m] for m in range(4)]
                first = [x * d32 for x in first]
            return tuple(out)

        zero = jnp.zeros((8, lanes), f32)
        acc = lax.fori_loop(0, order, mode, (zero,) * count)
        return jnp.concatenate(acc if falling else acc[::-1], axis=0)


    s0, s1 = scan_up(gated)
    states[0] = s0
    states[1] = s1
    x_copy = copy(x_out, x_in, x_sem.at[0], x_sem.at[1], {"ctx": lax.rem(k + 1, peers)})

    @pl.when(k == 0)
    def _():
        s_in[...] = jnp.zeros(s_in.shape, f32)
        x_out[...] = states[...].astype(bf16)
        x_copy.start()

    def state_hop(n):
        @pl.when(k == n)
        def _():
            x_copy.wait_recv()
            s_in[...] = x_in[...].astype(f32)
            if n < last:
                x_out[0] = (states[0] + drop[4] * s_in[0]).astype(bf16)
                x_out[1] = (states[1] + drop[4] * (s_in[1] + float(tokens) * s_in[0])).astype(bf16)
                x_copy.start()

    upper = jnp.where(k < peers // 2, 0, 1)
    place = jnp.where(upper == 0, k, last - k)

    def block_of(i, way):
        return jnp.where(way == 0, last - i, i)

    for i in range(peers):
        b = block_of(i, upper)

        @pl.when((j != k) | (k != b))
        def _():
            gm_arrived(b)

        @pl.when((j == k) & (k == b))
        def _():
            gm_own().wait()

        for d in range(1, chans):
            gm_second(b, d).start()

    state_hop(1)

    def conv(at):
        filt = spread(lambda row: drop[5, row, at], at, 0.0, True)
        f = forward(filt)
        x = gated[:, at]
        u = forward_exact(x.astype(bf16))
        pq[:, at] = f
        ab[:, at] = u
        p, q, a, b = f[:tokens], f[tokens:], u[:tokens], u[tokens:]
        mix[:, at] = backward(p * a - q * b, p * b + q * a) + par[2 * order : 2 * order + 1, at] * x

    tiles(conv)
    for n in range(2, last):
        state_hop(n)

    def line_copy(way, i, c):
        b = block_of(i, way)
        rows = pl.ds(c * half, half)
        return copy(
            line_out.at[way, b, rows],
            line_in.at[way, b, rows],
            line_sem.at[0, way, i, c],
            line_sem.at[1, way, i, c],
            {"ctx": lax.rem(k + 1 + way * (peers - 2), peers)},
        )

    for i in range(peers):
        b = block_of(i, upper)
        for d in range(1, chans):
            gm_second(b, d).wait_recv()

        def part(at):
            parts[b, :, at] = lax.dot_general(
                gm_all[b].reshape(tokens, gm_all.shape[-1]),
                weight[at, :],
                (((1,), (1,)), ((), ())),
                preferred_element_type=f32,
            )

        tiles(part)

        if i < last:

            @pl.when(place == 0)
            def _():
                for c in range(2):
                    rows = slice(c * half, (c + 1) * half)
                    line_out[upper, b, rows] = parts[b, rows].astype(bf16)
                    line_copy(upper, i, c).start()

    def gm_store():
        return pltpu.make_async_copy(gm_all, gm_out, out_sem.at[0])

    gm_store().start()

    state_hop(last)

    def finish_mix(at):
        total = mix[:, at] + spread(lambda row: drop[5, row, at] * s_in[0, row, at], at, 0.0, True)
        total = total.astype(bf16).astype(f32)
        mix[:, at] = total
        mo_all[k, at] = (qkv[0, :, at] * total).T.astype(bf16)

    tiles(finish_mix)

    def agu_copy(d):
        s = lax.rem(k + peers - d, peers)
        return copy(
            mo_all.at[s], mo_all.at[s], agu_sem.at[0, d], agu_sem.at[1, d + 1], {"ctx": lax.rem(k + 1, peers)}
        )

    def agu_wait(d):
        s = lax.rem(k + peers - d, peers)
        copy(mo_all.at[s], mo_all.at[s], agu_sem.at[0, d], agu_sem.at[1, d], {"ctx": k}).wait_recv()

    def agd_copy(d):
        s = lax.rem(k + d, peers)
        return copy(
            mo_all.at[s], mo_all.at[s], agd_sem.at[0, d], agd_sem.at[1, d + 1],
            {"ctx": lax.rem(k + peers - 1, peers)},
        )

    def agd_wait(d):
        s = lax.rem(k + d, peers)
        copy(mo_all.at[s], mo_all.at[s], agd_sem.at[0, d], agd_sem.at[1, d], {"ctx": k}).wait_recv()

    @pl.when(k < last)
    def _():
        agu_copy(0).start()

    @pl.when(k > 0)
    def _():
        agd_copy(0).start()

    def relay(d):
        @pl.when((k >= d) & (k < last))
        def _():
            agu_wait(d)
            agu_copy(d).start()

        @pl.when((k + d < peers) & (k > 0))
        def _():
            agd_wait(d)
            agd_copy(d).start()

    def relay_end(d):
        @pl.when((k >= d) & (k == last))
        def _():
            agu_wait(d)

        @pl.when((k + d < peers) & (k == 0))
        def _():
            agd_wait(d)

    def hop(way, spot, i, c):
        @pl.when((spot > 0) & (spot < last - i))
        def _():
            b = block_of(i, way)
            rows = slice(c * half, (c + 1) * half)
            line_copy(way, i, c).wait_recv()
            line_out[way, b, rows] = (parts[b, rows] + line_in[way, b, rows].astype(f32)).astype(bf16)
            line_copy(way, i, c).start()

    steps = [(i, c) for i in range(peers - 1) for c in range(2)]
    for n in range(len(steps) + 2):
        if n < len(steps):
            hop(upper, place, *steps[n])
        if n >= 2:
            hop(1 - upper, last - place, *steps[n - 2])

    relay(1)

    def line_wait(way, spot):
        for i in range(peers - 1):

            @pl.when(spot == last - i)
            def _():
                for c in range(2):
                    line_copy(way, i, c).wait_recv()

        @pl.when(spot == 0)
        def _():
            line_in[way, k] = jnp.zeros((tokens, width), bf16)

    line_wait(1 - upper, last - place)
    line_wait(upper, place)

    def own(at):
        total = parts[k, :, at] + line_in[0, k, :, at].astype(f32) + line_in[1, k, :, at].astype(f32)
        go[:, at] = total
        gy[:, at] = (total * qkv[0, :, at]).astype(bf16).astype(f32)

    tiles(own)

    g0, g1 = scan_down(gy)
    states[0] = g0
    states[1] = g1
    g_out[...] = g0.astype(bf16)

    def r_copy(d):
        return copy(g_out, g_in.at[d], r_sem.at[0, d], r_sem.at[1, d], {"ctx": lax.rem(k + peers - d, peers)})

    for d in range(1, peers):

        @pl.when(k >= d)
        def _():
            r_copy(d).start()

    def conv_back(at):
        x = gy[:, at]
        w = forward_exact(x.astype(bf16))
        f, u = pq[:, at], ab[:, at]
        p, q, a, b = f[:tokens], f[tokens:], u[:tokens], u[tokens:]
        d, e = w[:tokens], w[tokens:]
        gg[:, at] = backward(p * d + q * e, p * e - q * d) + par[2 * order : 2 * order + 1, at] * x
        gf[:, at] = backward(d * a + e * b, e * a - d * b)
        skip[:, at] = jnp.broadcast_to(jnp.sum(x * gated[:, at], axis=0, keepdims=True) / norm, (8, x.shape[1]))
        gx[0, 0:tokens, at] = go[:, at] * mix[:, at]

    for d in range(2, peers):
        relay(d)
    tiles(conv_back)

    def sums(at, groups):
        rows = []
        for lag in range(SHORT):
            for g in groups:
                rows.append(
                    jnp.sum(gx[g, 0:tokens, at] * ext[g, 8 - lag : 8 - lag + tokens, at], axis=0, keepdims=True)
                )
        return [row * (1.0 / norm) for row in rows]

    quad = width // 4

    def shorts_q(at):
        sh_q[0:3, at] = jnp.concatenate(sums(at, (0,)), axis=0)

    tiles(shorts_q, 128)
    sh_q[3:4] = skip[0:1]
    few = sh_q[0:4]
    shq[k] = jnp.concatenate([few[:, q * quad : (q + 1) * quad] for q in range(4)], axis=0).astype(bf16)

    def shq_copy(d):
        return copy(shq.at[k], shq.at[k], shq_sem.at[0, d], shq_sem.at[1, d], {"ctx": lax.rem(k + d, peers)})

    for d in range(1, peers):
        shq_copy(d).start()

    m0, m1 = scan_down(gf)
    m0 = m0 + states[0] * s_in[0]
    m1 = m1 + states[1] * s_in[0] + states[0] * s_in[1]
    mom_out[0:order] = (jnp.sqrt(2.0 * par[0:order] / seq_len) * m0 * (1.0 / norm)).astype(bf16)
    grad_log = drop[5] * (0.5 * m0 - par[0:order] * m1 * (1.0 / seq_len)) * (1.0 / norm)
    mom_out[order : 2 * order] = grad_log.astype(bf16)

    def mom_copy(d):
        to = lax.rem(k + d, peers)
        return copy(
            mom_out.at[:, pl.ds(pl.multiple_of(to * cols, cols), cols)],
            mom_in.at[d],
            mom_sem.at[0, d],
            mom_sem.at[1, d],
            {"ctx": to},
        )

    for d in range(1, peers):
        mom_copy(d).start()

    r_in[...] = jnp.zeros(r_in.shape, f32)
    for d in range(1, peers):

        @pl.when(k + d < peers)
        def _():
            r_copy(d).wait_recv()
            r_in[...] = r_in[...] + drop[4] ** (d - 1) * g_in[d].astype(f32)

    def grads(at):
        total = gg[:, at] + spread(lambda row: drop[5, row, at] * r_in[row, at], at, 1.0, False)
        total = total.astype(bf16).astype(f32)
        gx[1, 0:tokens, at] = total * qkv[2, :, at]
        gx[2, 0:tokens, at] = total * qkv[1, :, at]

    tiles(grads)

    edge = [gx[g, 0 : SHORT - 1] for g in range(3)] + [jnp.zeros((2, width), f32)]
    gx_out[...] = jnp.concatenate(edge, axis=0)
    gx_copy = copy(gx_out, gx_in, gx_sem.at[0], gx_sem.at[1], {"ctx": lax.rem(k + peers - 1, peers)})

    @pl.when(k > 0)
    def _():
        gx_copy.start()

    def shorts_v(at):
        rows = sums(at, (1, 2))
        sh_v[:, at] = jnp.concatenate(rows + [jnp.zeros((2, at.size), f32)], axis=0)

    tiles(shorts_v, 128)
    shv[k] = jnp.concatenate([sh_v[:, : width // 2], sh_v[:, width // 2 :]], axis=0).astype(bf16)

    def shv_copy(d):
        return copy(shv.at[k], shv.at[k], shv_sem.at[0, d], shv_sem.at[1, d], {"ctx": lax.rem(k + d, peers)})

    for d in range(1, peers):
        shv_copy(d).start()

    def out_rows(at, start, count):
        for g in range(3):
            total = taps[0, g : g + 1, at] * gx[g, start : start + count, at]
            for lag in range(1, SHORT):
                total = total + taps[lag, g : g + 1, at] * gx[g, start + lag : start + lag + count, at]
            gproj[g, start : start + count, at] = total.astype(bf16)

    def out_most(at):
        out_rows(at, 0, tokens - 16)

    tiles(out_most, 128)

    @pl.when(k < last)
    def _():
        gx_copy.wait_recv()
        for g in range(3):
            gx[g, tokens : tokens + 2] = gx_in[2 * g : 2 * g + 2]

    @pl.when(k == last)
    def _():
        gx[:, tokens : tokens + 8] = jnp.zeros((3, 8, width), f32)

    def out_end(at):
        out_rows(at, tokens - 16, 16)

    tiles(out_end)
    gproj_store = pltpu.make_async_copy(gproj, gproj_out, out_sem.at[1])
    gproj_store.start()
    for d in range(1, peers):
        relay_end(d)
    mo_store = pltpu.make_async_copy(mo_all, mo_out, out_sem.at[2])
    mo_store.start()

    for d in range(1, peers):
        mom_copy(d).wait_recv()
    par_out[0 : 2 * order] = sum((mom_in[d].astype(f32) for d in range(1, peers)), mom_out[:, mine].astype(f32))
    for d in range(1, peers):
        shq_copy(d).wait_recv()
        shv_copy(d).wait_recv()
    few = sum((shq[d].astype(f32) for d in range(1, peers)), shq[0].astype(f32))
    for q in range(4):
        sh_out[0:4, q * quad : (q + 1) * quad] = few[4 * q : 4 * q + 4]
    many = sum((shv[d].astype(f32) for d in range(1, peers)), shv[0].astype(f32))
    sh_out[8:16, : width // 2] = many[0:8]
    sh_out[8:16, width // 2 :] = many[8:16]
    par_out[2 * order : 2 * order + 8] = jnp.broadcast_to(sh_out[3:4, mine], (8, cols))

    for d in range(1, chans):
        gm_first(d).wait_send()

    @pl.when(j != k)
    def _():
        gm_first(0).wait_send()

    for b in range(peers):
        for d in range(1, chans):
            gm_second(b, d).wait_send()
    for d in range(1, peers):
        par_copy(d).wait_send()
        mom_copy(d).wait_send()
        shq_copy(d).wait_send()
        shv_copy(d).wait_send()

        @pl.when(k >= d)
        def _():
            r_copy(d).wait_send()

    @pl.when(k < last)
    def _():
        halo_copy.wait_send()
        x_copy.wait_send()

    @pl.when(k > 0)
    def _():
        gx_copy.wait_send()

    for i in range(peers - 1):
        for c in range(2):

            @pl.when(k < last - i)
            def _():
                line_copy(0, i, c).wait_send()

            @pl.when(k > i)
            def _():
                line_copy(1, i, c).wait_send()

    for d in range(peers - 1):

        @pl.when((k >= d) & (k < last))
        def _():
            agu_copy(d).wait_send()

        @pl.when((k + d < peers) & (k > 0))
        def _():
            agd_copy(d).wait_send()

    gm_store().wait()
    gproj_store.wait()
    mo_store.wait()


def finish_kernel(peers, order, norm, mo, gm, rows, sums, params, gproj, gshort, gskip, gres, glog, gweight):
    gproj[...] = rows[...]
    left = jnp.concatenate([mo[b] for b in range(peers)], axis=1)
    gweight[...] = lax.dot_general(
        left, gm[...], (((1,), (0,)), ((), ())), preferred_element_type=jnp.float32
    ) * (1.0 / norm)
    for lag in range(SHORT):
        gshort[lag, 0:1] = sums[lag : lag + 1]
        gshort[lag, 1:3] = sums[8 + 2 * lag : 10 + 2 * lag]
    gres[...] = params[0:order]
    glog[...] = params[order : 2 * order]
    gskip[...] = params[2 * order : 2 * order + 1]


def body_fused(projections, short_taps, residues, decay_rates, skip_gain, grad_mixed, out_weight):
    tokens, _, width = projections.shape
    peers, chans = lax.axis_size("ctx"), lax.axis_size("ch")
    order = residues.shape[1]
    cols = width // peers
    wide = out_weight.shape[1]
    seq_len = tokens * peers
    f32, bf16 = jnp.float32, jnp.bfloat16
    ahead, back = line_tables(tokens)
    rows = 2 * order + 8
    vmem = pl.BlockSpec(memory_space=pltpu.VMEM)
    far = pl.BlockSpec(memory_space=pl.ANY)
    dma = pltpu.SemaphoreType.DMA
    shape = jax.ShapeDtypeStruct
    gproj, sums, params, mo, gm = pl.pallas_call(
        partial(fused_kernel, peers, chans, order),
        out_shape=(
            shape((3, tokens, width), bf16),
            shape((16, width), f32),
            shape((rows, cols), f32),
            shape((peers, width, tokens), bf16),
            shape((peers, chans, tokens // chans, wide), bf16),
        ),
        in_specs=[vmem] * 9,
        out_specs=(far, vmem, vmem, far, far),
        scratch_shapes=[
            pltpu.VMEM((rows, width), f32),
            pltpu.VMEM((16, width // 2), bf16),
            pltpu.VMEM((16, width // 2), bf16),
            pltpu.VMEM((3, tokens + 8, width), f32),
            pltpu.VMEM((3, tokens, width), f32),
            pltpu.VMEM((tokens, width), f32),
            pltpu.VMEM((6, order, width), f32),
            pltpu.VMEM((2, order, width), f32),
            pltpu.VMEM((2, order, width), bf16),
            pltpu.VMEM((2, order, width), bf16),
            pltpu.VMEM((2, order, width), f32),
            pltpu.VMEM((2 * tokens, width), f32),
            pltpu.VMEM((2 * tokens, width), f32),
            pltpu.VMEM((tokens, width), f32),
            pltpu.VMEM((peers, chans, tokens // chans, wide), bf16),
            pltpu.VMEM((peers, tokens, width), f32),
            pltpu.VMEM((2, peers, tokens, width), bf16),
            pltpu.VMEM((2, peers, tokens, width), bf16),
            pltpu.VMEM((peers, width, tokens), bf16),
            pltpu.VMEM((tokens, width), f32),
            pltpu.VMEM((tokens, width), f32),
            pltpu.VMEM((tokens, width), f32),
            pltpu.VMEM((tokens, width), f32),
            pltpu.VMEM((order, width), bf16),
            pltpu.VMEM((peers, order, width), bf16),
            pltpu.VMEM((order, width), f32),
            pltpu.VMEM((2 * order, width), bf16),
            pltpu.VMEM((peers, 2 * order, cols), bf16),
            pltpu.VMEM((3, tokens + 8, width), f32),
            pltpu.VMEM((8, width), f32),
            pltpu.VMEM((8, width), f32),
            pltpu.VMEM((8, width), f32),
            pltpu.VMEM((8, width), f32),
            pltpu.VMEM((8, width), f32),
            pltpu.VMEM((peers, 16, width // 4), bf16),
            pltpu.VMEM((peers, 16, width // 2), bf16),
            pltpu.VMEM((3, tokens, width), bf16),
            dma,
            dma((2,)),
            dma((2, peers)),
            dma((2, max(peers, chans))),
            dma((2, peers, chans)),
            dma((2,)),
            dma((2, 2, peers, 2)),
            dma((2, peers)),
            dma((2, peers)),
            dma((2, peers)),
            dma((2, peers)),
            dma((2,)),
            dma((2, peers)),
            dma((2, peers)),
            dma((3,)),
        ],
        compiler_params=pltpu.CompilerParams(
            collective_id=0, has_side_effects=True, vmem_limit_bytes=56 * 1024 * 1024
        ),
    )(
        projections.transpose(1, 0, 2),
        short_taps,
        decay_rates.T,
        residues.T,
        skip_gain[None],
        grad_mixed,
        out_weight,
        jnp.asarray(ahead),
        jnp.asarray(back),
    )
    lanes = LANES
    whole = lambda *dims: pl.BlockSpec(dims, lambda i: (0,) * len(dims))
    gproj, gshort, gskip, gres, glog, gweight = pl.pallas_call(
        partial(finish_kernel, peers, order, math.sqrt(seq_len)),
        grid=(width // lanes,),
        out_shape=(
            shape((3, tokens, width), bf16),
            shape((SHORT, 3, width), f32),
            shape((1, cols), f32),
            shape((order, cols), f32),
            shape((order, cols), f32),
            shape((width, wide), f32),
        ),
        in_specs=[
            pl.BlockSpec((peers, lanes, tokens), lambda i: (0, i, 0)),
            whole(seq_len, wide),
            pl.BlockSpec((3, tokens, lanes), lambda i: (0, 0, i)),
            pl.BlockSpec((16, lanes), lambda i: (0, i)),
            whole(rows, cols),
        ],
        out_specs=(
            pl.BlockSpec((3, tokens, lanes), lambda i: (0, 0, i)),
            pl.BlockSpec((SHORT, 3, lanes), lambda i: (0, 0, i)),
            whole(1, cols),
            whole(order, cols),
            whole(order, cols),
            pl.BlockSpec((lanes, wide), lambda i: (i, 0)),
        ),
    )(mo, gm.reshape(seq_len, wide), gproj, sums, params)
    return (gproj.transpose(1, 0, 2), gshort, gskip[0], gres.T, glog.T, gweight)


def body(*args):
    peers, chans = lax.axis_size("ctx"), lax.axis_size("ch")
    if peers * args[0].shape[0] > 1024 or peers != chans:
        return body_factored(*args)
    return body_fused(*args)


def solution(mesh):
    return jax.shard_map(
        body,
        mesh=mesh,
        in_specs=(
            P(("groups", "ctx"), None, "ch"),
            P(None, None, "ch"),
            P(("ch", "ctx"), None),
            P(("ch", "ctx"), None),
            P(("ch", "ctx")),
            P(("groups", "ctx"), "ch"),
            P("ch", "ctx"),
        ),
        out_specs=(
            P(("groups", "ctx"), None, "ch"),
            P("groups", None, "ch"),
            P(("groups", "ch", "ctx")),
            P(("groups", "ch", "ctx"), None),
            P(("groups", "ch", "ctx"), None),
            P(("groups", "ch"), "ctx"),
        ),
        check_vma=False,
    )
```

```python
from functools import partial
import math

import jax
import jax.numpy as jnp
import numpy as np
from jax import lax
from jax.experimental import pallas as pl
from jax.experimental.pallas import tpu as pltpu
from jax.sharding import PartitionSpec as P

SHORT = 3


def from_behind(x, axis, by):
    peers = lax.axis_size(axis)
    pairs = [(i, i + by) for i in range(peers) if 0 <= i + by < peers]
    return lax.ppermute(x, axis, pairs)


def make_filter(residues, decay_rates, seq_len):
    positions = jnp.arange(seq_len, dtype=jnp.float32) / seq_len
    amplitude = residues * jnp.sqrt(2.0 * decay_rates / seq_len)
    basis = jnp.exp(-decay_rates[:, :, None] * positions[None, None, :])
    return jnp.einsum("cn,cnt->ct", amplitude, basis, precision=lax.Precision.HIGHEST)


def circle(rows_count, cols_count, period):
    left_idx = jnp.arange(rows_count, dtype=jnp.int32)[:, None]
    right_idx = jnp.arange(cols_count, dtype=jnp.int32)[None, :]
    angle = (left_idx * right_idx % period).astype(jnp.float32) * (2.0 * math.pi / period)
    return (jnp.cos(angle), jnp.sin(angle))


def spectral_tables(length):
    factor_a = 1
    while factor_a * factor_a * 4 <= length and length % (factor_a * 2) == 0:
        factor_a = factor_a * 2
    factor_b = length // factor_a
    a_cos, a_sin = circle(factor_a, factor_a, factor_a)
    b_cos, b_sin = circle(factor_b, factor_b, factor_b)
    t_cos, t_sin = circle(factor_a, factor_b, length)
    return (length, factor_a, factor_b, a_cos, a_sin, b_cos, b_sin, t_cos, t_sin)


def forward_dft(signal, tables):
    length, factor_a, factor_b, a_cos, a_sin, b_cos, b_sin, t_cos, t_sin = tables
    highest = lax.Precision.HIGHEST
    channels, seq_len = signal.shape
    grid = jnp.pad(signal, ((0, 0), (0, length - seq_len))).reshape(channels, factor_a, factor_b)
    part_real = jnp.einsum("ka,cab->ckb", a_cos, grid, precision=highest)
    part_imag = -jnp.einsum("ka,cab->ckb", a_sin, grid, precision=highest)
    turn_real = part_real * t_cos + part_imag * t_sin
    turn_imag = part_imag * t_cos - part_real * t_sin
    out_real = jnp.einsum("ckb,bm->ckm", turn_real, b_cos, precision=highest) + jnp.einsum(
        "ckb,bm->ckm", turn_imag, b_sin, precision=highest
    )
    out_imag = jnp.einsum("ckb,bm->ckm", turn_imag, b_cos, precision=highest) - jnp.einsum(
        "ckb,bm->ckm", turn_real, b_sin, precision=highest
    )
    return (out_real, out_imag)


def inverse_dft(spec_real, spec_imag, seq_len, tables):
    length, factor_a, factor_b, a_cos, a_sin, b_cos, b_sin, t_cos, t_sin = tables
    highest = lax.Precision.HIGHEST
    channels = spec_real.shape[0]
    mid_real = jnp.einsum("ckm,mb->ckb", spec_real, b_cos, precision=highest) - jnp.einsum(
        "ckm,mb->ckb", spec_imag, b_sin, precision=highest
    )
    mid_imag = jnp.einsum("ckm,mb->ckb", spec_imag, b_cos, precision=highest) + jnp.einsum(
        "ckm,mb->ckb", spec_real, b_sin, precision=highest
    )
    turn_real = mid_real * t_cos - mid_imag * t_sin
    turn_imag = mid_imag * t_cos + mid_real * t_sin
    values = jnp.einsum("ak,ckb->cab", a_cos, turn_real, precision=highest) - jnp.einsum(
        "ak,ckb->cab", a_sin, turn_imag, precision=highest
    )
    return values.reshape(channels, length)[:, :seq_len] / length


def short_mix(extended, short_taps, tokens):
    running = jnp.zeros((tokens,) + extended.shape[1:], jnp.float32)
    for lag_index in range(SHORT):
        start_row = SHORT - 1 - lag_index
        running = running + short_taps[lag_index] * extended[start_row : start_row + tokens]
    return running


def mix_long(gate_cols, spec_h, gain, seq_len, tables):
    gate_f = gate_cols.astype(jnp.float32)
    u_real, u_imag = forward_dft(gate_f, tables)
    prod_real = spec_h[0] * u_real - spec_h[1] * u_imag
    prod_imag = spec_h[0] * u_imag + spec_h[1] * u_real
    mix_cols = (inverse_dft(prod_real, prod_imag, seq_len, tables) + gain[:, None] * gate_f).astype(
        jnp.bfloat16
    )
    return (mix_cols, (u_real, u_imag))


def grad_long(grad_cols_in, gate_cols, spec_u, spec_h, gain, seq_len, tables):
    grad_f = grad_cols_in.astype(jnp.float32)
    g_real, g_imag = forward_dft(grad_f, tables)
    back_real = spec_h[0] * g_real + spec_h[1] * g_imag
    back_imag = spec_h[0] * g_imag - spec_h[1] * g_real
    grad_cols = (
        inverse_dft(back_real, back_imag, seq_len, tables) + gain[:, None] * grad_f
    ).astype(jnp.bfloat16)
    corr_real = g_real * spec_u[0] + g_imag * spec_u[1]
    corr_imag = g_imag * spec_u[0] - g_real * spec_u[1]
    grad_filter = inverse_dft(corr_real, corr_imag, seq_len, tables)
    skip_sum = jnp.sum(grad_f * gate_cols.astype(jnp.float32), axis=1)
    return (grad_cols, grad_filter, skip_sum)


def body_factored(projections, short_taps, residues, decay_rates, skip_gain, grad_mixed, out_weight):
    tokens = projections.shape[0]
    seq_len = tokens * lax.axis_size("ctx")
    norm_factor = math.sqrt(seq_len)
    tables = spectral_tables(2 * seq_len)
    earlier = from_behind(projections[tokens - SHORT + 1 :], "ctx", 1)
    ext_proj = jnp.concatenate([earlier, projections], axis=0)
    mixed_in = short_mix(ext_proj, short_taps, tokens)
    query_rows = mixed_in[:, 0]
    key_rows = mixed_in[:, 1]
    value_rows = mixed_in[:, 2]
    gated_rows = (key_rows * value_rows).astype(jnp.bfloat16)
    long_filter, filter_vjp = jax.vjp(partial(make_filter, seq_len=seq_len), residues, decay_rates)
    spec_h = forward_dft(long_filter, tables)
    out_rows = lax.all_gather(grad_mixed, "ch", axis=1, tiled=True)
    grad_out = lax.dot_general(
        out_rows,
        lax.all_gather(out_weight, "ctx", axis=1, tiled=True),
        (((1,), (1,)), ((), ())),
        preferred_element_type=jnp.float32,
    )
    grad_y = (grad_out * query_rows).astype(jnp.bfloat16)
    gate_cols, grad_cols_in = (
        lax.all_to_all(gated_rows.T, "ctx", split_axis=0, concat_axis=1, tiled=True),
        lax.all_to_all(grad_y.T, "ctx", split_axis=0, concat_axis=1, tiled=True),
    )
    mix_cols, spec_u = mix_long(gate_cols, spec_h, skip_gain, seq_len, tables)
    grad_cols, grad_filter, skip_sum = grad_long(
        grad_cols_in, gate_cols, spec_u, spec_h, skip_gain, seq_len, tables
    )
    returned = (
        lax.all_to_all(mix_cols, "ctx", split_axis=1, concat_axis=0, tiled=True),
        lax.all_to_all(grad_cols, "ctx", split_axis=1, concat_axis=0, tiled=True),
    )
    mix_rows = returned[0].T
    grad_gated = returned[1].T
    grad_res, grad_rate = filter_vjp(grad_filter)
    grad_residues = grad_res / norm_factor
    grad_log_rates = grad_rate * decay_rates / norm_factor
    grad_skip = skip_sum / norm_factor
    mixed_out = (query_rows * mix_rows).astype(jnp.bfloat16)
    grad_mix = jnp.stack(
        [grad_out * mix_rows, grad_gated * value_rows, grad_gated * key_rows], axis=1
    )
    later = from_behind(grad_mix[: SHORT - 1], "ctx", -1)
    ext_grad = jnp.concatenate([grad_mix, later], axis=0)
    running = jnp.zeros(grad_mix.shape, jnp.float32)
    short_terms = []
    for lag_index in range(SHORT):
        running = running + short_taps[lag_index] * ext_grad[lag_index : lag_index + tokens]
        start_row = SHORT - 1 - lag_index
        short_terms.append(jnp.sum(grad_mix * ext_proj[start_row : start_row + tokens], axis=0))
    grad_projections = running.astype(jnp.bfloat16)
    grad_short = lax.psum(jnp.stack(short_terms, axis=0), "ctx") / norm_factor
    partial_term = lax.dot_general(
        mixed_out, out_rows, (((0,), (0,)), ((), ())), preferred_element_type=jnp.float32
    )
    weight_sum = lax.psum_scatter(partial_term, "ctx", scatter_dimension=1, tiled=True)
    grad_weight = weight_sum / norm_factor
    return (grad_projections, grad_short, grad_skip, grad_residues, grad_log_rates, grad_weight)


def split(x):
    high = x.astype(jnp.bfloat16)
    return high, (x - high.astype(jnp.float32)).astype(jnp.bfloat16)


LANES = 256
WIDE = 512


def line_tables(tokens):
    steps = np.arange(tokens, dtype=np.int64)[None, :]
    freqs = 2 * np.arange(tokens, dtype=np.int64)[:, None] + 1
    angle = (freqs * steps % (4 * tokens)) * (2.0 * math.pi / (4 * tokens))
    wave = np.concatenate([np.cos(angle), np.sin(angle)], axis=0).astype(np.float32)
    high = wave.astype(jnp.bfloat16)
    low = (wave - high.astype(np.float32)).astype(jnp.bfloat16)
    ahead = np.concatenate([high, low], axis=1)
    back = np.concatenate([high.T, low.T], axis=0)
    return ahead, back


def fused_kernel(
    peers, chans, order,
    proj_far, taps, rates, amps, gain, gm, weight_far, ahead_far, back_far,
    gproj_out, sh_out, par_out, mo_out, gm_out,
    proj, weight, ahead, back, par, hal_out, hal_in, ext, qkv, gated, drop, states, x_out, x_in, s_in, pq, ab, mix, gm_all, parts, line_in, line_out,
    mo_all, go, gy, gg, gf, g_out, g_in, r_in, mom_out, mom_in, gx, gx_out, gx_in, skip, sh_q, sh_v, shq, shv, gproj,
    load_sem, local_sem, halo_sem, par_sem, gm1_sem, gm2_sem, x_sem, line_sem, ag_sem, r_sem, mom_sem, gx_sem,
    shq_sem, shv_sem, out_sem,
):
    f32, bf16 = jnp.float32, jnp.bfloat16
    k = lax.axis_index("ctx")
    j = lax.axis_index("ch")
    loads = [
        pltpu.make_async_copy(far, near, load_sem.at[n])
        for n, (far, near) in enumerate(
            ((proj_far, proj), (weight_far, weight), (ahead_far, ahead), (back_far, back))
        )
    ]
    for load in loads:
        load.start()
    _, tokens, width = proj.shape
    cols = width // peers
    quarter = tokens // chans
    half = tokens // 2
    seq_len = tokens * peers
    norm = math.sqrt(seq_len)
    last = peers - 1

    def copy(src, dst, send, recv, where):
        return pltpu.make_async_remote_copy(
            src_ref=src,
            dst_ref=dst,
            send_sem=send,
            recv_sem=recv,
            device_id=where,
            device_id_type=pl.DeviceIdType.MESH,
        )

    def tiles(fn, lanes=LANES, start=0, stop=width):
        def step(i, carry):
            fn(pl.ds(pl.multiple_of(i * lanes, lanes), lanes))
            return carry

        lax.fori_loop(start // lanes, stop // lanes, step, 0)

    def dot(a, b):
        return lax.dot_general(a, b, (((1,), (0,)), ((), ())), preferred_element_type=f32)

    def forward_exact(x):
        return dot(ahead[...], jnp.concatenate([x, x], axis=0))

    def forward(x):
        high, low = split(x)
        return forward_exact(high) + dot(ahead[:, :tokens], low)

    def backward(top, bottom):
        high, low = split(jnp.concatenate([top, bottom], axis=0))
        both = dot(back[...], high)
        return (both[:tokens] + both[tokens:] + dot(back[:tokens], low)) * (1.0 / tokens)

    barrier = pltpu.get_barrier_semaphore()
    for dk in range(peers):
        for dj in range(chans):
            if dk or dj:
                pl.semaphore_signal(
                    barrier,
                    inc=1,
                    device_id={"ctx": lax.rem(k + dk, peers), "ch": lax.rem(j + dj, chans)},
                    device_id_type=pl.DeviceIdType.MESH,
                )

    loads[0].wait()

    def widen(at):
        for g in range(3):
            ext[g, 0:8, at] = jnp.zeros((8, at.size), f32)
            ext[g, 8 : 8 + tokens, at] = proj[g, :, at].astype(f32)

    tiles(widen)

    def short_rows(at, count):
        rows = []
        for g in range(3):
            total = taps[0, g : g + 1, at] * ext[g, 8 : 8 + count, at]
            for lag in range(1, SHORT):
                total = total + taps[lag, g : g + 1, at] * ext[g, 8 - lag : 8 - lag + count, at]
            qkv[g, 0:count, at] = total
            rows.append(total)
        gated[0:count, at] = (rows[1] * rows[2]).astype(bf16).astype(f32)

    def short(at):
        short_rows(at, tokens)

    tiles(short, 128)
    mine = pl.ds(pl.multiple_of(k * cols, cols), cols)
    par[0:order, mine] = rates[...]
    par[order : 2 * order, mine] = amps[...]
    edge = [ext[g, 8 + tokens - (SHORT - 1) : 8 + tokens] for g in range(3)]
    edge = jnp.concatenate(edge + [jnp.zeros((2, width), f32)], axis=0)
    hal_out[...] = jnp.concatenate([edge[:, : width // 2], edge[:, width // 2 :]], axis=0).astype(bf16)
    par[2 * order : 2 * order + 8, mine] = jnp.broadcast_to(gain[...], (8, cols))
    pl.semaphore_wait(barrier, peers * chans - 1)

    def gm_first(d):
        q = lax.rem(j + d, chans)
        return copy(
            gm.at[pl.ds(pl.multiple_of(q * quarter, quarter), quarter)],
            gm_all.at[k, q],
            gm1_sem.at[0, d],
            gm1_sem.at[1, k],
            {"ctx": j, "ch": q},
        )

    def gm_own():
        return pltpu.make_async_copy(
            gm.at[pl.ds(pl.multiple_of(j * quarter, quarter), quarter)], gm_all.at[k, j], local_sem
        )

    halo_copy = copy(hal_out, hal_in, halo_sem.at[0], halo_sem.at[1], {"ctx": lax.rem(k + 1, peers)})

    @pl.when(k < last)
    def _():
        halo_copy.start()


    def par_copy(d):
        return copy(par.at[:, mine], par.at[:, mine], par_sem.at[0, d], par_sem.at[1, d], {"ctx": lax.rem(k + d, peers)})

    for d in range(1, peers):
        par_copy(d).start()

    for d in range(1, chans):
        gm_first(d).start()

    @pl.when(j != k)
    def _():
        gm_first(0).start()

    @pl.when(j == k)
    def _():
        gm_own().start()

    @pl.when(k > 0)
    def _():
        halo_copy.wait_recv()
        edge = hal_in[...].astype(f32)
        for g in range(3):
            ext[g, 6:8, : width // 2] = edge[2 * g : 2 * g + 2]
            ext[g, 6:8, width // 2 :] = edge[8 + 2 * g : 10 + 2 * g]

        def short_head(at):
            short_rows(at, 8)

        tiles(short_head)

    mate = j + 1 - 2 * lax.rem(j, 2)

    def gm_mate(b):
        return copy(gm_all.at[b, j], gm_all.at[b, j], gm2_sem.at[0, b, 0], gm2_sem.at[1, b, 0], {"ch": mate})

    def gm_chip(b, o):
        return copy(
            gm_all.at[b, j],
            gm_all.at[b, j],
            gm2_sem.at[0, b, o],
            gm2_sem.at[1, b, o],
            {"ch": lax.rem(j + o, chans)},
        )

    def gm_pass(b, o):
        f = lax.rem(j + chans - o, chans)
        return copy(
            gm_all.at[b, f], gm_all.at[b, f], gm2_sem.at[0, b, o + 1], gm2_sem.at[1, b, o + 1], {"ch": mate}
        )

    def gm_arrived(b):
        copy(gm_all.at[b, j], gm_all.at[b, j], gm1_sem.at[0, 0], gm1_sem.at[1, b], {"ctx": k, "ch": j}).wait_recv()

    for load in loads[1:]:
        load.wait()
    for d in range(1, peers):
        par_copy(d).wait_recv()
    rate = par[0:order]
    drop[0] = jnp.exp(rate * (-1.0 / seq_len))
    drop[1] = jnp.exp(rate * (-8.0 / seq_len))
    drop[2] = jnp.exp(rate * (-16.0 / seq_len))
    drop[3] = jnp.exp(rate * (-32.0 / seq_len))
    drop[4] = jnp.exp(rate * (-float(tokens) / seq_len))
    drop[5] = par[order : 2 * order] * jnp.sqrt(2.0 * rate / seq_len)

    def scan_up(source):
        decay = drop[0]

        def step(i, carry):
            s, s1 = carry
            for r in range(8):
                u = s + source[pl.ds(i * 8 + r, 1)]
                s1 = decay * (s1 + u)
                s = decay * u
            return s, s1

        zero = jnp.zeros((order, width), f32)
        return lax.fori_loop(0, tokens // 8, step, (zero, zero))

    def scan_down(source):
        decay = drop[0]

        def step(i, carry):
            s, s1 = carry
            for r in range(8):
                s1 = decay * (s1 + s)
                s = decay * s + source[pl.ds(tokens - 1 - i * 8 - r, 1)]
            return s, s1

        zero = jnp.zeros((order, width), f32)
        return lax.fori_loop(0, tokens // 8, step, (zero, zero))

    def scan_one(source):
        decay = drop[0]

        def step(i, s):
            for r in range(8):
                s = decay * (s + source[pl.ds(i * 8 + r, 1)])
            return s

        return lax.fori_loop(0, tokens // 8, step, jnp.zeros((order, width), f32))

    def spread(head, at, start, falling):
        lanes = at.size
        iota = lax.broadcasted_iota(jnp.int32, (8, lanes), 0).astype(f32)
        place = (iota if falling else 7.0 - iota) + start
        count = tokens // 8

        def mode(n, acc):
            row = pl.ds(n, 1)
            v = head(row) * jnp.exp(par[row, at] * (place * (-1.0 / seq_len)))
            d8, d16, d32 = drop[1, row, at], drop[2, row, at], drop[3, row, at]
            first = [v, v * d8]
            first = first + [x * d16 for x in first]
            out = []
            for i in range(0, count, 4):
                out += [acc[i + m] + first[m] for m in range(4)]
                first = [x * d32 for x in first]
            return tuple(out)

        zero = jnp.zeros((8, lanes), f32)
        acc = lax.fori_loop(0, order, mode, (zero,) * count, unroll=order)
        return jnp.concatenate(acc if falling else acc[::-1], axis=0)


    def x_copy(i, d):
        return copy(x_out.at[i], x_in.at[i, d], x_sem.at[0, i, d], x_sem.at[1, i, d], {"ctx": lax.rem(k + d, peers)})

    def x_send(i, state):
        x_out[i] = state.astype(bf16)
        for d in range(1, peers):

            @pl.when(k + d < peers)
            def _():
                x_copy(i, d).start()

    x_send(0, scan_one(gated))

    def filters(at):
        gf[:, at] = spread(lambda row: drop[5, row, at], at, 0.0, True)

    def conv(at):
        f = forward(gf[:, at])
        x = gated[:, at]
        u = forward_exact(x.astype(bf16))
        pq[:, at] = f
        ab[:, at] = u
        p, q, a, b = f[:tokens], f[tokens:], u[:tokens], u[tokens:]
        mix[:, at] = backward(p * a - q * b, p * b + q * a) + par[2 * order : 2 * order + 1, at] * x

    upper = jnp.where(k < peers // 2, 0, 1)
    place = jnp.where(upper == 0, k, last - k)

    def block_of(i, way):
        return jnp.where(way == 0, last - i, i)

    tiles(filters)
    tiles(conv, WIDE, 0, width // 2)
    for i in range(peers):
        b = block_of(i, upper)

        @pl.when((j != k) | (k != b))
        def _():
            gm_arrived(b)

        @pl.when((j == k) & (k == b))
        def _():
            gm_own().wait()

        for o in range(2, chans, 2):
            gm_chip(b, o).start()
        gm_mate(b).start()

    tiles(conv, WIDE, width // 2, width)

    s_in[...] = jnp.zeros(s_in.shape, f32)
    for d in range(1, peers):

        @pl.when(k >= d)
        def _():
            x_copy(0, d).wait_recv()
            s_in[0] = s_in[0] + drop[4] ** (d - 1) * x_in[0, d].astype(f32)

    def finish_mix(at):
        total = mix[:, at] + spread(lambda row: drop[5, row, at] * s_in[0, row, at], at, 0.0, True)
        total = total.astype(bf16).astype(f32)
        mix[:, at] = total
        mo_all[k, at] = (qkv[0, :, at] * total).T.astype(bf16)

    tiles(finish_mix)

    def ag_copy(way, d, c):
        s = lax.rem(k + peers + (2 * way - 1) * d, peers)
        rows = pl.ds(c * (width // 2), width // 2)
        return copy(
            mo_all.at[s, rows],
            mo_all.at[s, rows],
            ag_sem.at[0, way, d, c],
            ag_sem.at[1, way, d + 1, c],
            {"ctx": lax.rem(k + 1 + way * (peers - 2), peers)},
        )

    def ag_wait(way, d, c):
        s = lax.rem(k + peers + (2 * way - 1) * d, peers)
        part = mo_all.at[s, pl.ds(c * (width // 2), width // 2)]
        copy(part, part, ag_sem.at[0, way, d, c], ag_sem.at[1, way, d, c], {"ctx": k}).wait_recv()

    def relay(way, spot, d):
        @pl.when((spot >= d) & (spot < last))
        def _():
            for c in range(2):
                ag_wait(way, d, c)
                ag_copy(way, d, c).start()

    for c in range(2):

        @pl.when(k < last)
        def _():
            ag_copy(0, 0, c).start()

        @pl.when(k > 0)
        def _():
            ag_copy(1, 0, c).start()

    def line_copy(way, i, c):
        b = block_of(i, way)
        rows = pl.ds(c * half, half)
        return copy(
            line_out.at[way, b, rows],
            line_in.at[way, b, rows],
            line_sem.at[0, way, i, c],
            line_sem.at[1, way, i, c],
            {"ctx": lax.rem(k + 1 + way * (peers - 2), peers)},
        )

    for i in range(peers):
        b = block_of(i, upper)
        for o in range(2, chans, 2):
            gm_chip(b, o).wait_recv()
            gm_pass(b, o).start()

    for i in range(0, peers, 2):
        pair = [block_of(i, upper), block_of(i + 1, upper)]
        for b in pair:
            gm_mate(b).wait_recv()
            for o in range(2, chans, 2):
                gm_pass(b, o).wait_recv()

        def part(at):
            both = lax.dot_general(
                jnp.concatenate([gm_all[b].reshape(tokens, gm_all.shape[-1]) for b in pair], axis=0),
                weight[at, :],
                (((1,), (1,)), ((), ())),
                preferred_element_type=f32,
            )
            parts[pair[0], :, at] = both[:tokens]
            parts[pair[1], :, at] = both[tokens:]

        tiles(part)

        @pl.when(place == 0)
        def _():
            for n in range(i, min(i + 2, last)):
                for c in range(2):
                    rows = slice(c * half, (c + 1) * half)
                    line_out[upper, pair[n - i], rows] = parts[pair[n - i], rows].astype(bf16)
                    line_copy(upper, n, c).start()

    def gm_store():
        return pltpu.make_async_copy(gm_all, gm_out, out_sem.at[0])

    gm_store().start()

    s0, s1 = scan_up(gated)
    x_send(1, s1)

    def hop(way, spot, i, c):
        @pl.when((spot > 0) & (spot < last - i))
        def _():
            b = block_of(i, way)
            rows = slice(c * half, (c + 1) * half)
            line_copy(way, i, c).wait_recv()
            line_out[way, b, rows] = (parts[b, rows] + line_in[way, b, rows].astype(f32)).astype(bf16)
            line_copy(way, i, c).start()

    steps = [(i, c) for i in range(peers - 1) for c in range(2)]
    def hops(start, stop):
        for n in range(start, stop):
            if n < len(steps):
                hop(upper, place, *steps[n])
            if n >= 2:
                hop(1 - upper, last - place, *steps[n - 2])

    relay(1 - upper, last - place, 1)
    relay(upper, place, 1)
    hops(0, len(steps) // 2)
    for d in range(2, peers - 1):
        relay(1 - upper, last - place, d)
        relay(upper, place, d)
    hops(len(steps) // 2, len(steps) + 2)

    def line_wait(way, spot):
        for i in range(peers - 1):

            @pl.when(spot == last - i)
            def _():
                for c in range(2):
                    line_copy(way, i, c).wait_recv()

        @pl.when(spot == 0)
        def _():
            line_in[way, k] = jnp.zeros((tokens, width), bf16)

    line_wait(1 - upper, last - place)
    line_wait(upper, place)

    def own(at):
        total = parts[k, :, at] + line_in[0, k, :, at].astype(f32) + line_in[1, k, :, at].astype(f32)
        go[:, at] = total
        gy[:, at] = (total * qkv[0, :, at]).astype(bf16).astype(f32)

    tiles(own)

    g0, g1 = scan_down(gy)
    g_out[...] = g0.astype(bf16)
    states[0] = g0
    states[1] = g1

    def r_copy(d):
        return copy(g_out, g_in.at[d], r_sem.at[0, d], r_sem.at[1, d], {"ctx": lax.rem(k + peers - d, peers)})

    for d in range(1, peers):

        @pl.when(k >= d)
        def _():
            r_copy(d).start()

    def conv_back(at):
        x = gy[:, at]
        w = forward_exact(x.astype(bf16))
        f, u = pq[:, at], ab[:, at]
        p, q, a, b = f[:tokens], f[tokens:], u[:tokens], u[tokens:]
        d, e = w[:tokens], w[tokens:]
        gg[:, at] = backward(p * d + q * e, p * e - q * d) + par[2 * order : 2 * order + 1, at] * x
        gf[:, at] = backward(d * a + e * b, e * a - d * b)
        skip[:, at] = jnp.broadcast_to(jnp.sum(x * gated[:, at], axis=0, keepdims=True) / norm, (8, x.shape[1]))
        gx[0, 0:tokens, at] = go[:, at] * mix[:, at]

    tiles(conv_back, WIDE)

    def sums(at, groups):
        rows = []
        for lag in range(SHORT):
            for g in groups:
                rows.append(
                    jnp.sum(gx[g, 0:tokens, at] * ext[g, 8 - lag : 8 - lag + tokens, at], axis=0, keepdims=True)
                )
        return [row * (1.0 / norm) for row in rows]

    quad = width // 4

    def shorts_q(at):
        sh_q[0:3, at] = jnp.concatenate(sums(at, (0,)), axis=0)

    tiles(shorts_q, 128)
    sh_q[3:4] = skip[0:1]
    few = sh_q[0:4]
    shq[k] = jnp.concatenate([few[:, q * quad : (q + 1) * quad] for q in range(4)], axis=0).astype(bf16)

    def shq_copy(d):
        return copy(shq.at[k], shq.at[k], shq_sem.at[0, d], shq_sem.at[1, d], {"ctx": lax.rem(k + d, peers)})

    for d in range(1, peers):
        shq_copy(d).start()

    m0, m1 = scan_down(gf)
    for d in range(1, peers):

        @pl.when(k >= d)
        def _():
            x_copy(1, d).wait_recv()
            s_in[1] = s_in[1] + drop[4] ** (d - 1) * (
                x_in[1, d].astype(f32) + float((d - 1) * tokens) * x_in[0, d].astype(f32)
            )

    m0 = m0 + states[0] * s_in[0]
    m1 = m1 + states[1] * s_in[0] + states[0] * s_in[1]
    mom_out[0:order] = (jnp.sqrt(2.0 * par[0:order] / seq_len) * m0 * (1.0 / norm)).astype(bf16)
    grad_log = drop[5] * (0.5 * m0 - par[0:order] * m1 * (1.0 / seq_len)) * (1.0 / norm)
    mom_out[order : 2 * order] = grad_log.astype(bf16)

    def mom_copy(d):
        to = lax.rem(k + d, peers)
        return copy(
            mom_out.at[:, pl.ds(pl.multiple_of(to * cols, cols), cols)],
            mom_in.at[d],
            mom_sem.at[0, d],
            mom_sem.at[1, d],
            {"ctx": to},
        )

    for d in range(1, peers):
        mom_copy(d).start()

    r_in[...] = jnp.zeros(r_in.shape, f32)
    for d in range(1, peers):

        @pl.when(k + d < peers)
        def _():
            r_copy(d).wait_recv()
            r_in[...] = r_in[...] + drop[4] ** (d - 1) * g_in[d].astype(f32)

    def grads(at):
        total = gg[:, at] + spread(lambda row: drop[5, row, at] * r_in[row, at], at, 1.0, False)
        total = total.astype(bf16).astype(f32)
        gx[1, 0:tokens, at] = total * qkv[2, :, at]
        gx[2, 0:tokens, at] = total * qkv[1, :, at]

    tiles(grads)

    edge = [gx[g, 0 : SHORT - 1] for g in range(3)] + [jnp.zeros((2, width), f32)]
    gx_out[...] = jnp.concatenate(edge, axis=0)
    gx_copy = copy(gx_out, gx_in, gx_sem.at[0], gx_sem.at[1], {"ctx": lax.rem(k + peers - 1, peers)})

    @pl.when(k > 0)
    def _():
        gx_copy.start()

    def shorts_v(at):
        rows = sums(at, (1, 2))
        sh_v[:, at] = jnp.concatenate(rows + [jnp.zeros((2, at.size), f32)], axis=0)

    tiles(shorts_v, 128)
    shv[k] = jnp.concatenate([sh_v[:, : width // 2], sh_v[:, width // 2 :]], axis=0).astype(bf16)

    def shv_copy(d):
        return copy(shv.at[k], shv.at[k], shv_sem.at[0, d], shv_sem.at[1, d], {"ctx": lax.rem(k + d, peers)})

    for d in range(1, peers):
        shv_copy(d).start()

    def out_rows(at, start, count):
        for g in range(3):
            total = taps[0, g : g + 1, at] * gx[g, start : start + count, at]
            for lag in range(1, SHORT):
                total = total + taps[lag, g : g + 1, at] * gx[g, start + lag : start + lag + count, at]
            gproj[g, start : start + count, at] = total.astype(bf16)

    def out_most(at):
        out_rows(at, 0, tokens - 16)

    tiles(out_most, 128)

    @pl.when(k < last)
    def _():
        gx_copy.wait_recv()
        for g in range(3):
            gx[g, tokens : tokens + 2] = gx_in[2 * g : 2 * g + 2]

    @pl.when(k == last)
    def _():
        gx[:, tokens : tokens + 8] = jnp.zeros((3, 8, width), f32)

    def out_end(at):
        out_rows(at, tokens - 16, 16)

    tiles(out_end)
    gproj_store = pltpu.make_async_copy(gproj, gproj_out, out_sem.at[1])
    gproj_store.start()

    @pl.when(place == 0)
    def _():
        for d in range(1, peers):
            ag_wait(1 - upper, d, 0)
            ag_wait(1 - upper, d, 1)

    mo_store = pltpu.make_async_copy(mo_all, mo_out, out_sem.at[2])
    mo_store.start()

    for d in range(1, peers):
        mom_copy(d).wait_recv()
    par_out[0 : 2 * order] = sum((mom_in[d].astype(f32) for d in range(1, peers)), mom_out[:, mine].astype(f32))
    for d in range(1, peers):
        shq_copy(d).wait_recv()
        shv_copy(d).wait_recv()
    few = sum((shq[d].astype(f32) for d in range(1, peers)), shq[0].astype(f32))
    for q in range(4):
        sh_out[0:4, q * quad : (q + 1) * quad] = few[4 * q : 4 * q + 4]
    many = sum((shv[d].astype(f32) for d in range(1, peers)), shv[0].astype(f32))
    sh_out[8:16, : width // 2] = many[0:8]
    sh_out[8:16, width // 2 :] = many[8:16]
    par_out[2 * order : 2 * order + 8] = jnp.broadcast_to(sh_out[3:4, mine], (8, cols))

    for d in range(1, chans):
        gm_first(d).wait_send()

    @pl.when(j != k)
    def _():
        gm_first(0).wait_send()

    for b in range(peers):
        gm_mate(b).wait_send()
        for o in range(2, chans, 2):
            gm_chip(b, o).wait_send()
            gm_pass(b, o).wait_send()
    for d in range(1, peers):
        par_copy(d).wait_send()
        mom_copy(d).wait_send()
        shq_copy(d).wait_send()
        shv_copy(d).wait_send()

        @pl.when(k + d < peers)
        def _():
            x_copy(0, d).wait_send()
            x_copy(1, d).wait_send()

        @pl.when(k >= d)
        def _():
            r_copy(d).wait_send()

    @pl.when(k < last)
    def _():
        halo_copy.wait_send()

    @pl.when(k > 0)
    def _():
        gx_copy.wait_send()

    for i in range(peers - 1):
        for c in range(2):

            @pl.when(k < last - i)
            def _():
                line_copy(0, i, c).wait_send()

            @pl.when(k > i)
            def _():
                line_copy(1, i, c).wait_send()

    for d in range(peers - 1):

        @pl.when((k >= d) & (k < last))
        def _():
            ag_copy(0, d, 0).wait_send()
            ag_copy(0, d, 1).wait_send()

        @pl.when((k + d < peers) & (k > 0))
        def _():
            ag_copy(1, d, 0).wait_send()
            ag_copy(1, d, 1).wait_send()

    gm_store().wait()
    gproj_store.wait()
    mo_store.wait()


def finish_kernel(peers, order, norm, mo, gm, rows, sums, params, gproj, gshort, gskip, gres, glog, gweight):
    gproj[...] = rows[...]
    left = jnp.concatenate([mo[b] for b in range(peers)], axis=1)
    gweight[...] = lax.dot_general(
        left, gm[...], (((1,), (0,)), ((), ())), preferred_element_type=jnp.float32
    ) * (1.0 / norm)
    for lag in range(SHORT):
        gshort[lag, 0:1] = sums[lag : lag + 1]
        gshort[lag, 1:3] = sums[8 + 2 * lag : 10 + 2 * lag]
    gres[...] = params[0:order]
    glog[...] = params[order : 2 * order]
    gskip[...] = params[2 * order : 2 * order + 1]


def body_fused(projections, short_taps, residues, decay_rates, skip_gain, grad_mixed, out_weight):
    tokens, _, width = projections.shape
    peers, chans = lax.axis_size("ctx"), lax.axis_size("ch")
    order = residues.shape[1]
    cols = width // peers
    wide = out_weight.shape[1]
    seq_len = tokens * peers
    f32, bf16 = jnp.float32, jnp.bfloat16
    ahead, back = line_tables(tokens)
    rows = 2 * order + 8
    vmem = pl.BlockSpec(memory_space=pltpu.VMEM)
    far = pl.BlockSpec(memory_space=pl.ANY)
    dma = pltpu.SemaphoreType.DMA
    shape = jax.ShapeDtypeStruct
    gproj, sums, params, mo, gm = pl.pallas_call(
        partial(fused_kernel, peers, chans, order),
        out_shape=(
            shape((3, tokens, width), bf16),
            shape((16, width), f32),
            shape((rows, cols), f32),
            shape((peers, width, tokens), bf16),
            shape((peers, chans, tokens // chans, wide), bf16),
        ),
        in_specs=[far, vmem, vmem, vmem, vmem, far, far, far, far],
        out_specs=(far, vmem, vmem, far, far),
        scratch_shapes=[
            pltpu.VMEM((3, tokens, width), bf16),
            pltpu.VMEM((width, wide), bf16),
            pltpu.VMEM(ahead.shape, bf16),
            pltpu.VMEM(back.shape, bf16),
            pltpu.VMEM((rows, width), f32),
            pltpu.VMEM((16, width // 2), bf16),
            pltpu.VMEM((16, width // 2), bf16),
            pltpu.VMEM((3, tokens + 8, width), f32),
            pltpu.VMEM((3, tokens, width), f32),
            pltpu.VMEM((tokens, width), f32),
            pltpu.VMEM((6, order, width), f32),
            pltpu.VMEM((2, order, width), f32),
            pltpu.VMEM((2, order, width), bf16),
            pltpu.VMEM((2, peers, order, width), bf16),
            pltpu.VMEM((2, order, width), f32),
            pltpu.VMEM((2 * tokens, width), f32),
            pltpu.VMEM((2 * tokens, width), f32),
            pltpu.VMEM((tokens, width), f32),
            pltpu.VMEM((peers, chans, tokens // chans, wide), bf16),
            pltpu.VMEM((peers, tokens, width), f32),
            pltpu.VMEM((2, peers, tokens, width), bf16),
            pltpu.VMEM((2, peers, tokens, width), bf16),
            pltpu.VMEM((peers, width, tokens), bf16),
            pltpu.VMEM((tokens, width), f32),
            pltpu.VMEM((tokens, width), f32),
            pltpu.VMEM((tokens, width), f32),
            pltpu.VMEM((tokens, width), f32),
            pltpu.VMEM((order, width), bf16),
            pltpu.VMEM((peers, order, width), bf16),
            pltpu.VMEM((order, width), f32),
            pltpu.VMEM((2 * order, width), bf16),
            pltpu.VMEM((peers, 2 * order, cols), bf16),
            pltpu.VMEM((3, tokens + 8, width), f32),
            pltpu.VMEM((8, width), f32),
            pltpu.VMEM((8, width), f32),
            pltpu.VMEM((8, width), f32),
            pltpu.VMEM((8, width), f32),
            pltpu.VMEM((8, width), f32),
            pltpu.VMEM((peers, 16, width // 4), bf16),
            pltpu.VMEM((peers, 16, width // 2), bf16),
            pltpu.VMEM((3, tokens, width), bf16),
            dma((4,)),
            dma,
            dma((2,)),
            dma((2, peers)),
            dma((2, max(peers, chans))),
            dma((2, peers, chans)),
            dma((2, 2, peers)),
            dma((2, 2, peers, 2)),
            dma((2, 2, peers, 2)),
            dma((2, peers)),
            dma((2, peers)),
            dma((2,)),
            dma((2, peers)),
            dma((2, peers)),
            dma((3,)),
        ],
        compiler_params=pltpu.CompilerParams(
            collective_id=0, has_side_effects=True, vmem_limit_bytes=56 * 1024 * 1024
        ),
    )(
        projections.transpose(1, 0, 2),
        short_taps,
        decay_rates.T,
        residues.T,
        skip_gain[None],
        grad_mixed,
        out_weight,
        jnp.asarray(ahead),
        jnp.asarray(back),
    )
    lanes = WIDE
    whole = lambda *dims: pl.BlockSpec(dims, lambda i: (0,) * len(dims))
    gproj, gshort, gskip, gres, glog, gweight = pl.pallas_call(
        partial(finish_kernel, peers, order, math.sqrt(seq_len)),
        grid=(width // lanes,),
        out_shape=(
            shape((3, tokens, width), bf16),
            shape((SHORT, 3, width), f32),
            shape((1, cols), f32),
            shape((order, cols), f32),
            shape((order, cols), f32),
            shape((width, wide), f32),
        ),
        in_specs=[
            pl.BlockSpec((peers, lanes, tokens), lambda i: (0, i, 0)),
            whole(seq_len, wide),
            pl.BlockSpec((3, tokens, lanes), lambda i: (0, 0, i)),
            pl.BlockSpec((16, lanes), lambda i: (0, i)),
            whole(rows, cols),
        ],
        out_specs=(
            pl.BlockSpec((3, tokens, lanes), lambda i: (0, 0, i)),
            pl.BlockSpec((SHORT, 3, lanes), lambda i: (0, 0, i)),
            whole(1, cols),
            whole(order, cols),
            whole(order, cols),
            pl.BlockSpec((lanes, wide), lambda i: (i, 0)),
        ),
    )(mo, gm.reshape(seq_len, wide), gproj, sums, params)
    return (gproj.transpose(1, 0, 2), gshort, gskip[0], gres.T, glog.T, gweight)


def body(*args):
    peers, chans = lax.axis_size("ctx"), lax.axis_size("ch")
    if peers * args[0].shape[0] > 1024 or peers != chans:
        return body_factored(*args)
    return body_fused(*args)


def solution(mesh):
    return jax.shard_map(
        body,
        mesh=mesh,
        in_specs=(
            P(("groups", "ctx"), None, "ch"),
            P(None, None, "ch"),
            P(("ch", "ctx"), None),
            P(("ch", "ctx"), None),
            P(("ch", "ctx")),
            P(("groups", "ctx"), "ch"),
            P("ch", "ctx"),
        ),
        out_specs=(
            P(("groups", "ctx"), None, "ch"),
            P("groups", None, "ch"),
            P(("groups", "ch", "ctx")),
            P(("groups", "ch", "ctx"), None),
            P(("groups", "ch", "ctx"), None),
            P(("groups", "ch"), "ctx"),
        ),
        check_vma=False,
    )
```

```python
from functools import partial
import math

import jax
import jax.numpy as jnp
import numpy as np
from jax import lax
from jax.experimental import pallas as pl
from jax.experimental.pallas import tpu as pltpu
from jax.sharding import PartitionSpec as P

SHORT = 3


def from_behind(x, axis, by):
    peers = lax.axis_size(axis)
    pairs = [(i, i + by) for i in range(peers) if 0 <= i + by < peers]
    return lax.ppermute(x, axis, pairs)


def make_filter(residues, decay_rates, seq_len):
    positions = jnp.arange(seq_len, dtype=jnp.float32) / seq_len
    amplitude = residues * jnp.sqrt(2.0 * decay_rates / seq_len)
    basis = jnp.exp(-decay_rates[:, :, None] * positions[None, None, :])
    return jnp.einsum("cn,cnt->ct", amplitude, basis, precision=lax.Precision.HIGHEST)


def circle(rows_count, cols_count, period):
    left_idx = jnp.arange(rows_count, dtype=jnp.int32)[:, None]
    right_idx = jnp.arange(cols_count, dtype=jnp.int32)[None, :]
    angle = (left_idx * right_idx % period).astype(jnp.float32) * (2.0 * math.pi / period)
    return (jnp.cos(angle), jnp.sin(angle))


def spectral_tables(length):
    factor_a = 1
    while factor_a * factor_a * 4 <= length and length % (factor_a * 2) == 0:
        factor_a = factor_a * 2
    factor_b = length // factor_a
    a_cos, a_sin = circle(factor_a, factor_a, factor_a)
    b_cos, b_sin = circle(factor_b, factor_b, factor_b)
    t_cos, t_sin = circle(factor_a, factor_b, length)
    return (length, factor_a, factor_b, a_cos, a_sin, b_cos, b_sin, t_cos, t_sin)


def forward_dft(signal, tables):
    length, factor_a, factor_b, a_cos, a_sin, b_cos, b_sin, t_cos, t_sin = tables
    highest = lax.Precision.HIGHEST
    channels, seq_len = signal.shape
    grid = jnp.pad(signal, ((0, 0), (0, length - seq_len))).reshape(channels, factor_a, factor_b)
    part_real = jnp.einsum("ka,cab->ckb", a_cos, grid, precision=highest)
    part_imag = -jnp.einsum("ka,cab->ckb", a_sin, grid, precision=highest)
    turn_real = part_real * t_cos + part_imag * t_sin
    turn_imag = part_imag * t_cos - part_real * t_sin
    out_real = jnp.einsum("ckb,bm->ckm", turn_real, b_cos, precision=highest) + jnp.einsum(
        "ckb,bm->ckm", turn_imag, b_sin, precision=highest
    )
    out_imag = jnp.einsum("ckb,bm->ckm", turn_imag, b_cos, precision=highest) - jnp.einsum(
        "ckb,bm->ckm", turn_real, b_sin, precision=highest
    )
    return (out_real, out_imag)


def inverse_dft(spec_real, spec_imag, seq_len, tables):
    length, factor_a, factor_b, a_cos, a_sin, b_cos, b_sin, t_cos, t_sin = tables
    highest = lax.Precision.HIGHEST
    channels = spec_real.shape[0]
    mid_real = jnp.einsum("ckm,mb->ckb", spec_real, b_cos, precision=highest) - jnp.einsum(
        "ckm,mb->ckb", spec_imag, b_sin, precision=highest
    )
    mid_imag = jnp.einsum("ckm,mb->ckb", spec_imag, b_cos, precision=highest) + jnp.einsum(
        "ckm,mb->ckb", spec_real, b_sin, precision=highest
    )
    turn_real = mid_real * t_cos - mid_imag * t_sin
    turn_imag = mid_imag * t_cos + mid_real * t_sin
    values = jnp.einsum("ak,ckb->cab", a_cos, turn_real, precision=highest) - jnp.einsum(
        "ak,ckb->cab", a_sin, turn_imag, precision=highest
    )
    return values.reshape(channels, length)[:, :seq_len] / length


def short_mix(extended, short_taps, tokens):
    running = jnp.zeros((tokens,) + extended.shape[1:], jnp.float32)
    for lag_index in range(SHORT):
        start_row = SHORT - 1 - lag_index
        running = running + short_taps[lag_index] * extended[start_row : start_row + tokens]
    return running


def mix_long(gate_cols, spec_h, gain, seq_len, tables):
    gate_f = gate_cols.astype(jnp.float32)
    u_real, u_imag = forward_dft(gate_f, tables)
    prod_real = spec_h[0] * u_real - spec_h[1] * u_imag
    prod_imag = spec_h[0] * u_imag + spec_h[1] * u_real
    mix_cols = (inverse_dft(prod_real, prod_imag, seq_len, tables) + gain[:, None] * gate_f).astype(
        jnp.bfloat16
    )
    return (mix_cols, (u_real, u_imag))


def grad_long(grad_cols_in, gate_cols, spec_u, spec_h, gain, seq_len, tables):
    grad_f = grad_cols_in.astype(jnp.float32)
    g_real, g_imag = forward_dft(grad_f, tables)
    back_real = spec_h[0] * g_real + spec_h[1] * g_imag
    back_imag = spec_h[0] * g_imag - spec_h[1] * g_real
    grad_cols = (
        inverse_dft(back_real, back_imag, seq_len, tables) + gain[:, None] * grad_f
    ).astype(jnp.bfloat16)
    corr_real = g_real * spec_u[0] + g_imag * spec_u[1]
    corr_imag = g_imag * spec_u[0] - g_real * spec_u[1]
    grad_filter = inverse_dft(corr_real, corr_imag, seq_len, tables)
    skip_sum = jnp.sum(grad_f * gate_cols.astype(jnp.float32), axis=1)
    return (grad_cols, grad_filter, skip_sum)


def body_factored(projections, short_taps, residues, decay_rates, skip_gain, grad_mixed, out_weight):
    tokens = projections.shape[0]
    seq_len = tokens * lax.axis_size("ctx")
    norm_factor = math.sqrt(seq_len)
    tables = spectral_tables(2 * seq_len)
    earlier = from_behind(projections[tokens - SHORT + 1 :], "ctx", 1)
    ext_proj = jnp.concatenate([earlier, projections], axis=0)
    mixed_in = short_mix(ext_proj, short_taps, tokens)
    query_rows = mixed_in[:, 0]
    key_rows = mixed_in[:, 1]
    value_rows = mixed_in[:, 2]
    gated_rows = (key_rows * value_rows).astype(jnp.bfloat16)
    long_filter, filter_vjp = jax.vjp(partial(make_filter, seq_len=seq_len), residues, decay_rates)
    spec_h = forward_dft(long_filter, tables)
    out_rows = lax.all_gather(grad_mixed, "ch", axis=1, tiled=True)
    grad_out = lax.dot_general(
        out_rows,
        lax.all_gather(out_weight, "ctx", axis=1, tiled=True),
        (((1,), (1,)), ((), ())),
        preferred_element_type=jnp.float32,
    )
    grad_y = (grad_out * query_rows).astype(jnp.bfloat16)
    gate_cols, grad_cols_in = (
        lax.all_to_all(gated_rows.T, "ctx", split_axis=0, concat_axis=1, tiled=True),
        lax.all_to_all(grad_y.T, "ctx", split_axis=0, concat_axis=1, tiled=True),
    )
    mix_cols, spec_u = mix_long(gate_cols, spec_h, skip_gain, seq_len, tables)
    grad_cols, grad_filter, skip_sum = grad_long(
        grad_cols_in, gate_cols, spec_u, spec_h, skip_gain, seq_len, tables
    )
    returned = (
        lax.all_to_all(mix_cols, "ctx", split_axis=1, concat_axis=0, tiled=True),
        lax.all_to_all(grad_cols, "ctx", split_axis=1, concat_axis=0, tiled=True),
    )
    mix_rows = returned[0].T
    grad_gated = returned[1].T
    grad_res, grad_rate = filter_vjp(grad_filter)
    grad_residues = grad_res / norm_factor
    grad_log_rates = grad_rate * decay_rates / norm_factor
    grad_skip = skip_sum / norm_factor
    mixed_out = (query_rows * mix_rows).astype(jnp.bfloat16)
    grad_mix = jnp.stack(
        [grad_out * mix_rows, grad_gated * value_rows, grad_gated * key_rows], axis=1
    )
    later = from_behind(grad_mix[: SHORT - 1], "ctx", -1)
    ext_grad = jnp.concatenate([grad_mix, later], axis=0)
    running = jnp.zeros(grad_mix.shape, jnp.float32)
    short_terms = []
    for lag_index in range(SHORT):
        running = running + short_taps[lag_index] * ext_grad[lag_index : lag_index + tokens]
        start_row = SHORT - 1 - lag_index
        short_terms.append(jnp.sum(grad_mix * ext_proj[start_row : start_row + tokens], axis=0))
    grad_projections = running.astype(jnp.bfloat16)
    grad_short = lax.psum(jnp.stack(short_terms, axis=0), "ctx") / norm_factor
    partial_term = lax.dot_general(
        mixed_out, out_rows, (((0,), (0,)), ((), ())), preferred_element_type=jnp.float32
    )
    weight_sum = lax.psum_scatter(partial_term, "ctx", scatter_dimension=1, tiled=True)
    grad_weight = weight_sum / norm_factor
    return (grad_projections, grad_short, grad_skip, grad_residues, grad_log_rates, grad_weight)


def split(x):
    high = x.astype(jnp.bfloat16)
    return high, (x - high.astype(jnp.float32)).astype(jnp.bfloat16)


LANES = 256
WIDE = 512


def line_tables(tokens):
    steps = np.arange(tokens, dtype=np.int64)[None, :]
    freqs = 2 * np.arange(tokens, dtype=np.int64)[:, None] + 1
    angle = (freqs * steps % (4 * tokens)) * (2.0 * math.pi / (4 * tokens))
    wave = np.concatenate([np.cos(angle), np.sin(angle)], axis=0).astype(np.float32)
    high = wave.astype(jnp.bfloat16)
    low = (wave - high.astype(np.float32)).astype(jnp.bfloat16)
    ahead = np.concatenate([high, low], axis=1)
    back = np.concatenate([high.T, low.T], axis=0)
    return ahead, back


def fused_kernel(
    peers, chans, order,
    proj_far, taps, rates, amps, gain, gm, weight_far, ahead_far, back_far,
    gproj_out, sh_out, par_out, mo_out, gm_out,
    proj, weight, ahead, back, par, hal_out, hal_in, ext, qkv, gated, drop, states, x_out, x_in, s_in, pq, ab, mix, gm_all, parts, line_in, line_out,
    mo_all, go, gy, gg, gf, g_out, g_in, r_in, mom_out, mom_in, gx, gx_out, gx_in, skip, sh_q, sh_v, shq, shv, gproj,
    load_sem, local_sem, halo_sem, par_sem, gm1_sem, gm2_sem, x_sem, line_sem, ag_sem, r_sem, mom_sem, gx_sem,
    shq_sem, shv_sem, out_sem,
):
    f32, bf16 = jnp.float32, jnp.bfloat16
    k = lax.axis_index("ctx")
    j = lax.axis_index("ch")
    loads = [
        pltpu.make_async_copy(far, near, load_sem.at[n])
        for n, (far, near) in enumerate(
            ((proj_far, proj), (weight_far, weight), (ahead_far, ahead), (back_far, back))
        )
    ]
    for load in loads:
        load.start()
    _, tokens, width = proj.shape
    cols = width // peers
    quarter = tokens // chans
    half = tokens // 2
    seq_len = tokens * peers
    norm = math.sqrt(seq_len)
    last = peers - 1

    def copy(src, dst, send, recv, where):
        return pltpu.make_async_remote_copy(
            src_ref=src,
            dst_ref=dst,
            send_sem=send,
            recv_sem=recv,
            device_id=where,
            device_id_type=pl.DeviceIdType.MESH,
        )

    def tiles(fn, lanes=LANES, start=0, stop=width):
        def step(i, carry):
            fn(pl.ds(pl.multiple_of(i * lanes, lanes), lanes))
            return carry

        lax.fori_loop(start // lanes, stop // lanes, step, 0)

    def dot(a, b):
        return lax.dot_general(a, b, (((1,), (0,)), ((), ())), preferred_element_type=f32)

    def forward_exact(x):
        return dot(ahead[...], jnp.concatenate([x, x], axis=0))

    def forward(x):
        high, low = split(x)
        return forward_exact(high) + dot(ahead[:, :tokens], low)

    def backward(top, bottom):
        high, low = split(jnp.concatenate([top, bottom], axis=0))
        both = dot(back[...], high)
        return (both[:tokens] + both[tokens:] + dot(back[:tokens], low)) * (1.0 / tokens)

    barrier = pltpu.get_barrier_semaphore()
    for dk in range(peers):
        for dj in range(chans):
            if dk or dj:
                pl.semaphore_signal(
                    barrier,
                    inc=1,
                    device_id={"ctx": lax.rem(k + dk, peers), "ch": lax.rem(j + dj, chans)},
                    device_id_type=pl.DeviceIdType.MESH,
                )

    loads[0].wait()

    def widen(at):
        for g in range(3):
            ext[g, 0:8, at] = jnp.zeros((8, at.size), f32)
            ext[g, 8 : 8 + tokens, at] = proj[g, :, at].astype(f32)

    tiles(widen)

    def short_rows(at, count):
        rows = []
        for g in range(3):
            total = taps[0, g : g + 1, at] * ext[g, 8 : 8 + count, at]
            for lag in range(1, SHORT):
                total = total + taps[lag, g : g + 1, at] * ext[g, 8 - lag : 8 - lag + count, at]
            qkv[g, 0:count, at] = total
            rows.append(total)
        gated[0:count, at] = (rows[1] * rows[2]).astype(bf16).astype(f32)

    def short(at):
        short_rows(at, tokens)

    tiles(short, 128)
    mine = pl.ds(pl.multiple_of(k * cols, cols), cols)
    par[0:order, mine] = rates[...]
    par[order : 2 * order, mine] = amps[...]
    edge = [ext[g, 8 + tokens - (SHORT - 1) : 8 + tokens] for g in range(3)]
    edge = jnp.concatenate(edge + [jnp.zeros((2, width), f32)], axis=0)
    hal_out[...] = jnp.concatenate([edge[:, : width // 2], edge[:, width // 2 :]], axis=0).astype(bf16)
    par[2 * order : 2 * order + 8, mine] = jnp.broadcast_to(gain[...], (8, cols))
    pl.semaphore_wait(barrier, peers * chans - 1)

    def gm_first(d):
        q = lax.rem(j + d, chans)
        return copy(
            gm.at[pl.ds(pl.multiple_of(q * quarter, quarter), quarter)],
            gm_all.at[k, q],
            gm1_sem.at[0, d],
            gm1_sem.at[1, k],
            {"ctx": j, "ch": q},
        )

    def gm_own():
        return pltpu.make_async_copy(
            gm.at[pl.ds(pl.multiple_of(j * quarter, quarter), quarter)], gm_all.at[k, j], local_sem
        )

    halo_copy = copy(hal_out, hal_in, halo_sem.at[0], halo_sem.at[1], {"ctx": lax.rem(k + 1, peers)})

    @pl.when(k < last)
    def _():
        halo_copy.start()


    def par_copy(d):
        return copy(par.at[:, mine], par.at[:, mine], par_sem.at[0, d], par_sem.at[1, d], {"ctx": lax.rem(k + d, peers)})

    for d in range(1, peers):
        par_copy(d).start()

    for d in range(1, chans):
        gm_first(d).start()

    @pl.when(j != k)
    def _():
        gm_first(0).start()

    @pl.when(j == k)
    def _():
        gm_own().start()

    @pl.when(k > 0)
    def _():
        halo_copy.wait_recv()
        edge = hal_in[...].astype(f32)
        for g in range(3):
            ext[g, 6:8, : width // 2] = edge[2 * g : 2 * g + 2]
            ext[g, 6:8, width // 2 :] = edge[8 + 2 * g : 10 + 2 * g]

        def short_head(at):
            short_rows(at, 8)

        tiles(short_head)

    mate = j + 1 - 2 * lax.rem(j, 2)

    def gm_mate(b):
        return copy(gm_all.at[b, j], gm_all.at[b, j], gm2_sem.at[0, b, 0], gm2_sem.at[1, b, 0], {"ch": mate})

    def gm_chip(b, o):
        return copy(
            gm_all.at[b, j],
            gm_all.at[b, j],
            gm2_sem.at[0, b, o],
            gm2_sem.at[1, b, o],
            {"ch": lax.rem(j + o, chans)},
        )

    def gm_pass(b, o):
        f = lax.rem(j + chans - o, chans)
        return copy(
            gm_all.at[b, f], gm_all.at[b, f], gm2_sem.at[0, b, o + 1], gm2_sem.at[1, b, o + 1], {"ch": mate}
        )

    def gm_arrived(b):
        copy(gm_all.at[b, j], gm_all.at[b, j], gm1_sem.at[0, 0], gm1_sem.at[1, b], {"ctx": k, "ch": j}).wait_recv()

    for load in loads[1:]:
        load.wait()
    for d in range(1, peers):
        par_copy(d).wait_recv()
    rate = par[0:order]
    drop[0] = jnp.exp(rate * (-1.0 / seq_len))
    drop[1] = jnp.exp(rate * (-8.0 / seq_len))
    drop[2] = jnp.exp(rate * (-16.0 / seq_len))
    drop[3] = jnp.exp(rate * (-32.0 / seq_len))
    drop[4] = jnp.exp(rate * (-float(tokens) / seq_len))
    drop[5] = par[order : 2 * order] * jnp.sqrt(2.0 * rate / seq_len)

    def scan_up(source):
        decay = drop[0]

        def step(i, carry):
            s, s1 = carry
            for r in range(8):
                u = s + source[pl.ds(i * 8 + r, 1)]
                s1 = decay * (s1 + u)
                s = decay * u
            return s, s1

        zero = jnp.zeros((order, width), f32)
        return lax.fori_loop(0, tokens // 8, step, (zero, zero), unroll=4)

    def scan_down(source):
        decay = drop[0]

        def step(i, carry):
            s, s1 = carry
            for r in range(8):
                s1 = decay * (s1 + s)
                s = decay * s + source[pl.ds(tokens - 1 - i * 8 - r, 1)]
            return s, s1

        zero = jnp.zeros((order, width), f32)
        return lax.fori_loop(0, tokens // 8, step, (zero, zero), unroll=4)

    def scan_one(source):
        decay = drop[0]

        def step(i, s):
            for r in range(8):
                s = decay * (s + source[pl.ds(i * 8 + r, 1)])
            return s

        return lax.fori_loop(0, tokens // 8, step, jnp.zeros((order, width), f32), unroll=4)

    def spread(head, at, start, falling):
        lanes = at.size
        iota = lax.broadcasted_iota(jnp.int32, (8, lanes), 0).astype(f32)
        place = (iota if falling else 7.0 - iota) + start
        count = tokens // 8

        def mode(n, acc):
            row = pl.ds(n, 1)
            v = head(row) * jnp.exp(par[row, at] * (place * (-1.0 / seq_len)))
            d8, d16, d32 = drop[1, row, at], drop[2, row, at], drop[3, row, at]
            first = [v, v * d8]
            first = first + [x * d16 for x in first]
            out = []
            for i in range(0, count, 4):
                out += [acc[i + m] + first[m] for m in range(4)]
                first = [x * d32 for x in first]
            return tuple(out)

        zero = jnp.zeros((8, lanes), f32)
        acc = lax.fori_loop(0, order, mode, (zero,) * count, unroll=order)
        return jnp.concatenate(acc if falling else acc[::-1], axis=0)


    def x_copy(i, d):
        return copy(x_out.at[i], x_in.at[i, d], x_sem.at[0, i, d], x_sem.at[1, i, d], {"ctx": lax.rem(k + d, peers)})

    def x_send(i, state):
        x_out[i] = state.astype(bf16)
        for d in range(1, peers):

            @pl.when(k + d < peers)
            def _():
                x_copy(i, d).start()

    x_send(0, scan_one(gated))

    def filters(at):
        gf[:, at] = spread(lambda row: drop[5, row, at], at, 0.0, True)

    def conv(at):
        f = forward(gf[:, at])
        x = gated[:, at]
        u = forward_exact(x.astype(bf16))
        pq[:, at] = f
        ab[:, at] = u
        p, q, a, b = f[:tokens], f[tokens:], u[:tokens], u[tokens:]
        mix[:, at] = backward(p * a - q * b, p * b + q * a) + par[2 * order : 2 * order + 1, at] * x

    upper = jnp.where(k < peers // 2, 0, 1)
    place = jnp.where(upper == 0, k, last - k)

    def block_of(i, way):
        return jnp.where(way == 0, last - i, i)

    tiles(filters)
    tiles(conv, WIDE, 0, width // 2)
    for i in range(peers):
        b = block_of(i, upper)

        @pl.when((j != k) | (k != b))
        def _():
            gm_arrived(b)

        @pl.when((j == k) & (k == b))
        def _():
            gm_own().wait()

        for o in range(2, chans, 2):
            gm_chip(b, o).start()
        gm_mate(b).start()

    tiles(conv, WIDE, width // 2, width)

    s_in[...] = jnp.zeros(s_in.shape, f32)
    for d in range(1, peers):

        @pl.when(k >= d)
        def _():
            x_copy(0, d).wait_recv()
            s_in[0] = s_in[0] + drop[4] ** (d - 1) * x_in[0, d].astype(f32)

    def finish_mix(at):
        total = mix[:, at] + spread(lambda row: drop[5, row, at] * s_in[0, row, at], at, 0.0, True)
        total = total.astype(bf16).astype(f32)
        mix[:, at] = total
        mo_all[k, at] = (qkv[0, :, at] * total).T.astype(bf16)

    tiles(finish_mix)

    def ag_copy(way, d, c):
        s = lax.rem(k + peers + (2 * way - 1) * d, peers)
        rows = pl.ds(c * (width // 2), width // 2)
        return copy(
            mo_all.at[s, rows],
            mo_all.at[s, rows],
            ag_sem.at[0, way, d, c],
            ag_sem.at[1, way, d + 1, c],
            {"ctx": lax.rem(k + 1 + way * (peers - 2), peers)},
        )

    def ag_wait(way, d, c):
        s = lax.rem(k + peers + (2 * way - 1) * d, peers)
        part = mo_all.at[s, pl.ds(c * (width // 2), width // 2)]
        copy(part, part, ag_sem.at[0, way, d, c], ag_sem.at[1, way, d, c], {"ctx": k}).wait_recv()

    def relay(way, spot, d):
        @pl.when((spot >= d) & (spot < last))
        def _():
            for c in range(2):
                ag_wait(way, d, c)
                ag_copy(way, d, c).start()

    for c in range(2):

        @pl.when(k < last)
        def _():
            ag_copy(0, 0, c).start()

        @pl.when(k > 0)
        def _():
            ag_copy(1, 0, c).start()

    def line_copy(way, i, c):
        b = block_of(i, way)
        rows = pl.ds(c * half, half)
        return copy(
            line_out.at[way, b, rows],
            line_in.at[way, b, rows],
            line_sem.at[0, way, i, c],
            line_sem.at[1, way, i, c],
            {"ctx": lax.rem(k + 1 + way * (peers - 2), peers)},
        )

    for i in range(peers):
        b = block_of(i, upper)
        for o in range(2, chans, 2):
            gm_chip(b, o).wait_recv()
            gm_pass(b, o).start()

    for i in range(0, peers, 2):
        pair = [block_of(i, upper), block_of(i + 1, upper)]
        for b in pair:
            gm_mate(b).wait_recv()
            for o in range(2, chans, 2):
                gm_pass(b, o).wait_recv()

        def part(at):
            both = lax.dot_general(
                jnp.concatenate([gm_all[b].reshape(tokens, gm_all.shape[-1]) for b in pair], axis=0),
                weight[at, :],
                (((1,), (1,)), ((), ())),
                preferred_element_type=f32,
            )
            parts[pair[0], :, at] = both[:tokens]
            parts[pair[1], :, at] = both[tokens:]

        tiles(part)

        @pl.when(place == 0)
        def _():
            for n in range(i, min(i + 2, last)):
                for c in range(2):
                    rows = slice(c * half, (c + 1) * half)
                    line_out[upper, pair[n - i], rows] = parts[pair[n - i], rows].astype(bf16)
                    line_copy(upper, n, c).start()

    def gm_store():
        return pltpu.make_async_copy(gm_all, gm_out, out_sem.at[0])

    gm_store().start()

    s0, s1 = scan_up(gated)
    x_send(1, s1)

    def hop(way, spot, i, c):
        @pl.when((spot > 0) & (spot < last - i))
        def _():
            b = block_of(i, way)
            rows = slice(c * half, (c + 1) * half)
            line_copy(way, i, c).wait_recv()
            line_out[way, b, rows] = (parts[b, rows] + line_in[way, b, rows].astype(f32)).astype(bf16)
            line_copy(way, i, c).start()

    steps = [(i, c) for i in range(peers - 1) for c in range(2)]
    def hops(start, stop):
        for n in range(start, stop):
            if n < len(steps):
                hop(upper, place, *steps[n])
            if n >= 2:
                hop(1 - upper, last - place, *steps[n - 2])

    hops(0, 1)
    relay(1 - upper, last - place, 1)
    relay(upper, place, 1)
    hops(1, len(steps) // 2)
    for d in range(2, peers - 1):
        relay(1 - upper, last - place, d)
        relay(upper, place, d)
    hops(len(steps) // 2, len(steps) + 2)

    def line_wait(way, spot):
        for i in range(peers - 1):

            @pl.when(spot == last - i)
            def _():
                for c in range(2):
                    line_copy(way, i, c).wait_recv()

        @pl.when(spot == 0)
        def _():
            line_in[way, k] = jnp.zeros((tokens, width), bf16)

    line_wait(1 - upper, last - place)
    line_wait(upper, place)

    def own(at):
        total = parts[k, :, at] + line_in[0, k, :, at].astype(f32) + line_in[1, k, :, at].astype(f32)
        go[:, at] = total
        gy[:, at] = (total * qkv[0, :, at]).astype(bf16).astype(f32)

    tiles(own)

    g0, g1 = scan_down(gy)
    g_out[...] = g0.astype(bf16)
    states[0] = g0
    states[1] = g1

    def r_copy(d):
        return copy(g_out, g_in.at[d], r_sem.at[0, d], r_sem.at[1, d], {"ctx": lax.rem(k + peers - d, peers)})

    for d in range(1, peers):

        @pl.when(k >= d)
        def _():
            r_copy(d).start()

    def conv_back(at):
        x = gy[:, at]
        w = forward_exact(x.astype(bf16))
        f, u = pq[:, at], ab[:, at]
        p, q, a, b = f[:tokens], f[tokens:], u[:tokens], u[tokens:]
        d, e = w[:tokens], w[tokens:]
        gg[:, at] = backward(p * d + q * e, p * e - q * d) + par[2 * order : 2 * order + 1, at] * x
        gf[:, at] = backward(d * a + e * b, e * a - d * b)
        skip[:, at] = jnp.broadcast_to(jnp.sum(x * gated[:, at], axis=0, keepdims=True) / norm, (8, x.shape[1]))
        gx[0, 0:tokens, at] = go[:, at] * mix[:, at]

    tiles(conv_back, WIDE)

    def sums(at, groups):
        rows = []
        for lag in range(SHORT):
            for g in groups:
                rows.append(
                    jnp.sum(gx[g, 0:tokens, at] * ext[g, 8 - lag : 8 - lag + tokens, at], axis=0, keepdims=True)
                )
        return [row * (1.0 / norm) for row in rows]

    quad = width // 4

    def shorts_q(at):
        sh_q[0:3, at] = jnp.concatenate(sums(at, (0,)), axis=0)

    tiles(shorts_q, 128)
    sh_q[3:4] = skip[0:1]
    few = sh_q[0:4]
    shq[k] = jnp.concatenate([few[:, q * quad : (q + 1) * quad] for q in range(4)], axis=0).astype(bf16)

    def shq_copy(d):
        return copy(shq.at[k], shq.at[k], shq_sem.at[0, d], shq_sem.at[1, d], {"ctx": lax.rem(k + d, peers)})

    for d in range(1, peers):
        shq_copy(d).start()

    m0, m1 = scan_down(gf)
    for d in range(1, peers):

        @pl.when(k >= d)
        def _():
            x_copy(1, d).wait_recv()
            s_in[1] = s_in[1] + drop[4] ** (d - 1) * (
                x_in[1, d].astype(f32) + float((d - 1) * tokens) * x_in[0, d].astype(f32)
            )

    m0 = m0 + states[0] * s_in[0]
    m1 = m1 + states[1] * s_in[0] + states[0] * s_in[1]
    mom_out[0:order] = (jnp.sqrt(2.0 * par[0:order] / seq_len) * m0 * (1.0 / norm)).astype(bf16)
    grad_log = drop[5] * (0.5 * m0 - par[0:order] * m1 * (1.0 / seq_len)) * (1.0 / norm)
    mom_out[order : 2 * order] = grad_log.astype(bf16)

    def mom_copy(d):
        to = lax.rem(k + d, peers)
        return copy(
            mom_out.at[:, pl.ds(pl.multiple_of(to * cols, cols), cols)],
            mom_in.at[d],
            mom_sem.at[0, d],
            mom_sem.at[1, d],
            {"ctx": to},
        )

    for d in range(1, peers):
        mom_copy(d).start()

    r_in[...] = jnp.zeros(r_in.shape, f32)
    for d in range(1, peers):

        @pl.when(k + d < peers)
        def _():
            r_copy(d).wait_recv()
            r_in[...] = r_in[...] + drop[4] ** (d - 1) * g_in[d].astype(f32)

    def grads(at):
        total = gg[:, at] + spread(lambda row: drop[5, row, at] * r_in[row, at], at, 1.0, False)
        total = total.astype(bf16).astype(f32)
        gx[1, 0:tokens, at] = total * qkv[2, :, at]
        gx[2, 0:tokens, at] = total * qkv[1, :, at]

    tiles(grads)

    edge = [gx[g, 0 : SHORT - 1] for g in range(3)] + [jnp.zeros((2, width), f32)]
    gx_out[...] = jnp.concatenate(edge, axis=0)
    gx_copy = copy(gx_out, gx_in, gx_sem.at[0], gx_sem.at[1], {"ctx": lax.rem(k + peers - 1, peers)})

    @pl.when(k > 0)
    def _():
        gx_copy.start()

    def shorts_v(at):
        rows = sums(at, (1, 2))
        sh_v[:, at] = jnp.concatenate(rows + [jnp.zeros((2, at.size), f32)], axis=0)

    tiles(shorts_v, 128)
    shv[k] = jnp.concatenate([sh_v[:, : width // 2], sh_v[:, width // 2 :]], axis=0).astype(bf16)

    def shv_copy(d):
        return copy(shv.at[k], shv.at[k], shv_sem.at[0, d], shv_sem.at[1, d], {"ctx": lax.rem(k + d, peers)})

    for d in range(1, peers):
        shv_copy(d).start()

    def out_rows(at, start, count):
        for g in range(3):
            total = taps[0, g : g + 1, at] * gx[g, start : start + count, at]
            for lag in range(1, SHORT):
                total = total + taps[lag, g : g + 1, at] * gx[g, start + lag : start + lag + count, at]
            gproj[g, start : start + count, at] = total.astype(bf16)

    def out_most(at):
        out_rows(at, 0, tokens - 16)

    tiles(out_most, 128)

    @pl.when(k < last)
    def _():
        gx_copy.wait_recv()
        for g in range(3):
            gx[g, tokens : tokens + 2] = gx_in[2 * g : 2 * g + 2]

    @pl.when(k == last)
    def _():
        gx[:, tokens : tokens + 8] = jnp.zeros((3, 8, width), f32)

    def out_end(at):
        out_rows(at, tokens - 16, 16)

    tiles(out_end)
    gproj_store = pltpu.make_async_copy(gproj, gproj_out, out_sem.at[1])
    gproj_store.start()

    @pl.when(place == 0)
    def _():
        for d in range(1, peers):
            ag_wait(1 - upper, d, 0)
            ag_wait(1 - upper, d, 1)

    mo_store = pltpu.make_async_copy(mo_all, mo_out, out_sem.at[2])
    mo_store.start()

    for d in range(1, peers):
        mom_copy(d).wait_recv()
    par_out[0 : 2 * order] = sum((mom_in[d].astype(f32) for d in range(1, peers)), mom_out[:, mine].astype(f32))
    for d in range(1, peers):
        shq_copy(d).wait_recv()
        shv_copy(d).wait_recv()
    few = sum((shq[d].astype(f32) for d in range(1, peers)), shq[0].astype(f32))
    for q in range(4):
        sh_out[0:4, q * quad : (q + 1) * quad] = few[4 * q : 4 * q + 4]
    many = sum((shv[d].astype(f32) for d in range(1, peers)), shv[0].astype(f32))
    sh_out[8:16, : width // 2] = many[0:8]
    sh_out[8:16, width // 2 :] = many[8:16]
    par_out[2 * order : 2 * order + 8] = jnp.broadcast_to(sh_out[3:4, mine], (8, cols))

    for d in range(1, chans):
        gm_first(d).wait_send()

    @pl.when(j != k)
    def _():
        gm_first(0).wait_send()

    for b in range(peers):
        gm_mate(b).wait_send()
        for o in range(2, chans, 2):
            gm_chip(b, o).wait_send()
            gm_pass(b, o).wait_send()
    for d in range(1, peers):
        par_copy(d).wait_send()
        mom_copy(d).wait_send()
        shq_copy(d).wait_send()
        shv_copy(d).wait_send()

        @pl.when(k + d < peers)
        def _():
            x_copy(0, d).wait_send()
            x_copy(1, d).wait_send()

        @pl.when(k >= d)
        def _():
            r_copy(d).wait_send()

    @pl.when(k < last)
    def _():
        halo_copy.wait_send()

    @pl.when(k > 0)
    def _():
        gx_copy.wait_send()

    for i in range(peers - 1):
        for c in range(2):

            @pl.when(k < last - i)
            def _():
                line_copy(0, i, c).wait_send()

            @pl.when(k > i)
            def _():
                line_copy(1, i, c).wait_send()

    for d in range(peers - 1):

        @pl.when((k >= d) & (k < last))
        def _():
            ag_copy(0, d, 0).wait_send()
            ag_copy(0, d, 1).wait_send()

        @pl.when((k + d < peers) & (k > 0))
        def _():
            ag_copy(1, d, 0).wait_send()
            ag_copy(1, d, 1).wait_send()

    gm_store().wait()
    gproj_store.wait()
    mo_store.wait()


def finish_kernel(peers, order, norm, mo, gm, rows, sums, params, gproj, gshort, gskip, gres, glog, gweight):
    gproj[...] = rows[...]
    left = jnp.concatenate([mo[b] for b in range(peers)], axis=1)
    gweight[...] = lax.dot_general(
        left, gm[...], (((1,), (0,)), ((), ())), preferred_element_type=jnp.float32
    ) * (1.0 / norm)
    for lag in range(SHORT):
        gshort[lag, 0:1] = sums[lag : lag + 1]
        gshort[lag, 1:3] = sums[8 + 2 * lag : 10 + 2 * lag]
    gres[...] = params[0:order]
    glog[...] = params[order : 2 * order]
    gskip[...] = params[2 * order : 2 * order + 1]


def body_fused(projections, short_taps, residues, decay_rates, skip_gain, grad_mixed, out_weight):
    tokens, _, width = projections.shape
    peers, chans = lax.axis_size("ctx"), lax.axis_size("ch")
    order = residues.shape[1]
    cols = width // peers
    wide = out_weight.shape[1]
    seq_len = tokens * peers
    f32, bf16 = jnp.float32, jnp.bfloat16
    ahead, back = line_tables(tokens)
    rows = 2 * order + 8
    vmem = pl.BlockSpec(memory_space=pltpu.VMEM)
    far = pl.BlockSpec(memory_space=pl.ANY)
    dma = pltpu.SemaphoreType.DMA
    shape = jax.ShapeDtypeStruct
    gproj, sums, params, mo, gm = pl.pallas_call(
        partial(fused_kernel, peers, chans, order),
        out_shape=(
            shape((3, tokens, width), bf16),
            shape((16, width), f32),
            shape((rows, cols), f32),
            shape((peers, width, tokens), bf16),
            shape((peers, chans, tokens // chans, wide), bf16),
        ),
        in_specs=[far, vmem, vmem, vmem, vmem, far, far, far, far],
        out_specs=(far, vmem, vmem, far, far),
        scratch_shapes=[
            pltpu.VMEM((3, tokens, width), bf16),
            pltpu.VMEM((width, wide), bf16),
            pltpu.VMEM(ahead.shape, bf16),
            pltpu.VMEM(back.shape, bf16),
            pltpu.VMEM((rows, width), f32),
            pltpu.VMEM((16, width // 2), bf16),
            pltpu.VMEM((16, width // 2), bf16),
            pltpu.VMEM((3, tokens + 8, width), f32),
            pltpu.VMEM((3, tokens, width), f32),
            pltpu.VMEM((tokens, width), f32),
            pltpu.VMEM((6, order, width), f32),
            pltpu.VMEM((2, order, width), f32),
            pltpu.VMEM((2, order, width), bf16),
            pltpu.VMEM((2, peers, order, width), bf16),
            pltpu.VMEM((2, order, width), f32),
            pltpu.VMEM((2 * tokens, width), f32),
            pltpu.VMEM((2 * tokens, width), f32),
            pltpu.VMEM((tokens, width), f32),
            pltpu.VMEM((peers, chans, tokens // chans, wide), bf16),
            pltpu.VMEM((peers, tokens, width), f32),
            pltpu.VMEM((2, peers, tokens, width), bf16),
            pltpu.VMEM((2, peers, tokens, width), bf16),
            pltpu.VMEM((peers, width, tokens), bf16),
            pltpu.VMEM((tokens, width), f32),
            pltpu.VMEM((tokens, width), f32),
            pltpu.VMEM((tokens, width), f32),
            pltpu.VMEM((tokens, width), f32),
            pltpu.VMEM((order, width), bf16),
            pltpu.VMEM((peers, order, width), bf16),
            pltpu.VMEM((order, width), f32),
            pltpu.VMEM((2 * order, width), bf16),
            pltpu.VMEM((peers, 2 * order, cols), bf16),
            pltpu.VMEM((3, tokens + 8, width), f32),
            pltpu.VMEM((8, width), f32),
            pltpu.VMEM((8, width), f32),
            pltpu.VMEM((8, width), f32),
            pltpu.VMEM((8, width), f32),
            pltpu.VMEM((8, width), f32),
            pltpu.VMEM((peers, 16, width // 4), bf16),
            pltpu.VMEM((peers, 16, width // 2), bf16),
            pltpu.VMEM((3, tokens, width), bf16),
            dma((4,)),
            dma,
            dma((2,)),
            dma((2, peers)),
            dma((2, max(peers, chans))),
            dma((2, peers, chans)),
            dma((2, 2, peers)),
            dma((2, 2, peers, 2)),
            dma((2, 2, peers, 2)),
            dma((2, peers)),
            dma((2, peers)),
            dma((2,)),
            dma((2, peers)),
            dma((2, peers)),
            dma((3,)),
        ],
        compiler_params=pltpu.CompilerParams(
            collective_id=0, has_side_effects=True, vmem_limit_bytes=56 * 1024 * 1024
        ),
    )(
        projections.transpose(1, 0, 2),
        short_taps,
        decay_rates.T,
        residues.T,
        skip_gain[None],
        grad_mixed,
        out_weight,
        jnp.asarray(ahead),
        jnp.asarray(back),
    )
    lanes = WIDE
    whole = lambda *dims: pl.BlockSpec(dims, lambda i: (0,) * len(dims))
    gproj, gshort, gskip, gres, glog, gweight = pl.pallas_call(
        partial(finish_kernel, peers, order, math.sqrt(seq_len)),
        grid=(width // lanes,),
        out_shape=(
            shape((3, tokens, width), bf16),
            shape((SHORT, 3, width), f32),
            shape((1, cols), f32),
            shape((order, cols), f32),
            shape((order, cols), f32),
            shape((width, wide), f32),
        ),
        in_specs=[
            pl.BlockSpec((peers, lanes, tokens), lambda i: (0, i, 0)),
            whole(seq_len, wide),
            pl.BlockSpec((3, tokens, lanes), lambda i: (0, 0, i)),
            pl.BlockSpec((16, lanes), lambda i: (0, i)),
            whole(rows, cols),
        ],
        out_specs=(
            pl.BlockSpec((3, tokens, lanes), lambda i: (0, 0, i)),
            pl.BlockSpec((SHORT, 3, lanes), lambda i: (0, 0, i)),
            whole(1, cols),
            whole(order, cols),
            whole(order, cols),
            pl.BlockSpec((lanes, wide), lambda i: (i, 0)),
        ),
    )(mo, gm.reshape(seq_len, wide), gproj, sums, params)
    return (gproj.transpose(1, 0, 2), gshort, gskip[0], gres.T, glog.T, gweight)


def body(*args):
    peers, chans = lax.axis_size("ctx"), lax.axis_size("ch")
    if peers * args[0].shape[0] > 1024 or peers != chans:
        return body_factored(*args)
    return body_fused(*args)


def solution(mesh):
    return jax.shard_map(
        body,
        mesh=mesh,
        in_specs=(
            P(("groups", "ctx"), None, "ch"),
            P(None, None, "ch"),
            P(("ch", "ctx"), None),
            P(("ch", "ctx"), None),
            P(("ch", "ctx")),
            P(("groups", "ctx"), "ch"),
            P("ch", "ctx"),
        ),
        out_specs=(
            P(("groups", "ctx"), None, "ch"),
            P("groups", None, "ch"),
            P(("groups", "ch", "ctx")),
            P(("groups", "ch", "ctx"), None),
            P(("groups", "ch", "ctx"), None),
            P(("groups", "ch"), "ctx"),
        ),
        check_vma=False,
    )
```

```python
from functools import partial
import math

import jax
import jax.numpy as jnp
import numpy as np
from jax import lax
from jax.experimental import pallas as pl
from jax.experimental.pallas import tpu as pltpu
from jax.sharding import PartitionSpec as P

SHORT = 3


def from_behind(x, axis, by):
    peers = lax.axis_size(axis)
    pairs = [(i, i + by) for i in range(peers) if 0 <= i + by < peers]
    return lax.ppermute(x, axis, pairs)


def make_filter(residues, decay_rates, seq_len):
    positions = jnp.arange(seq_len, dtype=jnp.float32) / seq_len
    amplitude = residues * jnp.sqrt(2.0 * decay_rates / seq_len)
    basis = jnp.exp(-decay_rates[:, :, None] * positions[None, None, :])
    return jnp.einsum("cn,cnt->ct", amplitude, basis, precision=lax.Precision.HIGHEST)


def circle(rows_count, cols_count, period):
    left_idx = jnp.arange(rows_count, dtype=jnp.int32)[:, None]
    right_idx = jnp.arange(cols_count, dtype=jnp.int32)[None, :]
    angle = (left_idx * right_idx % period).astype(jnp.float32) * (2.0 * math.pi / period)
    return (jnp.cos(angle), jnp.sin(angle))


def spectral_tables(length):
    factor_a = 1
    while factor_a * factor_a * 4 <= length and length % (factor_a * 2) == 0:
        factor_a = factor_a * 2
    factor_b = length // factor_a
    a_cos, a_sin = circle(factor_a, factor_a, factor_a)
    b_cos, b_sin = circle(factor_b, factor_b, factor_b)
    t_cos, t_sin = circle(factor_a, factor_b, length)
    return (length, factor_a, factor_b, a_cos, a_sin, b_cos, b_sin, t_cos, t_sin)


def forward_dft(signal, tables):
    length, factor_a, factor_b, a_cos, a_sin, b_cos, b_sin, t_cos, t_sin = tables
    highest = lax.Precision.HIGHEST
    channels, seq_len = signal.shape
    grid = jnp.pad(signal, ((0, 0), (0, length - seq_len))).reshape(channels, factor_a, factor_b)
    part_real = jnp.einsum("ka,cab->ckb", a_cos, grid, precision=highest)
    part_imag = -jnp.einsum("ka,cab->ckb", a_sin, grid, precision=highest)
    turn_real = part_real * t_cos + part_imag * t_sin
    turn_imag = part_imag * t_cos - part_real * t_sin
    out_real = jnp.einsum("ckb,bm->ckm", turn_real, b_cos, precision=highest) + jnp.einsum(
        "ckb,bm->ckm", turn_imag, b_sin, precision=highest
    )
    out_imag = jnp.einsum("ckb,bm->ckm", turn_imag, b_cos, precision=highest) - jnp.einsum(
        "ckb,bm->ckm", turn_real, b_sin, precision=highest
    )
    return (out_real, out_imag)


def inverse_dft(spec_real, spec_imag, seq_len, tables):
    length, factor_a, factor_b, a_cos, a_sin, b_cos, b_sin, t_cos, t_sin = tables
    highest = lax.Precision.HIGHEST
    channels = spec_real.shape[0]
    mid_real = jnp.einsum("ckm,mb->ckb", spec_real, b_cos, precision=highest) - jnp.einsum(
        "ckm,mb->ckb", spec_imag, b_sin, precision=highest
    )
    mid_imag = jnp.einsum("ckm,mb->ckb", spec_imag, b_cos, precision=highest) + jnp.einsum(
        "ckm,mb->ckb", spec_real, b_sin, precision=highest
    )
    turn_real = mid_real * t_cos - mid_imag * t_sin
    turn_imag = mid_imag * t_cos + mid_real * t_sin
    values = jnp.einsum("ak,ckb->cab", a_cos, turn_real, precision=highest) - jnp.einsum(
        "ak,ckb->cab", a_sin, turn_imag, precision=highest
    )
    return values.reshape(channels, length)[:, :seq_len] / length


def short_mix(extended, short_taps, tokens):
    running = jnp.zeros((tokens,) + extended.shape[1:], jnp.float32)
    for lag_index in range(SHORT):
        start_row = SHORT - 1 - lag_index
        running = running + short_taps[lag_index] * extended[start_row : start_row + tokens]
    return running


def mix_long(gate_cols, spec_h, gain, seq_len, tables):
    gate_f = gate_cols.astype(jnp.float32)
    u_real, u_imag = forward_dft(gate_f, tables)
    prod_real = spec_h[0] * u_real - spec_h[1] * u_imag
    prod_imag = spec_h[0] * u_imag + spec_h[1] * u_real
    mix_cols = (inverse_dft(prod_real, prod_imag, seq_len, tables) + gain[:, None] * gate_f).astype(
        jnp.bfloat16
    )
    return (mix_cols, (u_real, u_imag))


def grad_long(grad_cols_in, gate_cols, spec_u, spec_h, gain, seq_len, tables):
    grad_f = grad_cols_in.astype(jnp.float32)
    g_real, g_imag = forward_dft(grad_f, tables)
    back_real = spec_h[0] * g_real + spec_h[1] * g_imag
    back_imag = spec_h[0] * g_imag - spec_h[1] * g_real
    grad_cols = (
        inverse_dft(back_real, back_imag, seq_len, tables) + gain[:, None] * grad_f
    ).astype(jnp.bfloat16)
    corr_real = g_real * spec_u[0] + g_imag * spec_u[1]
    corr_imag = g_imag * spec_u[0] - g_real * spec_u[1]
    grad_filter = inverse_dft(corr_real, corr_imag, seq_len, tables)
    skip_sum = jnp.sum(grad_f * gate_cols.astype(jnp.float32), axis=1)
    return (grad_cols, grad_filter, skip_sum)


def body_factored(projections, short_taps, residues, decay_rates, skip_gain, grad_mixed, out_weight):
    tokens = projections.shape[0]
    seq_len = tokens * lax.axis_size("ctx")
    norm_factor = math.sqrt(seq_len)
    tables = spectral_tables(2 * seq_len)
    earlier = from_behind(projections[tokens - SHORT + 1 :], "ctx", 1)
    ext_proj = jnp.concatenate([earlier, projections], axis=0)
    mixed_in = short_mix(ext_proj, short_taps, tokens)
    query_rows = mixed_in[:, 0]
    key_rows = mixed_in[:, 1]
    value_rows = mixed_in[:, 2]
    gated_rows = (key_rows * value_rows).astype(jnp.bfloat16)
    long_filter, filter_vjp = jax.vjp(partial(make_filter, seq_len=seq_len), residues, decay_rates)
    spec_h = forward_dft(long_filter, tables)
    out_rows = lax.all_gather(grad_mixed, "ch", axis=1, tiled=True)
    grad_out = lax.dot_general(
        out_rows,
        lax.all_gather(out_weight, "ctx", axis=1, tiled=True),
        (((1,), (1,)), ((), ())),
        preferred_element_type=jnp.float32,
    )
    grad_y = (grad_out * query_rows).astype(jnp.bfloat16)
    gate_cols, grad_cols_in = (
        lax.all_to_all(gated_rows.T, "ctx", split_axis=0, concat_axis=1, tiled=True),
        lax.all_to_all(grad_y.T, "ctx", split_axis=0, concat_axis=1, tiled=True),
    )
    mix_cols, spec_u = mix_long(gate_cols, spec_h, skip_gain, seq_len, tables)
    grad_cols, grad_filter, skip_sum = grad_long(
        grad_cols_in, gate_cols, spec_u, spec_h, skip_gain, seq_len, tables
    )
    returned = (
        lax.all_to_all(mix_cols, "ctx", split_axis=1, concat_axis=0, tiled=True),
        lax.all_to_all(grad_cols, "ctx", split_axis=1, concat_axis=0, tiled=True),
    )
    mix_rows = returned[0].T
    grad_gated = returned[1].T
    grad_res, grad_rate = filter_vjp(grad_filter)
    grad_residues = grad_res / norm_factor
    grad_log_rates = grad_rate * decay_rates / norm_factor
    grad_skip = skip_sum / norm_factor
    mixed_out = (query_rows * mix_rows).astype(jnp.bfloat16)
    grad_mix = jnp.stack(
        [grad_out * mix_rows, grad_gated * value_rows, grad_gated * key_rows], axis=1
    )
    later = from_behind(grad_mix[: SHORT - 1], "ctx", -1)
    ext_grad = jnp.concatenate([grad_mix, later], axis=0)
    running = jnp.zeros(grad_mix.shape, jnp.float32)
    short_terms = []
    for lag_index in range(SHORT):
        running = running + short_taps[lag_index] * ext_grad[lag_index : lag_index + tokens]
        start_row = SHORT - 1 - lag_index
        short_terms.append(jnp.sum(grad_mix * ext_proj[start_row : start_row + tokens], axis=0))
    grad_projections = running.astype(jnp.bfloat16)
    grad_short = lax.psum(jnp.stack(short_terms, axis=0), "ctx") / norm_factor
    partial_term = lax.dot_general(
        mixed_out, out_rows, (((0,), (0,)), ((), ())), preferred_element_type=jnp.float32
    )
    weight_sum = lax.psum_scatter(partial_term, "ctx", scatter_dimension=1, tiled=True)
    grad_weight = weight_sum / norm_factor
    return (grad_projections, grad_short, grad_skip, grad_residues, grad_log_rates, grad_weight)


def split(x):
    high = x.astype(jnp.bfloat16)
    return high, (x - high.astype(jnp.float32)).astype(jnp.bfloat16)


LANES = 256
WIDE = 512


def line_tables(tokens):
    steps = np.arange(tokens, dtype=np.int64)[None, :]
    freqs = 2 * np.arange(tokens, dtype=np.int64)[:, None] + 1
    angle = (freqs * steps % (4 * tokens)) * (2.0 * math.pi / (4 * tokens))
    wave = np.concatenate([np.cos(angle), np.sin(angle)], axis=0).astype(np.float32)
    high = wave.astype(jnp.bfloat16)
    low = (wave - high.astype(np.float32)).astype(jnp.bfloat16)
    ahead = np.concatenate([high, low], axis=1)
    back = np.concatenate([high.T, low.T], axis=0)
    return ahead, back


def fused_kernel(
    peers, chans, order,
    proj_far, taps, rates, amps, gain, gm, weight_far, ahead_far, back_far,
    gproj_out, sh_out, par_out, mo_out, gm_out,
    proj, weight, ahead, back, par, hal_out, hal_in, ext, qkv, gated, drop, states, x_out, x_in, s_in, pq, ab, mix, gm_all, parts, line_in, line_out,
    mo_all, go, gy, gg, gf, g_out, g_in, r_in, mom_out, mom_in, gx, gx_out, gx_in, skip, sh_q, sh_v, shq, shv, gproj,
    load_sem, local_sem, halo_sem, par_sem, gm1_sem, gm2_sem, x_sem, line_sem, ag_sem, r_sem, mom_sem, gx_sem,
    shq_sem, shv_sem, out_sem,
):
    f32, bf16 = jnp.float32, jnp.bfloat16
    k = lax.axis_index("ctx")
    j = lax.axis_index("ch")
    loads = [
        pltpu.make_async_copy(far, near, load_sem.at[n])
        for n, (far, near) in enumerate(
            ((proj_far, proj), (weight_far, weight), (ahead_far, ahead), (back_far, back))
        )
    ]
    for load in loads:
        load.start()
    _, tokens, width = proj.shape
    cols = width // peers
    quarter = tokens // chans
    half = tokens // 2
    seq_len = tokens * peers
    norm = math.sqrt(seq_len)
    last = peers - 1

    def copy(src, dst, send, recv, where):
        return pltpu.make_async_remote_copy(
            src_ref=src,
            dst_ref=dst,
            send_sem=send,
            recv_sem=recv,
            device_id=where,
            device_id_type=pl.DeviceIdType.MESH,
        )

    def tiles(fn, lanes=LANES, start=0, stop=width):
        def step(i, carry):
            fn(pl.ds(pl.multiple_of(i * lanes, lanes), lanes))
            return carry

        lax.fori_loop(start // lanes, stop // lanes, step, 0)

    def dot(a, b):
        return lax.dot_general(a, b, (((1,), (0,)), ((), ())), preferred_element_type=f32)

    def forward_exact(x):
        return dot(ahead[...], jnp.concatenate([x, x], axis=0))

    def forward(x):
        high, low = split(x)
        return forward_exact(high) + dot(ahead[:, :tokens], low)

    def backward(top, bottom):
        high, low = split(jnp.concatenate([top, bottom], axis=0))
        both = dot(back[...], high)
        return (both[:tokens] + both[tokens:] + dot(back[:tokens], low)) * (1.0 / tokens)

    barrier = pltpu.get_barrier_semaphore()
    for dk in range(peers):
        for dj in range(chans):
            if dk or dj:
                pl.semaphore_signal(
                    barrier,
                    inc=1,
                    device_id={"ctx": lax.rem(k + dk, peers), "ch": lax.rem(j + dj, chans)},
                    device_id_type=pl.DeviceIdType.MESH,
                )

    loads[0].wait()

    def widen(at):
        for g in range(3):
            ext[g, 0:8, at] = jnp.zeros((8, at.size), f32)
            ext[g, 8 : 8 + tokens, at] = proj[g, :, at].astype(f32)

    tiles(widen)

    def short_rows(at, count):
        rows = []
        for g in range(3):
            total = taps[0, g : g + 1, at] * ext[g, 8 : 8 + count, at]
            for lag in range(1, SHORT):
                total = total + taps[lag, g : g + 1, at] * ext[g, 8 - lag : 8 - lag + count, at]
            qkv[g, 0:count, at] = total
            rows.append(total)
        gated[0:count, at] = (rows[1] * rows[2]).astype(bf16).astype(f32)

    def short(at):
        short_rows(at, tokens)

    tiles(short, 128)
    mine = pl.ds(pl.multiple_of(k * cols, cols), cols)
    par[0:order, mine] = rates[...]
    par[order : 2 * order, mine] = amps[...]
    edge = [ext[g, 8 + tokens - (SHORT - 1) : 8 + tokens] for g in range(3)]
    edge = jnp.concatenate(edge + [jnp.zeros((2, width), f32)], axis=0)
    hal_out[...] = jnp.concatenate([edge[:, : width // 2], edge[:, width // 2 :]], axis=0).astype(bf16)
    par[2 * order : 2 * order + 8, mine] = jnp.broadcast_to(gain[...], (8, cols))
    pl.semaphore_wait(barrier, peers * chans - 1)

    def gm_first(d):
        q = lax.rem(j + d, chans)
        return copy(
            gm.at[pl.ds(pl.multiple_of(q * quarter, quarter), quarter)],
            gm_all.at[k, q],
            gm1_sem.at[0, d],
            gm1_sem.at[1, k],
            {"ctx": j, "ch": q},
        )

    def gm_own():
        return pltpu.make_async_copy(
            gm.at[pl.ds(pl.multiple_of(j * quarter, quarter), quarter)], gm_all.at[k, j], local_sem
        )

    halo_copy = copy(hal_out, hal_in, halo_sem.at[0], halo_sem.at[1], {"ctx": lax.rem(k + 1, peers)})

    @pl.when(k < last)
    def _():
        halo_copy.start()


    def par_copy(d):
        return copy(par.at[:, mine], par.at[:, mine], par_sem.at[0, d], par_sem.at[1, d], {"ctx": lax.rem(k + d, peers)})

    for d in range(1, peers):
        par_copy(d).start()

    for d in range(1, chans):
        gm_first(d).start()

    @pl.when(j != k)
    def _():
        gm_first(0).start()

    @pl.when(j == k)
    def _():
        gm_own().start()

    @pl.when(k > 0)
    def _():
        halo_copy.wait_recv()
        edge = hal_in[...].astype(f32)
        for g in range(3):
            ext[g, 6:8, : width // 2] = edge[2 * g : 2 * g + 2]
            ext[g, 6:8, width // 2 :] = edge[8 + 2 * g : 10 + 2 * g]

        def short_head(at):
            short_rows(at, 8)

        tiles(short_head)

    mate = j + 1 - 2 * lax.rem(j, 2)

    def gm_mate(b):
        return copy(gm_all.at[b, j], gm_all.at[b, j], gm2_sem.at[0, b, 0], gm2_sem.at[1, b, 0], {"ch": mate})

    def gm_chip(b, o):
        return copy(
            gm_all.at[b, j],
            gm_all.at[b, j],
            gm2_sem.at[0, b, o],
            gm2_sem.at[1, b, o],
            {"ch": lax.rem(j + o, chans)},
        )

    def gm_pass(b, o):
        f = lax.rem(j + chans - o, chans)
        return copy(
            gm_all.at[b, f], gm_all.at[b, f], gm2_sem.at[0, b, o + 1], gm2_sem.at[1, b, o + 1], {"ch": mate}
        )

    def gm_arrived(b):
        copy(gm_all.at[b, j], gm_all.at[b, j], gm1_sem.at[0, 0], gm1_sem.at[1, b], {"ctx": k, "ch": j}).wait_recv()

    for load in loads[1:]:
        load.wait()
    for d in range(1, peers):
        par_copy(d).wait_recv()
    rate = par[0:order]
    drop[0] = jnp.exp(rate * (-1.0 / seq_len))
    drop[1] = jnp.exp(rate * (-8.0 / seq_len))
    drop[2] = jnp.exp(rate * (-16.0 / seq_len))
    drop[3] = jnp.exp(rate * (-32.0 / seq_len))
    drop[4] = jnp.exp(rate * (-float(tokens) / seq_len))
    drop[5] = par[order : 2 * order] * jnp.sqrt(2.0 * rate / seq_len)

    def scan_up(source):
        decay = drop[0]

        def step(i, carry):
            s, s1 = carry
            for r in range(8):
                u = s + source[pl.ds(i * 8 + r, 1)]
                s1 = decay * (s1 + u)
                s = decay * u
            return s, s1

        zero = jnp.zeros((order, width), f32)
        return lax.fori_loop(0, tokens // 8, step, (zero, zero), unroll=4)

    def scan_down(source):
        decay = drop[0]

        def step(i, carry):
            s, s1 = carry
            for r in range(8):
                s1 = decay * (s1 + s)
                s = decay * s + source[pl.ds(tokens - 1 - i * 8 - r, 1)]
            return s, s1

        zero = jnp.zeros((order, width), f32)
        return lax.fori_loop(0, tokens // 8, step, (zero, zero), unroll=4)

    def scan_one(source):
        decay = drop[0]

        def step(i, s):
            for r in range(8):
                s = decay * (s + source[pl.ds(i * 8 + r, 1)])
            return s

        return lax.fori_loop(0, tokens // 8, step, jnp.zeros((order, width), f32), unroll=4)

    def spread(head, at, start, falling):
        lanes = at.size
        iota = lax.broadcasted_iota(jnp.int32, (8, lanes), 0).astype(f32)
        place = (iota if falling else 7.0 - iota) + start
        count = tokens // 8

        def mode(n, acc):
            row = pl.ds(n, 1)
            v = head(row) * jnp.exp(par[row, at] * (place * (-1.0 / seq_len)))
            d8, d16, d32 = drop[1, row, at], drop[2, row, at], drop[3, row, at]
            first = [v, v * d8]
            first = first + [x * d16 for x in first]
            out = []
            for i in range(0, count, 4):
                out += [acc[i + m] + first[m] for m in range(4)]
                first = [x * d32 for x in first]
            return tuple(out)

        zero = jnp.zeros((8, lanes), f32)
        acc = lax.fori_loop(0, order, mode, (zero,) * count, unroll=order)
        return jnp.concatenate(acc if falling else acc[::-1], axis=0)


    def x_copy(i, d):
        return copy(x_out.at[i], x_in.at[i, d], x_sem.at[0, i, d], x_sem.at[1, i, d], {"ctx": lax.rem(k + d, peers)})

    def x_send(i, state):
        x_out[i] = state.astype(bf16)
        for d in range(1, peers):

            @pl.when(k + d < peers)
            def _():
                x_copy(i, d).start()

    x_send(0, scan_one(gated))

    def filters(at):
        gf[:, at] = spread(lambda row: drop[5, row, at], at, 0.0, True)

    def conv(at):
        f = forward(gf[:, at])
        x = gated[:, at]
        u = forward_exact(x.astype(bf16))
        pq[:, at] = f
        ab[:, at] = u
        p, q, a, b = f[:tokens], f[tokens:], u[:tokens], u[tokens:]
        mix[:, at] = backward(p * a - q * b, p * b + q * a) + par[2 * order : 2 * order + 1, at] * x

    upper = jnp.where(k < peers // 2, 0, 1)
    place = jnp.where(upper == 0, k, last - k)

    def block_of(i, way):
        return jnp.where(way == 0, last - i, i)

    tiles(filters)
    tiles(conv, WIDE, 0, width // 2)
    for i in range(peers):
        b = block_of(i, upper)

        @pl.when((j != k) | (k != b))
        def _():
            gm_arrived(b)

        @pl.when((j == k) & (k == b))
        def _():
            gm_own().wait()

        for o in range(2, chans, 2):
            gm_chip(b, o).start()
        gm_mate(b).start()

    tiles(conv, WIDE, width // 2, width)

    s_in[...] = jnp.zeros(s_in.shape, f32)
    for d in range(1, peers):

        @pl.when(k >= d)
        def _():
            x_copy(0, d).wait_recv()
            s_in[0] = s_in[0] + drop[4] ** (d - 1) * x_in[0, d].astype(f32)

    def finish_mix(at):
        total = mix[:, at] + spread(lambda row: drop[5, row, at] * s_in[0, row, at], at, 0.0, True)
        total = total.astype(bf16).astype(f32)
        mix[:, at] = total
        mo_all[k, at] = (qkv[0, :, at] * total).T.astype(bf16)

    tiles(finish_mix)

    def ag_copy(way, d, c):
        s = lax.rem(k + peers + (2 * way - 1) * d, peers)
        rows = pl.ds(c * (width // 2), width // 2)
        return copy(
            mo_all.at[s, rows],
            mo_all.at[s, rows],
            ag_sem.at[0, way, d, c],
            ag_sem.at[1, way, d + 1, c],
            {"ctx": lax.rem(k + 1 + way * (peers - 2), peers)},
        )

    def ag_wait(way, d, c):
        s = lax.rem(k + peers + (2 * way - 1) * d, peers)
        part = mo_all.at[s, pl.ds(c * (width // 2), width // 2)]
        copy(part, part, ag_sem.at[0, way, d, c], ag_sem.at[1, way, d, c], {"ctx": k}).wait_recv()

    def relay(way, spot, d):
        @pl.when((spot >= d) & (spot < last))
        def _():
            for c in range(2):
                ag_wait(way, d, c)
                ag_copy(way, d, c).start()

    for c in range(2):

        @pl.when(k < last)
        def _():
            ag_copy(0, 0, c).start()

        @pl.when(k > 0)
        def _():
            ag_copy(1, 0, c).start()

    def line_copy(way, i, c):
        b = block_of(i, way)
        rows = pl.ds(c * half, half)
        return copy(
            line_out.at[way, b, rows],
            line_in.at[way, b, rows],
            line_sem.at[0, way, i, c],
            line_sem.at[1, way, i, c],
            {"ctx": lax.rem(k + 1 + way * (peers - 2), peers)},
        )

    for i in range(peers):
        b = block_of(i, upper)
        for o in range(2, chans, 2):
            gm_chip(b, o).wait_recv()
            gm_pass(b, o).start()

    for i in range(0, peers, 2):
        pair = [block_of(i, upper), block_of(i + 1, upper)]
        for b in pair:
            gm_mate(b).wait_recv()
            for o in range(2, chans, 2):
                gm_pass(b, o).wait_recv()

        def part(at):
            both = lax.dot_general(
                jnp.concatenate([gm_all[b].reshape(tokens, gm_all.shape[-1]) for b in pair], axis=0),
                weight[at, :],
                (((1,), (1,)), ((), ())),
                preferred_element_type=f32,
            )
            parts[pair[0], :, at] = both[:tokens]
            parts[pair[1], :, at] = both[tokens:]

        tiles(part)

        @pl.when(place == 0)
        def _():
            for n in range(i, min(i + 2, last)):
                for c in range(2):
                    rows = slice(c * half, (c + 1) * half)
                    line_out[upper, pair[n - i], rows] = parts[pair[n - i], rows].astype(bf16)
                    line_copy(upper, n, c).start()

    def gm_store():
        return pltpu.make_async_copy(gm_all, gm_out, out_sem.at[0])

    gm_store().start()

    s0, s1 = scan_up(gated)
    x_send(1, s1)

    def hop(way, spot, i, c):
        @pl.when((spot > 0) & (spot < last - i))
        def _():
            b = block_of(i, way)
            rows = slice(c * half, (c + 1) * half)
            line_copy(way, i, c).wait_recv()
            line_out[way, b, rows] = (parts[b, rows] + line_in[way, b, rows].astype(f32)).astype(bf16)
            line_copy(way, i, c).start()

    steps = [(i, c) for i in range(peers - 1) for c in range(2)]
    def hops(start, stop):
        for n in range(start, stop):
            if n < len(steps):
                hop(upper, place, *steps[n])
            if n >= 2:
                hop(1 - upper, last - place, *steps[n - 2])

    relay(1 - upper, last - place, 1)
    hops(0, 1)
    relay(upper, place, 1)
    hops(1, 5)
    for d in range(2, peers - 1):
        relay(1 - upper, last - place, d)
        relay(upper, place, d)
    hops(5, len(steps) + 2)

    def line_wait(way, spot):
        for i in range(peers - 1):

            @pl.when(spot == last - i)
            def _():
                for c in range(2):
                    line_copy(way, i, c).wait_recv()

        @pl.when(spot == 0)
        def _():
            line_in[way, k] = jnp.zeros((tokens, width), bf16)

    line_wait(1 - upper, last - place)
    line_wait(upper, place)

    def own(at):
        total = parts[k, :, at] + line_in[0, k, :, at].astype(f32) + line_in[1, k, :, at].astype(f32)
        go[:, at] = total
        gy[:, at] = (total * qkv[0, :, at]).astype(bf16).astype(f32)

    tiles(own)

    g0, g1 = scan_down(gy)
    g_out[...] = g0.astype(bf16)
    states[0] = g0
    states[1] = g1

    def r_copy(d):
        return copy(g_out, g_in.at[d], r_sem.at[0, d], r_sem.at[1, d], {"ctx": lax.rem(k + peers - d, peers)})

    for d in range(1, peers):

        @pl.when(k >= d)
        def _():
            r_copy(d).start()

    def conv_back(at):
        x = gy[:, at]
        w = forward_exact(x.astype(bf16))
        f, u = pq[:, at], ab[:, at]
        p, q, a, b = f[:tokens], f[tokens:], u[:tokens], u[tokens:]
        d, e = w[:tokens], w[tokens:]
        gg[:, at] = backward(p * d + q * e, p * e - q * d) + par[2 * order : 2 * order + 1, at] * x
        gf[:, at] = backward(d * a + e * b, e * a - d * b)
        skip[:, at] = jnp.broadcast_to(jnp.sum(x * gated[:, at], axis=0, keepdims=True) / norm, (8, x.shape[1]))
        gx[0, 0:tokens, at] = go[:, at] * mix[:, at]

    tiles(conv_back, WIDE)

    def sums(at, groups):
        rows = []
        for lag in range(SHORT):
            for g in groups:
                rows.append(
                    jnp.sum(gx[g, 0:tokens, at] * ext[g, 8 - lag : 8 - lag + tokens, at], axis=0, keepdims=True)
                )
        return [row * (1.0 / norm) for row in rows]

    quad = width // 4

    def shorts_q(at):
        sh_q[0:3, at] = jnp.concatenate(sums(at, (0,)), axis=0)

    tiles(shorts_q, 128)
    sh_q[3:4] = skip[0:1]
    few = sh_q[0:4]
    shq[k] = jnp.concatenate([few[:, q * quad : (q + 1) * quad] for q in range(4)], axis=0).astype(bf16)

    def shq_copy(d):
        return copy(shq.at[k], shq.at[k], shq_sem.at[0, d], shq_sem.at[1, d], {"ctx": lax.rem(k + d, peers)})

    for d in range(1, peers):
        shq_copy(d).start()

    m0, m1 = scan_down(gf)
    for d in range(1, peers):

        @pl.when(k >= d)
        def _():
            x_copy(1, d).wait_recv()
            s_in[1] = s_in[1] + drop[4] ** (d - 1) * (
                x_in[1, d].astype(f32) + float((d - 1) * tokens) * x_in[0, d].astype(f32)
            )

    m0 = m0 + states[0] * s_in[0]
    m1 = m1 + states[1] * s_in[0] + states[0] * s_in[1]
    mom_out[0:order] = (jnp.sqrt(2.0 * par[0:order] / seq_len) * m0 * (1.0 / norm)).astype(bf16)
    grad_log = drop[5] * (0.5 * m0 - par[0:order] * m1 * (1.0 / seq_len)) * (1.0 / norm)
    mom_out[order : 2 * order] = grad_log.astype(bf16)

    def mom_copy(d):
        to = lax.rem(k + d, peers)
        return copy(
            mom_out.at[:, pl.ds(pl.multiple_of(to * cols, cols), cols)],
            mom_in.at[d],
            mom_sem.at[0, d],
            mom_sem.at[1, d],
            {"ctx": to},
        )

    for d in range(1, peers):
        mom_copy(d).start()

    r_in[...] = jnp.zeros(r_in.shape, f32)
    for d in range(1, peers):

        @pl.when(k + d < peers)
        def _():
            r_copy(d).wait_recv()
            r_in[...] = r_in[...] + drop[4] ** (d - 1) * g_in[d].astype(f32)

    def grads(at):
        total = gg[:, at] + spread(lambda row: drop[5, row, at] * r_in[row, at], at, 1.0, False)
        total = total.astype(bf16).astype(f32)
        gx[1, 0:tokens, at] = total * qkv[2, :, at]
        gx[2, 0:tokens, at] = total * qkv[1, :, at]

    tiles(grads)

    edge = [gx[g, 0 : SHORT - 1] for g in range(3)] + [jnp.zeros((2, width), f32)]
    gx_out[...] = jnp.concatenate(edge, axis=0)
    gx_copy = copy(gx_out, gx_in, gx_sem.at[0], gx_sem.at[1], {"ctx": lax.rem(k + peers - 1, peers)})

    @pl.when(k > 0)
    def _():
        gx_copy.start()

    def shorts_v(at):
        rows = sums(at, (1, 2))
        sh_v[:, at] = jnp.concatenate(rows + [jnp.zeros((2, at.size), f32)], axis=0)

    tiles(shorts_v, 128)
    shv[k] = jnp.concatenate([sh_v[:, : width // 2], sh_v[:, width // 2 :]], axis=0).astype(bf16)

    def shv_copy(d):
        return copy(shv.at[k], shv.at[k], shv_sem.at[0, d], shv_sem.at[1, d], {"ctx": lax.rem(k + d, peers)})

    for d in range(1, peers):
        shv_copy(d).start()

    def out_rows(at, start, count):
        for g in range(3):
            total = taps[0, g : g + 1, at] * gx[g, start : start + count, at]
            for lag in range(1, SHORT):
                total = total + taps[lag, g : g + 1, at] * gx[g, start + lag : start + lag + count, at]
            gproj[g, start : start + count, at] = total.astype(bf16)

    def out_most(at):
        out_rows(at, 0, tokens - 16)

    tiles(out_most, 128)

    @pl.when(k < last)
    def _():
        gx_copy.wait_recv()
        for g in range(3):
            gx[g, tokens : tokens + 2] = gx_in[2 * g : 2 * g + 2]

    @pl.when(k == last)
    def _():
        gx[:, tokens : tokens + 8] = jnp.zeros((3, 8, width), f32)

    def out_end(at):
        out_rows(at, tokens - 16, 16)

    tiles(out_end)
    gproj_store = pltpu.make_async_copy(gproj, gproj_out, out_sem.at[1])
    gproj_store.start()

    @pl.when(place == 0)
    def _():
        for d in range(1, peers):
            ag_wait(1 - upper, d, 0)
            ag_wait(1 - upper, d, 1)

    mo_store = pltpu.make_async_copy(mo_all, mo_out, out_sem.at[2])
    mo_store.start()

    for d in range(1, peers):
        mom_copy(d).wait_recv()
    par_out[0 : 2 * order] = sum((mom_in[d].astype(f32) for d in range(1, peers)), mom_out[:, mine].astype(f32))
    for d in range(1, peers):
        shq_copy(d).wait_recv()
        shv_copy(d).wait_recv()
    few = sum((shq[d].astype(f32) for d in range(1, peers)), shq[0].astype(f32))
    for q in range(4):
        sh_out[0:4, q * quad : (q + 1) * quad] = few[4 * q : 4 * q + 4]
    many = sum((shv[d].astype(f32) for d in range(1, peers)), shv[0].astype(f32))
    sh_out[8:16, : width // 2] = many[0:8]
    sh_out[8:16, width // 2 :] = many[8:16]
    par_out[2 * order : 2 * order + 8] = jnp.broadcast_to(sh_out[3:4, mine], (8, cols))

    for d in range(1, chans):
        gm_first(d).wait_send()

    @pl.when(j != k)
    def _():
        gm_first(0).wait_send()

    for b in range(peers):
        gm_mate(b).wait_send()
        for o in range(2, chans, 2):
            gm_chip(b, o).wait_send()
            gm_pass(b, o).wait_send()
    for d in range(1, peers):
        par_copy(d).wait_send()
        mom_copy(d).wait_send()
        shq_copy(d).wait_send()
        shv_copy(d).wait_send()

        @pl.when(k + d < peers)
        def _():
            x_copy(0, d).wait_send()
            x_copy(1, d).wait_send()

        @pl.when(k >= d)
        def _():
            r_copy(d).wait_send()

    @pl.when(k < last)
    def _():
        halo_copy.wait_send()

    @pl.when(k > 0)
    def _():
        gx_copy.wait_send()

    for i in range(peers - 1):
        for c in range(2):

            @pl.when(k < last - i)
            def _():
                line_copy(0, i, c).wait_send()

            @pl.when(k > i)
            def _():
                line_copy(1, i, c).wait_send()

    for d in range(peers - 1):

        @pl.when((k >= d) & (k < last))
        def _():
            ag_copy(0, d, 0).wait_send()
            ag_copy(0, d, 1).wait_send()

        @pl.when((k + d < peers) & (k > 0))
        def _():
            ag_copy(1, d, 0).wait_send()
            ag_copy(1, d, 1).wait_send()

    gm_store().wait()
    gproj_store.wait()
    mo_store.wait()


def finish_kernel(peers, order, norm, mo, gm, rows, sums, params, gproj, gshort, gskip, gres, glog, gweight):
    gproj[...] = rows[...]
    left = jnp.concatenate([mo[b] for b in range(peers)], axis=1)
    gweight[...] = lax.dot_general(
        left, gm[...], (((1,), (0,)), ((), ())), preferred_element_type=jnp.float32
    ) * (1.0 / norm)
    for lag in range(SHORT):
        gshort[lag, 0:1] = sums[lag : lag + 1]
        gshort[lag, 1:3] = sums[8 + 2 * lag : 10 + 2 * lag]
    gres[...] = params[0:order]
    glog[...] = params[order : 2 * order]
    gskip[...] = params[2 * order : 2 * order + 1]


def body_fused(projections, short_taps, residues, decay_rates, skip_gain, grad_mixed, out_weight):
    tokens, _, width = projections.shape
    peers, chans = lax.axis_size("ctx"), lax.axis_size("ch")
    order = residues.shape[1]
    cols = width // peers
    wide = out_weight.shape[1]
    seq_len = tokens * peers
    f32, bf16 = jnp.float32, jnp.bfloat16
    ahead, back = line_tables(tokens)
    rows = 2 * order + 8
    vmem = pl.BlockSpec(memory_space=pltpu.VMEM)
    far = pl.BlockSpec(memory_space=pl.ANY)
    dma = pltpu.SemaphoreType.DMA
    shape = jax.ShapeDtypeStruct
    gproj, sums, params, mo, gm = pl.pallas_call(
        partial(fused_kernel, peers, chans, order),
        out_shape=(
            shape((3, tokens, width), bf16),
            shape((16, width), f32),
            shape((rows, cols), f32),
            shape((peers, width, tokens), bf16),
            shape((peers, chans, tokens // chans, wide), bf16),
        ),
        in_specs=[far, vmem, vmem, vmem, vmem, far, far, far, far],
        out_specs=(far, vmem, vmem, far, far),
        scratch_shapes=[
            pltpu.VMEM((3, tokens, width), bf16),
            pltpu.VMEM((width, wide), bf16),
            pltpu.VMEM(ahead.shape, bf16),
            pltpu.VMEM(back.shape, bf16),
            pltpu.VMEM((rows, width), f32),
            pltpu.VMEM((16, width // 2), bf16),
            pltpu.VMEM((16, width // 2), bf16),
            pltpu.VMEM((3, tokens + 8, width), f32),
            pltpu.VMEM((3, tokens, width), f32),
            pltpu.VMEM((tokens, width), f32),
            pltpu.VMEM((6, order, width), f32),
            pltpu.VMEM((2, order, width), f32),
            pltpu.VMEM((2, order, width), bf16),
            pltpu.VMEM((2, peers, order, width), bf16),
            pltpu.VMEM((2, order, width), f32),
            pltpu.VMEM((2 * tokens, width), f32),
            pltpu.VMEM((2 * tokens, width), f32),
            pltpu.VMEM((tokens, width), f32),
            pltpu.VMEM((peers, chans, tokens // chans, wide), bf16),
            pltpu.VMEM((peers, tokens, width), f32),
            pltpu.VMEM((2, peers, tokens, width), bf16),
            pltpu.VMEM((2, peers, tokens, width), bf16),
            pltpu.VMEM((peers, width, tokens), bf16),
            pltpu.VMEM((tokens, width), f32),
            pltpu.VMEM((tokens, width), f32),
            pltpu.VMEM((tokens, width), f32),
            pltpu.VMEM((tokens, width), f32),
            pltpu.VMEM((order, width), bf16),
            pltpu.VMEM((peers, order, width), bf16),
            pltpu.VMEM((order, width), f32),
            pltpu.VMEM((2 * order, width), bf16),
            pltpu.VMEM((peers, 2 * order, cols), bf16),
            pltpu.VMEM((3, tokens + 8, width), f32),
            pltpu.VMEM((8, width), f32),
            pltpu.VMEM((8, width), f32),
            pltpu.VMEM((8, width), f32),
            pltpu.VMEM((8, width), f32),
            pltpu.VMEM((8, width), f32),
            pltpu.VMEM((peers, 16, width // 4), bf16),
            pltpu.VMEM((peers, 16, width // 2), bf16),
            pltpu.VMEM((3, tokens, width), bf16),
            dma((4,)),
            dma,
            dma((2,)),
            dma((2, peers)),
            dma((2, max(peers, chans))),
            dma((2, peers, chans)),
            dma((2, 2, peers)),
            dma((2, 2, peers, 2)),
            dma((2, 2, peers, 2)),
            dma((2, peers)),
            dma((2, peers)),
            dma((2,)),
            dma((2, peers)),
            dma((2, peers)),
            dma((3,)),
        ],
        compiler_params=pltpu.CompilerParams(
            collective_id=0, has_side_effects=True, vmem_limit_bytes=56 * 1024 * 1024
        ),
    )(
        projections.transpose(1, 0, 2),
        short_taps,
        decay_rates.T,
        residues.T,
        skip_gain[None],
        grad_mixed,
        out_weight,
        jnp.asarray(ahead),
        jnp.asarray(back),
    )
    lanes = WIDE
    whole = lambda *dims: pl.BlockSpec(dims, lambda i: (0,) * len(dims))
    gproj, gshort, gskip, gres, glog, gweight = pl.pallas_call(
        partial(finish_kernel, peers, order, math.sqrt(seq_len)),
        grid=(width // lanes,),
        out_shape=(
            shape((3, tokens, width), bf16),
            shape((SHORT, 3, width), f32),
            shape((1, cols), f32),
            shape((order, cols), f32),
            shape((order, cols), f32),
            shape((width, wide), f32),
        ),
        in_specs=[
            pl.BlockSpec((peers, lanes, tokens), lambda i: (0, i, 0)),
            whole(seq_len, wide),
            pl.BlockSpec((3, tokens, lanes), lambda i: (0, 0, i)),
            pl.BlockSpec((16, lanes), lambda i: (0, i)),
            whole(rows, cols),
        ],
        out_specs=(
            pl.BlockSpec((3, tokens, lanes), lambda i: (0, 0, i)),
            pl.BlockSpec((SHORT, 3, lanes), lambda i: (0, 0, i)),
            whole(1, cols),
            whole(order, cols),
            whole(order, cols),
            pl.BlockSpec((lanes, wide), lambda i: (i, 0)),
        ),
    )(mo, gm.reshape(seq_len, wide), gproj, sums, params)
    return (gproj.transpose(1, 0, 2), gshort, gskip[0], gres.T, glog.T, gweight)


def body(*args):
    peers, chans = lax.axis_size("ctx"), lax.axis_size("ch")
    if peers * args[0].shape[0] > 1024 or peers != chans:
        return body_factored(*args)
    return body_fused(*args)


def solution(mesh):
    return jax.shard_map(
        body,
        mesh=mesh,
        in_specs=(
            P(("groups", "ctx"), None, "ch"),
            P(None, None, "ch"),
            P(("ch", "ctx"), None),
            P(("ch", "ctx"), None),
            P(("ch", "ctx")),
            P(("groups", "ctx"), "ch"),
            P("ch", "ctx"),
        ),
        out_specs=(
            P(("groups", "ctx"), None, "ch"),
            P("groups", None, "ch"),
            P(("groups", "ch", "ctx")),
            P(("groups", "ch", "ctx"), None),
            P(("groups", "ch", "ctx"), None),
            P(("groups", "ch"), "ctx"),
        ),
        check_vma=False,
    )
```
